32 devices in a mesh: seq: 8 (over y, x, core), head: 4 (over z).
Axes of the slice: x: 2, y: 2, z: 4, core: 2. Of those that a mesh axis runs over, the one named last changes fastest.
Arguments:
- query_lin: bfloat16 [512, 4096], P('seq', 'head'), may hold values from -6 to 6
- key_lin: bfloat16 [512, 4096], P('seq', 'head'), may hold values from -6 to 6
- value_lin: bfloat16 [512, 4096], P('seq', 'head'), may hold values from -6 to 6
- log_decay: float32 [32, 512], P('head', 'seq'), may hold values from -1.6 to 0
- query_soft: bfloat16 [512, 4096], P(('seq', 'head')), may hold values from -4.5 to 4.5
- key_soft: bfloat16 [512, 512], P(('seq', 'head')), may hold values from -4.5 to 4.5
- value_soft: bfloat16 [512, 512], P(('seq', 'head')), may hold values from -6 to 6
- doc_start: int32 [512], P('seq'), may hold values from 0 to 480, as said below
Outputs:
- lin_out: bfloat16 [512, 4096], P('seq', 'head')
- soft_out: bfloat16 [512, 4096], P('seq', 'head')
- soft_lse: float32 [32, 512], P('head', 'seq')
The draws below stay inside these ranges and needn't reach their ends.
Inputs may be any that keep to these rules, and one draw needn't show every extreme that they name: doc_start[t] is the first position of the document that holds token t: 0 for the first document, never above t, the same over a document; at most 4 documents; every document but the first and the last starts at a position of 1 to 32; the last document starts at 480.
All inputs are finite; a program needn't handle non-finite values.
Results may differ from the reference program's by a relative error of at most 0.003.
Values may be sent and summed in bfloat16 or wider, within the bound.
A program may use at most 256 MiB of HBM per device.

```python
import math
import jax
import jax.numpy as jnp
from jax import lax

DH = 128
LINEAR_HEADS = 32
SOFT_HEADS = 32
KV_HEADS = 4
DOCS = 4
TOK_DEV = 64
TOKEN_COUNT = 512


def draw_log_decay(key, part):
    every_key_row = jax.random.split(key, 7)
    slow_count = LINEAR_HEADS // 2
    order = jax.random.permutation(every_key_row[0], LINEAR_HEADS)
    slow_heads = order < slow_count
    slow_rate = jnp.exp(jax.random.uniform(every_key_row[1], (LINEAR_HEADS,), jnp.float32, math.log(0.2 / TOKEN_COUNT), math.log(0.6 / TOKEN_COUNT)))
    fast_rate = jnp.exp(jax.random.uniform(every_key_row[2], (LINEAR_HEADS,), jnp.float32, math.log(1.0 / 200.0), math.log(1.0 / 30.0)))
    rate = jnp.where(slow_heads, slow_rate, fast_rate)
    blocks = TOKEN_COUNT // TOK_DEV
    block_factor = jnp.exp(jax.random.uniform(every_key_row[3], (LINEAR_HEADS, blocks, 1), jnp.float32, -0.7, 0.7))
    token_factor = jax.random.uniform(every_key_row[4], (LINEAR_HEADS, blocks, TOK_DEV), jnp.float32, 0.5, 1.5)
    base_offset = -(rate[:, None, None] * block_factor * token_factor).reshape(LINEAR_HEADS, TOKEN_COUNT)
    cluster_positions = jax.random.randint(every_key_row[5], (LINEAR_HEADS, 2), 0, TOKEN_COUNT)
    cluster_depth = jnp.log(jax.random.uniform(every_key_row[6], (LINEAR_HEADS, 2), jnp.float32, 0.5, 0.8))
    token_positions = jnp.arange(TOKEN_COUNT, dtype=jnp.int32)
    cluster_matches = token_positions[None, None, :] == cluster_positions[:, :, None]
    token_clusters = jnp.sum(jnp.where(cluster_matches, cluster_depth[:, :, None], 0.0), axis=1)
    return (base_offset + token_clusters).astype(jnp.float32)


def draw_doc_start(key, part):
    last_edge = TOKEN_COUNT - TOK_DEV // 2
    drawn_edges = jax.random.randint(jax.random.fold_in(key, 5), (DOCS - 2,), 1, TOK_DEV // 2 + 1)
    doc_edges = jnp.concatenate([drawn_edges.astype(jnp.int32), jnp.full((1,), last_edge, jnp.int32)])
    token_positions = jnp.arange(TOKEN_COUNT, dtype=jnp.int32)
    picked = jnp.where(doc_edges[None, :] <= token_positions[:, None], doc_edges[None, :], 0)
    return jnp.max(picked, axis=1).astype(jnp.int32)


def soft_pair(key):
    base_key = jax.random.fold_in(key, 17)
    key_key, query_key = jax.random.split(base_key, 2)
    keys_drawn = jnp.clip(jax.random.normal(key_key, (TOKEN_COUNT, KV_HEADS * DH), jnp.float32), -4.5, 4.5)
    queries_drawn = jnp.clip(jax.random.normal(query_key, (TOKEN_COUNT, SOFT_HEADS * DH), jnp.float32), -4.5, 4.5)
    return (keys_drawn, queries_drawn)


def draw_key_soft(key, part):
    return soft_pair(key)[0].astype(jnp.bfloat16)


def draw_query_soft(key, part):
    return soft_pair(key)[1].astype(jnp.bfloat16)


def block_scale(rng, extent, pieces, least, high):
    def one(axis_at, shards_of):
        heights = jax.random.uniform(jax.random.fold_in(jax.random.fold_in(rng, 6), axis_at), (shards_of,), jnp.float32, least / len(pieces), high / len(pieces))
        return jnp.repeat(jnp.exp(heights), extent[axis_at] // shards_of).reshape((-1,) + (1,) * (len(extent) - axis_at - 1))

    factor_of = one(*pieces[0])
    for cut in pieces[1:]:
        factor_of = factor_of * one(*cut)
    return factor_of


def gaussian(key, dims, spread, bound, cuts=(), held_as=jnp.bfloat16):
    result = spread * jax.random.normal(key, dims, jnp.float32)
    if cuts:
        result = result * block_scale(key, dims, cuts, -0.22, 0.18)
    return jnp.clip(result, -bound, bound).astype(held_as)


def setup_inputs(seed: int = 0) -> dict:
    key_of = jax.random.split(jax.random.key(seed), 9)
    query_lin = gaussian(key_of[0], (TOKEN_COUNT, LINEAR_HEADS * DH), 1.0, 6.0, ((0, 8), (1, 4)))
    key_lin = gaussian(key_of[1], (TOKEN_COUNT, LINEAR_HEADS * DH), 1.0, 6.0, ((0, 8), (1, 4)))
    value_lin = gaussian(key_of[2], (TOKEN_COUNT, LINEAR_HEADS * DH), 1.0, 6.0, ((0, 8), (1, 4)))
    log_decay = draw_log_decay(jax.random.fold_in(key_of[8], 71), 0)
    query_soft = draw_query_soft(jax.random.fold_in(key_of[8], 71), 0)
    key_soft = draw_key_soft(jax.random.fold_in(key_of[8], 71), 0)
    value_soft = gaussian(key_of[6], (TOKEN_COUNT, KV_HEADS * DH), 1.0, 6.0, ((0, 32),))
    doc_start = draw_doc_start(jax.random.fold_in(key_of[8], 71), 0)
    return {"query_lin": query_lin, "key_lin": key_lin, "value_lin": value_lin, "log_decay": log_decay, "query_soft": query_soft, "key_soft": key_soft, "value_soft": value_soft, "doc_start": doc_start}


HIGHEST = lax.Precision.HIGHEST

def span_terms(query_heads, key_heads, value_heads, decay_rows, doc_rows, first_place):
    span_len = query_heads.shape[0]
    cumulative = jnp.cumsum(decay_rows, axis=1)
    totals = cumulative[:, -1]
    token_positions = first_place + jnp.arange(span_len, dtype=jnp.int32)
    allowed = (token_positions[None, :] <= token_positions[:, None]) & (doc_rows[:, None] <= token_positions[None, :])
    decay_gap = jnp.where(allowed[None], cumulative[:, :, None] - cumulative[:, None, :], 0.0)
    decay_mat = jnp.where(allowed[None], jnp.exp(decay_gap), 0.0)
    query_float = query_heads.astype(jnp.float32)
    key_float = key_heads.astype(jnp.float32)
    value_float = value_heads.astype(jnp.float32)
    scores = jnp.einsum('thd,shd->hts', query_float, key_float, precision=HIGHEST)
    inner_part = jnp.einsum('hts,shd->thd', scores * decay_mat, value_float, precision=HIGHEST)
    keep_mask = (doc_rows == doc_rows[-1]).astype(jnp.float32)
    tail_weight = jnp.exp(totals[:, None] - cumulative) * keep_mask[None, :]
    weighted_keys = key_float * jnp.transpose(tail_weight)[:, :, None]
    fresh_state = jnp.einsum('shd,she->hde', weighted_keys, value_float, precision=HIGHEST)
    carry_on = (doc_rows[-1] < first_place).astype(jnp.float32)
    factor = jnp.exp(totals) * carry_on
    read_mask = (doc_rows < first_place).astype(jnp.float32)[:, None] * jnp.transpose(jnp.exp(cumulative))
    return (inner_part, fresh_state, factor, read_mask, query_float)

def lightning(query_lin, key_lin, value_lin, log_decay, doc_start):
    blocks = TOKEN_COUNT // TOK_DEV
    query_parts = query_lin.reshape(blocks, TOK_DEV, LINEAR_HEADS, DH)
    key_parts = key_lin.reshape(blocks, TOK_DEV, LINEAR_HEADS, DH)
    value_parts = value_lin.reshape(blocks, TOK_DEV, LINEAR_HEADS, DH)
    decay_parts = jnp.transpose(log_decay.reshape(LINEAR_HEADS, blocks, TOK_DEV), (1, 0, 2))
    doc_parts = doc_start.reshape(blocks, TOK_DEV)
    block_starts = jnp.arange(blocks, dtype=jnp.int32) * TOK_DEV

    def advance(carried, slices):
        query_block, key_block, value_block, decay_block, doc_block, first_place = slices
        inner_part, fresh_state, factor, read_mask, query_float = span_terms(query_block, key_block, value_block, decay_block, doc_block, first_place)
        outer_part = jnp.einsum('thd,hde->the', query_float, carried, precision=HIGHEST) * read_mask[:, :, None]
        mixed_out = inner_part + outer_part
        normed = mixed_out * lax.rsqrt(lax.optimization_barrier(jnp.mean(mixed_out * mixed_out, axis=-1, keepdims=True)) + 1e-06)
        return (factor[:, None, None] * carried + fresh_state, normed.astype(jnp.bfloat16))
    start_state = jnp.zeros((LINEAR_HEADS, DH, DH), jnp.float32)
    final_state, outputs = lax.scan(advance, start_state, (query_parts, key_parts, value_parts, decay_parts, doc_parts, block_starts))
    return outputs.reshape(TOKEN_COUNT, LINEAR_HEADS * DH)

def softmax_layer(query_soft, key_soft, value_soft, doc_start):
    group_size = SOFT_HEADS // KV_HEADS
    blocks = TOKEN_COUNT // TOK_DEV
    keys_float = key_soft.astype(jnp.float32).reshape(TOKEN_COUNT, KV_HEADS, DH)
    values_float = value_soft.astype(jnp.float32).reshape(TOKEN_COUNT, KV_HEADS, DH)
    token_positions = jnp.arange(TOKEN_COUNT, dtype=jnp.int32)
    query_parts = query_soft.reshape(blocks, TOK_DEV, KV_HEADS, group_size, DH)
    doc_parts = doc_start.reshape(blocks, TOK_DEV)
    block_starts = jnp.arange(blocks, dtype=jnp.int32) * TOK_DEV

    def one_block(slices):
        query_block, doc_block, first_place = slices
        query_places = first_place + jnp.arange(TOK_DEV, dtype=jnp.int32)
        allowed = (token_positions[None, :] <= query_places[:, None]) & (doc_block[:, None] <= token_positions[None, :])
        allowed = allowed[:, None, None, :]
        scores = jnp.einsum('tkgd,skd->tkgs', query_block.astype(jnp.float32), keys_float, precision=HIGHEST) * DH ** (-0.5)
        masked = jnp.where(allowed, scores, -jnp.inf)
        row_max = lax.optimization_barrier(jnp.max(masked, axis=-1, keepdims=True))
        raw_weight = jnp.where(allowed, jnp.exp(masked - row_max), 0.0)
        norm_sum = lax.optimization_barrier(jnp.sum(raw_weight, axis=-1))
        rounded = lax.optimization_barrier(raw_weight.astype(jnp.bfloat16))
        mixed_out = jnp.einsum('tkgs,skd->tkgd', rounded.astype(jnp.float32), values_float, precision=HIGHEST)
        soft_rows = (mixed_out / norm_sum[..., None]).astype(jnp.bfloat16).reshape(TOK_DEV, SOFT_HEADS * DH)
        lse_rows = (row_max[..., 0] + jnp.log(norm_sum)).reshape(TOK_DEV, SOFT_HEADS)
        return (soft_rows, lse_rows)
    soft_parts, lse_parts = lax.map(one_block, (query_parts, doc_parts, block_starts))
    soft_out = soft_parts.reshape(TOKEN_COUNT, SOFT_HEADS * DH)
    soft_lse = jnp.transpose(lse_parts.reshape(TOKEN_COUNT, SOFT_HEADS))
    return (soft_out, soft_lse)

def reference(query_lin, key_lin, value_lin, log_decay, query_soft, key_soft, value_soft, doc_start):
    lin_out = lightning(query_lin, key_lin, value_lin, log_decay, doc_start)
    soft_out, soft_lse = softmax_layer(query_soft, key_soft, value_soft, doc_start)
    return (lin_out, soft_out, soft_lse)
```

```python
import functools

import jax
import jax.numpy as jnp
from jax import lax
from jax.experimental import pallas as pl
from jax.experimental.pallas import tpu as pltpu
from jax.sharding import PartitionSpec as P


DH = 128


HIGHEST = lax.Precision.HIGHEST
masked_score = -1e30


def prefix(array, axis, combine, identity):
    size, here = (lax.axis_size(axis), lax.axis_index(axis))
    everything = jax.tree.map(lambda part: lax.all_gather(part, axis), array)
    start = jax.tree.map(
        lambda part, zero: jnp.broadcast_to(jnp.asarray(zero, part.dtype), part.shape),
        array,
        identity,
    )

    def lap(k, before):
        reached = k < here
        new = combine(before, jax.tree.map(lambda part: part[k], everything))
        return jax.tree.map(lambda a, b: jnp.where(reached, a, b), new, before)

    return lax.fori_loop(0, size, lap, start)


def span_terms(query_heads, key_heads, value_heads, decay_rows, doc_rows, first_place):
    span_len = query_heads.shape[0]
    places = jnp.arange(span_len, dtype=jnp.int32)
    not_later = places[None, :] <= places[:, None]
    cumulative = jnp.sum(jnp.where(not_later[None], decay_rows[:, None, :], 0.0), axis=2)
    totals = cumulative[:, -1]
    token_positions = first_place + jnp.arange(span_len, dtype=jnp.int32)
    allowed = (token_positions[None, :] <= token_positions[:, None]) & (
        doc_rows[:, None] <= token_positions[None, :]
    )
    decay_gap = jnp.where(allowed[None], cumulative[:, :, None] - cumulative[:, None, :], 0.0)
    decay_mat = jnp.where(allowed[None], jnp.exp(decay_gap), 0.0)
    scores = jnp.einsum("thd,shd->hts", query_heads, key_heads, preferred_element_type=jnp.float32)
    key_float = key_heads.astype(jnp.float32)
    value_float = value_heads.astype(jnp.float32)
    inner_part = jnp.einsum("hts,shd->thd", scores * decay_mat, value_float, precision=HIGHEST)
    keep_mask = (doc_rows == doc_rows[-1]).astype(jnp.float32)
    tail_weight = jnp.exp(totals[:, None] - cumulative) * keep_mask[None, :]
    weighted_keys = key_float * jnp.transpose(tail_weight)[:, :, None]
    fresh_state = jnp.einsum("shd,she->hde", weighted_keys, value_float, precision=HIGHEST)
    carry_on = (doc_rows[-1] < first_place).astype(jnp.float32)
    factor = jnp.exp(totals) * carry_on
    read_mask = (doc_rows < first_place).astype(jnp.float32)[:, None] * jnp.transpose(
        jnp.exp(cumulative)
    )
    return (inner_part, fresh_state, factor, read_mask)


def combine_states(earlier, later_part):
    return (earlier[0] * later_part[0], later_part[0][:, None, None] * earlier[1] + later_part[1])


def lightning_part(query_lin, key_lin, value_lin, log_decay, doc_start):
    span_len = query_lin.shape[0]
    head_count = log_decay.shape[0]
    first_place = lax.axis_index("seq") * span_len
    query_heads = query_lin.reshape(span_len, head_count, DH)
    key_heads = key_lin.reshape(span_len, head_count, DH)
    value_heads = value_lin.reshape(span_len, head_count, DH)
    inner_part, fresh_state, factor, read_mask = span_terms(
        query_heads, key_heads, value_heads, log_decay, doc_start, first_place
    )
    identity = (jnp.ones((head_count,), jnp.float32), jnp.zeros((head_count, DH, DH), jnp.float32))
    unused, carried = prefix((factor, fresh_state), "seq", combine_states, identity)
    outer_part = (
        jnp.einsum("thd,hde->the", query_heads.astype(jnp.float32), carried, precision=HIGHEST)
        * read_mask[:, :, None]
    )
    mixed_out = inner_part + outer_part
    normed = mixed_out * lax.rsqrt(jnp.mean(mixed_out * mixed_out, axis=-1, keepdims=True) + 1e-06)
    return normed.astype(jnp.bfloat16).reshape(span_len, head_count * DH)


def softmax_part(query_soft, key_soft, value_soft, doc_start):
    queries, keys_local, values_local = (
        lax.all_to_all(query_soft, "head", split_axis=1, concat_axis=0, tiled=True),
        lax.all_to_all(key_soft, "head", split_axis=1, concat_axis=0, tiled=True),
        lax.all_to_all(value_soft, "head", split_axis=1, concat_axis=0, tiled=True),
    )
    span_len = queries.shape[0]
    kv_count = keys_local.shape[1] // DH
    group_size = queries.shape[1] // keys_local.shape[1]
    first_place = lax.axis_index("seq") * span_len
    query_places = first_place + jnp.arange(span_len, dtype=jnp.int32)
    query_heads = queries.reshape(span_len, kv_count, group_size, DH)
    score_scale = DH ** (-0.5)
    start_state = (
        jnp.full((span_len, kv_count, group_size), masked_score, jnp.float32),
        jnp.zeros((span_len, kv_count, group_size), jnp.float32),
        jnp.zeros((span_len, kv_count, group_size, DH), jnp.float32),
    )
    key_piece = lax.all_gather(keys_local, "seq", axis=0, tiled=True)
    value_piece = lax.all_gather(values_local, "seq", axis=0, tiled=True)
    piece_rows = key_piece.shape[0]
    block_rows = max(
        (divisor for divisor in range(1, min(piece_rows, 1024) + 1) if piece_rows % divisor == 0)
    )
    block_count = piece_rows // block_rows
    key_parts = key_piece.reshape(block_count, block_rows, kv_count, DH)
    value_parts = value_piece.reshape(block_count, block_rows, kv_count, DH)
    begin_rows = jnp.int32(0) + block_rows * jnp.arange(block_count, dtype=jnp.int32)

    def absorb_block(running, slices):
        key_block, value_block, begin_row = slices
        running_max, norm_sum, accum_out = running
        token_positions = begin_row + jnp.arange(block_rows, dtype=jnp.int32)
        allowed = (token_positions[None, :] <= query_places[:, None]) & (
            doc_start[:, None] <= token_positions[None, :]
        )
        allowed = allowed[:, None, None, :]
        scores = (
            jnp.einsum("tkgd,skd->tkgs", query_heads, key_block, preferred_element_type=jnp.float32)
            * score_scale
        )
        new_max = jnp.maximum(
            running_max, jnp.max(jnp.where(allowed, scores, masked_score), axis=-1)
        )
        raw_weight = jnp.where(allowed, jnp.exp(scores - new_max[..., None]), 0.0)
        shrink = jnp.exp(running_max - new_max)
        norm_sum = norm_sum * shrink + jnp.sum(raw_weight, axis=-1)
        accum_out = accum_out * shrink[..., None] + jnp.einsum(
            "tkgs,skd->tkgd",
            raw_weight.astype(jnp.bfloat16),
            value_block,
            preferred_element_type=jnp.float32,
        )
        running = (new_max, norm_sum, accum_out)
        return (running, None)

    final_state, unused = lax.scan(absorb_block, start_state, (key_parts, value_parts, begin_rows))
    running_max, norm_sum, accum_out = final_state
    soft_out = (
        (accum_out / norm_sum[..., None])
        .astype(jnp.bfloat16)
        .reshape(span_len, kv_count * group_size * DH)
    )
    soft_lse = jnp.transpose(
        (running_max + jnp.log(norm_sum)).reshape(span_len, kv_count * group_size)
    )
    return (soft_out, soft_lse)


MESH = pl.DeviceIdType.MESH
NT = (((1,), (1,)), ((), ()))


TN = (((0,), (0,)), ((), ()))


def fused_kernel(
    n, m, q_in, k_in, v_in, ld_in, qs_in, ks_in, vs_in, doc_in,
    lin_out, soft_out, lse_out,
    lin_all, ld_v, doc_v, state_f, state, sums, sums_a, state_a, state_b, inner, col_v, lin_v,
    qs, kvs, kv, soft_v, lse_v, bias,
    loc_sem, pair_s, pair_r, kv1_s, kv1_r, qs_s, qs_r, kv2_s, kv2_r,
    a_s, a_r, b_s, b_r, out_s, out_r, go_xy, go_z, far_in,
):
    span, heads = doc_in.shape[1], ld_in.shape[0]
    rows = qs_in.shape[0]
    tokens = n * span
    chips, group, chunk = n // 2, heads // 2, 2 * span
    width = group * DH
    me, hd = lax.axis_index("seq"), lax.axis_index("head")
    chip, core = me // 2, lax.rem(me, 2)
    other = 1 - core
    sibling = {"seq": 2 * chip + other}
    first = chip * chunk
    seq_peers = [lax.rem(me + n - j, n) for j in range(1, n)]
    head_peers = [j + jnp.where(j >= hd, 1, 0) for j in range(m - 1)]

    def cols(index, size=DH):
        return pl.ds(pl.multiple_of(index * size, size), size)

    def own_rows(index, count):
        return pl.ds(pl.multiple_of(index * count, count), count)

    def greet(semaphore, device):
        pl.semaphore_signal(semaphore, inc=1, device_id=device, device_id_type=MESH)

    barrier = pltpu.get_barrier_semaphore()
    for peer in head_peers:
        greet(barrier, {"seq": 2 * chip + 1, "head": peer})
    early = hd < m // 2

    @pl.when((core == 1) & early)
    def _():
        greet(barrier, {"seq": me - 1})

    @pl.when((core == 0) & jnp.logical_not(early))
    def _():
        greet(barrier, {"seq": me + 1})

    for source, targets in ((0, (1,)), (1, (0, 2, 3)), (2, (3,))):
        for target in targets:

            @pl.when(chip == target)
            def _():
                greet(barrier, {"seq": 2 * source})

    mine = cols(core, width)
    here = own_rows(core, span)
    loads = [
        pltpu.make_async_copy(ld_in, ld_v.at[core], loc_sem.at[0]),
        pltpu.make_async_copy(doc_in, doc_v.at[core], loc_sem.at[1]),
        pltpu.make_async_copy(q_in.at[:, mine], lin_all.at[0, here, :], loc_sem.at[2]),
        pltpu.make_async_copy(k_in.at[:, mine], lin_all.at[1, here, :], loc_sem.at[3]),
        pltpu.make_async_copy(v_in.at[:, mine], lin_all.at[2, here, :], loc_sem.at[4]),
        pltpu.make_async_copy(ks_in, kvs.at[0], loc_sem.at[5]),
        pltpu.make_async_copy(vs_in, kvs.at[1], loc_sem.at[6]),
        pltpu.make_async_copy(
            qs_in.at[:, cols(hd, heads * DH)], qs.at[own_rows(hd, rows), :], loc_sem.at[7]
        ),
    ]
    for load in loads:
        load.start()
    own_kv = pltpu.make_async_copy(
        kvs.at[:, :, cols(hd)], kv.at[:, own_rows(me * m + hd, rows), :], loc_sem.at[8]
    )

    def remote(src, dst, send, recv, device):
        return pltpu.make_async_remote_copy(
            src_ref=src, dst_ref=dst, send_sem=send, recv_sem=recv,
            device_id=device, device_id_type=MESH,
        )

    theirs = cols(other, width)
    pair = [
        remote(k_in.at[:, theirs], lin_all.at[1, here, :], pair_s.at[0], pair_r.at[0], sibling),
        remote(v_in.at[:, theirs], lin_all.at[2, here, :], pair_s.at[1], pair_r.at[1], sibling),
        remote(ld_in, ld_v.at[core], pair_s.at[2], pair_r.at[2], sibling),
        remote(doc_in, doc_v.at[core], pair_s.at[3], pair_r.at[3], sibling),
        remote(q_in.at[:, theirs], lin_all.at[0, here, :], pair_s.at[4], pair_r.at[4], sibling),
    ]
    kv1, qsc = [], []
    for j, peer in enumerate(head_peers):
        kv1.append(
            remote(
                kvs.at[:, :, cols(peer)], kv.at[:, own_rows(me * m + hd, rows), :],
                kv1_s.at[j], kv1_r.at[hd], {"head": peer},
            )
        )
        qsc.append(
            remote(
                qs_in.at[:, cols(peer, heads * DH)], qs.at[own_rows(hd, rows), :],
                qs_s.at[j], qs_r.at[hd], {"head": peer},
            )
        )
    block = kv.at[:, own_rows(me, span), :]
    kv2 = [
        remote(block, block, kv2_s.at[j], kv2_r.at[me], {"seq": peer})
        for j, peer in enumerate(seq_peers)
    ]

    def state_to(i, device):
        return remote(state.at[i], state_a.at[i], a_s.at[i], a_r.at[i], device)

    def carry_to(i, target):
        return remote(
            state.at[i], state_b.at[i], b_s.at[target - 2, i], b_r.at[i],
            {"seq": 2 * target + core},
        )

    following = {"seq": lax.rem(me + 2, n)}
    sums_to = remote(sums, sums_a, a_s.at[group], a_r.at[group], following)

    def send_over_z():
        for load in loads[5:7]:
            load.wait()
        own_kv.start()
        for copy in kv1 + qsc:
            copy.start()

    n_xy = jnp.where(chip == 1, 6, 2)
    n_z = 2 * (m - 1)

    @pl.when(early)
    def _():
        @pl.when(core == 0)
        def _():
            pl.semaphore_wait(barrier, jnp.where(chip == 3, 1, n_xy + 1))
            greet(go_xy, sibling)

        @pl.when(core == 1)
        def _():
            pl.semaphore_wait(go_xy, 1)

        for copy in pair:
            copy.start()

    @pl.when(jnp.logical_not(early))
    def _():
        @pl.when(core == 1)
        def _():
            pl.semaphore_wait(barrier, n_z + 1)
            greet(go_z, sibling)

        @pl.when(core == 0)
        def _():
            pl.semaphore_wait(go_z, 1)

        for copy in pair:
            copy.start()
        send_over_z()

    for chip_block in range(1, n):

        @pl.when(chip_block > me)
        def _():
            part = slice(chip_block * span, (chip_block + 1) * span)
            kv[:, part, :] = jnp.zeros((2, span, DH), kv.dtype)

    def iota(shape, dim):
        return lax.broadcasted_iota(jnp.int32, shape, dim)

    for load in loads[:5]:
        load.wait()
    for copy in pair:
        copy.wait_recv()

    square = (chunk, chunk)
    at_row, at_col = iota(square, 0), iota(square, 1)
    eye, tri = at_row == at_col, at_row >= at_col
    doc_row = jnp.concatenate([doc_v[0], doc_v[1]], axis=1).astype(jnp.float32)
    doc_col = jnp.sum(jnp.where(eye, doc_row, 0.0), axis=1, keepdims=True)
    doc_last = doc_row[:, chunk - 1 : chunk]
    first_f = first.astype(jnp.float32)
    is_open = tri & (at_col + first >= doc_col.astype(jnp.int32))
    sums[...] = jnp.zeros_like(sums)
    for i in range(group):
        head = pl.ds(group * core + i, 1)
        decay = jnp.concatenate([ld_v[0, head, :], ld_v[1, head, :]], axis=1)
        column = jnp.sum(jnp.where(tri, decay, 0.0), axis=1, keepdims=True)
        total = jnp.sum(decay, axis=1, keepdims=True)
        sums[i : i + 1, :] = jnp.broadcast_to(total, (1, DH))
        col_v[i] = column
        part = slice(i * DH, (i + 1) * DH)
        keep = jnp.where(doc_col == doc_last, jnp.exp(total - column), 0.0)
        values = lin_all[2, :, part].astype(jnp.float32) * keep
        high = values.astype(jnp.bfloat16)
        low = (values - high.astype(jnp.float32)).astype(jnp.bfloat16)
        both = lax.dot_general(
            lin_all[1, :, part], jnp.concatenate([high, low], axis=1), TN,
            preferred_element_type=jnp.float32,
        )
        fresh = both[:, :DH] + both[:, DH:]
        state_f[i] = fresh
        state[i] = fresh.astype(jnp.bfloat16)

    @pl.when(early)
    def _():
        @pl.when((chip == 0) | (chip == 2))
        def _():
            sums_to.start()
            for i in range(group):
                state_to(i, following).start()

        @pl.when(core == 1)
        def _():
            pl.semaphore_wait(barrier, n_z)
            greet(go_z, sibling)

        @pl.when(core == 0)
        def _():
            pl.semaphore_wait(go_z, 1)

        send_over_z()

    @pl.when(jnp.logical_not(early))
    def _():
        @pl.when(core == 0)
        def _():
            @pl.when(chip < chips - 1)
            def _():
                pl.semaphore_wait(barrier, n_xy)

            greet(go_xy, sibling)

        @pl.when(core == 1)
        def _():
            pl.semaphore_wait(go_xy, 1)

        @pl.when((chip == 0) | (chip == 2))
        def _():
            sums_to.start()
            for i in range(group):
                state_to(i, following).start()

    @pl.when((chip == 1) & (core == 0))
    def _():
        greet(far_in, {"seq": 0})
        greet(far_in, {"seq": 1})

    for i in range(group):
        part = slice(i * DH, (i + 1) * DH)
        column = col_v[i]
        row = jnp.sum(jnp.where(eye, column, 0.0), axis=0, keepdims=True)
        values = lin_all[2, :, part]
        score = lax.dot_general(
            lin_all[0, :, part], lin_all[1, :, part], NT, preferred_element_type=jnp.float32
        )
        mix = jnp.where(is_open, score * jnp.exp(column - row), 0.0)
        high = mix.astype(jnp.bfloat16)
        low = (mix - high.astype(jnp.float32)).astype(jnp.bfloat16)
        inner[i] = jnp.dot(
            jnp.concatenate([high, low], axis=1), jnp.concatenate([values, values], axis=0),
            preferred_element_type=jnp.float32,
        )

    eye_s = iota((span, span), 0) == iota((span, span), 1)
    own_doc = jnp.sum(
        jnp.where(eye_s, doc_v[core].astype(jnp.float32), 0.0), axis=1, keepdims=True
    )
    place = me * span + iota((span, tokens), 0)
    key_at = iota((span, tokens), 1)
    open_s = (key_at <= place) & (key_at >= own_doc.astype(jnp.int32))
    half = jnp.where(open_s, 0.0, masked_score)
    bias[0:span, :] = half
    bias[span : 2 * span, :] = half

    own_kv.wait()
    for peer in head_peers:
        there = kv.at[:, own_rows(me * m + peer, rows), :]
        remote(there, there, kv1_s.at[0], kv1_r.at[peer], {"head": peer}).wait_recv()

    @pl.when(chip == 0)
    def _():
        pl.semaphore_wait(far_in, 1)

    for copy, peer in zip(kv2, seq_peers):
        pl.when(peer > me)(copy.start)

    def arrived_a(i):
        remote(state_a.at[i], state_a.at[i], a_s.at[i], a_r.at[i], sibling).wait_recv()

    def arrived_b(i):
        remote(state_b.at[i], state_b.at[i], b_s.at[0, i], b_r.at[i], sibling).wait_recv()

    @pl.when(chip == 1)
    def _():
        joined = jnp.where(doc_last < first_f, 1.0, 0.0)
        for i in range(group):
            arrived_a(i)
            factor = jnp.exp(sums[i : i + 1, 0:1]) * joined
            carried = state_f[i] + factor * state_a[i].astype(jnp.float32)
            state[i] = carried.astype(jnp.bfloat16)
            carry_to(i, 2).start()
            carry_to(i, 3).start()

    loads[7].wait()
    for peer in head_peers:
        there = qs.at[own_rows(peer, rows), :]
        remote(there, there, qs_s.at[0], qs_r.at[peer], {"head": peer}).wait_recv()
    for source in range(n - 1):

        @pl.when(source < me)
        def _():
            there = kv.at[:, source * span : (source + 1) * span, :]
            remote(there, there, kv2_s.at[0], kv2_r.at[source], {"seq": source}).wait_recv()

    stores = []
    for i in range(heads // 2):
        queries = jnp.concatenate(
            [qs[:, g * DH : (g + 1) * DH] for g in (2 * i, 2 * i + 1)], axis=0
        )
        score = lax.dot_general(queries, kv[0], NT, preferred_element_type=jnp.float32)
        score = score * DH ** (-0.5) + bias[...]
        top = jnp.max(score, axis=1, keepdims=True)
        weight = jnp.exp(score - top)
        total = jnp.sum(weight, axis=1, keepdims=True)
        out = jnp.dot(weight.astype(jnp.bfloat16), kv[1], preferred_element_type=jnp.float32)
        out = (out / total).astype(jnp.bfloat16)
        lse = top + jnp.log(total)
        for b in range(2):
            g = 2 * i + b
            part = slice(b * span, (b + 1) * span)
            soft_v[:, g * DH : (g + 1) * DH] = out[part]
            lse_v[g : g + 1, :] = jnp.sum(
                jnp.where(eye_s, lse[part], 0.0), axis=0, keepdims=True
            )
        both_heads = slice(2 * i * DH, 2 * (i + 1) * DH)
        stores.append(
            pltpu.make_async_copy(
                soft_v.at[:, both_heads], soft_out.at[:, both_heads], loc_sem.at[10 + i]
            )
        )
        stores[-1].start()
    stores.append(pltpu.make_async_copy(lse_v, lse_out, loc_sem.at[10 + heads // 2]))
    stores[-1].start()

    @pl.when(chip == 3)
    def _():
        remote(sums_a, sums_a, a_s.at[group], a_r.at[group], sibling).wait_recv()
        for i in range(group):
            arrived_a(i)

    @pl.when(chip == 1)
    def _():
        remote(sums_a, sums_a, a_s.at[group], a_r.at[group], sibling).wait_recv()

    result = lin_v.at[own_rows(other, span), :]
    back = remote(result, lin_out.at[:, mine], out_s, out_r, sibling)
    for i in range(group):
        part = slice(i * DH, (i + 1) * DH)
        queries = lin_all[0, :, part]
        column = col_v[i]

        def read(held, bound, gap):
            got = jnp.dot(queries, held, preferred_element_type=jnp.float32)
            inner[i] += jnp.where(doc_col < bound, jnp.exp(gap), 0.0) * got

        @pl.when(lax.rem(chip, 2) == 1)
        def _():
            read(state_a[i], first_f, column)

        @pl.when(chip >= 2)
        def _():
            arrived_b(i)

        @pl.when(chip == 2)
        def _():
            read(state_b[i], first_f, column)

        @pl.when(chip == 3)
        def _():
            read(state_b[i], first_f - chunk, column + sums_a[i : i + 1, 0:1])

        out = inner[i]
        normed = out * lax.rsqrt(jnp.mean(out * out, axis=1, keepdims=True) + 1e-06)
        lin_v[:, part] = normed.astype(jnp.bfloat16)
    back.start()
    own_out = pltpu.make_async_copy(lin_v.at[here, :], lin_out.at[:, mine], loc_sem.at[9])
    own_out.start()

    for copy in pair + kv1 + qsc:
        copy.wait_send()
    for copy, peer in zip(kv2, seq_peers):
        pl.when(peer > me)(copy.wait_send)

    @pl.when((chip == 0) | (chip == 2))
    def _():
        sums_to.wait_send()
        for i in range(group):
            state_to(i, following).wait_send()

    @pl.when(chip == 1)
    def _():
        for i in range(group):
            carry_to(i, 2).wait_send()
            carry_to(i, 3).wait_send()

    own_out.wait()
    for copy in stores:
        copy.wait()
    back.wait_send()
    there = lin_out.at[:, theirs]
    remote(there, there, out_s, out_r, sibling).wait_recv()


def fused(n, m, query_lin, key_lin, value_lin, log_decay, query_soft, key_soft, value_soft, doc_start):
    span, heads = query_lin.shape[0], log_decay.shape[0]
    tokens, rows = n * span, query_soft.shape[0]
    chunk, group = 2 * span, heads // 2
    bf16, f32 = jnp.bfloat16, jnp.float32
    any_spec = pl.BlockSpec(memory_space=pl.ANY)
    hbm_spec = pl.BlockSpec(memory_space=pltpu.HBM)
    dma = pltpu.SemaphoreType.DMA
    regular = pltpu.SemaphoreType.REGULAR
    results = pl.pallas_call(
        functools.partial(fused_kernel, n, m),
        out_shape=(
            jax.ShapeDtypeStruct((span, heads * DH), bf16),
            jax.ShapeDtypeStruct((span, heads * DH), bf16),
            jax.ShapeDtypeStruct((heads, span), f32),
        ),
        in_specs=[any_spec] * 8,
        out_specs=(any_spec,) * 3,
        scratch_shapes=[
            pltpu.VMEM((3, chunk, group * DH), bf16),
            pltpu.VMEM((2, heads, span), f32),
            pltpu.VMEM((2, 1, span), jnp.int32),
            pltpu.VMEM((group, DH, DH), f32),
            pltpu.VMEM((group, DH, DH), bf16),
            pltpu.VMEM((8, DH), f32),
            pltpu.VMEM((8, DH), f32),
            pltpu.VMEM((group, DH, DH), bf16),
            pltpu.VMEM((group, DH, DH), bf16),
            pltpu.VMEM((group, chunk, DH), f32),
            pltpu.VMEM((group, chunk, 1), f32),
            pltpu.VMEM((chunk, group * DH), bf16),
            pltpu.VMEM((span, heads * DH), bf16),
            pltpu.VMEM((2, rows, m * DH), bf16),
            pltpu.VMEM((2, tokens, DH), bf16),
            pltpu.VMEM((span, heads * DH), bf16),
            pltpu.VMEM((heads, span), f32),
            pltpu.VMEM((2 * span, tokens), f32),
            dma((11 + heads // 2,)),
            dma((5,)), dma((5,)),
            dma((m - 1,)), dma((m,)), dma((m - 1,)), dma((m,)),
            dma((n,)), dma((n,)),
            dma((group + 1,)), dma((group + 1,)),
            dma((2, group)), dma((group,)),
            dma, dma, regular, regular, regular,
        ],
        compiler_params=pltpu.CompilerParams(
            collective_id=0, has_side_effects=True, vmem_limit_bytes=32 * 1024 * 1024
        ),
    )(*(pltpu.with_memory_space_constraint(x, pltpu.HBM) for x in (
        query_lin, key_lin, value_lin, log_decay, query_soft, key_soft, value_soft,
        doc_start.reshape(1, span),
    )))
    return pl.pallas_call(
        store_kernel,
        out_shape=tuple(jax.ShapeDtypeStruct(part.shape, part.dtype) for part in results),
        in_specs=[any_spec] * 3,
        out_specs=(hbm_spec,) * 3,
        scratch_shapes=[dma((3,))],
    )(*(pltpu.with_memory_space_constraint(part, pltpu.VMEM) for part in results))


def store_kernel(a, b, c, a_out, b_out, c_out, sem):
    copies = [
        pltpu.make_async_copy(src, dst, sem.at[i])
        for i, (src, dst) in enumerate(((a, a_out), (b, b_out), (c, c_out)))
    ]
    for copy in copies:
        copy.start()
    for copy in copies:
        copy.wait()


def per_device(
    query_lin, key_lin, value_lin, log_decay, query_soft, key_soft, value_soft, doc_start
):
    n, m = lax.axis_size("seq"), lax.axis_size("head")
    span, heads = query_lin.shape[0], log_decay.shape[0]
    if heads == n == 8 and m == 4 and span == DH // 2 and key_soft.shape[1] == m * DH:
        return fused(
            n, m, query_lin, key_lin, value_lin, log_decay,
            query_soft, key_soft, value_soft, doc_start,
        )
    lin_out = lightning_part(query_lin, key_lin, value_lin, log_decay, doc_start)
    soft_out, soft_lse = softmax_part(query_soft, key_soft, value_soft, doc_start)
    return (lin_out, soft_out, soft_lse)


def solution(mesh):
    return jax.shard_map(
        per_device,
        mesh=mesh,
        in_specs=(
            P("seq", "head"),
            P("seq", "head"),
            P("seq", "head"),
            P("head", "seq"),
            P(("seq", "head"), None),
            P(("seq", "head"), None),
            P(("seq", "head"), None),
            P("seq"),
        ),
        out_specs=(P("seq", "head"), P("seq", "head"), P("head", "seq")),
        check_vma=False,
    )
```

```python
import functools

import jax
import jax.numpy as jnp
from jax import lax
from jax.experimental import pallas as pl
from jax.experimental.pallas import tpu as pltpu
from jax.sharding import PartitionSpec as P


DH = 128


HIGHEST = lax.Precision.HIGHEST
masked_score = -1e30


def prefix(array, axis, combine, identity):
    size, here = (lax.axis_size(axis), lax.axis_index(axis))
    everything = jax.tree.map(lambda part: lax.all_gather(part, axis), array)
    start = jax.tree.map(
        lambda part, zero: jnp.broadcast_to(jnp.asarray(zero, part.dtype), part.shape),
        array,
        identity,
    )

    def lap(k, before):
        reached = k < here
        new = combine(before, jax.tree.map(lambda part: part[k], everything))
        return jax.tree.map(lambda a, b: jnp.where(reached, a, b), new, before)

    return lax.fori_loop(0, size, lap, start)


def span_terms(query_heads, key_heads, value_heads, decay_rows, doc_rows, first_place):
    span_len = query_heads.shape[0]
    places = jnp.arange(span_len, dtype=jnp.int32)
    not_later = places[None, :] <= places[:, None]
    cumulative = jnp.sum(jnp.where(not_later[None], decay_rows[:, None, :], 0.0), axis=2)
    totals = cumulative[:, -1]
    token_positions = first_place + jnp.arange(span_len, dtype=jnp.int32)
    allowed = (token_positions[None, :] <= token_positions[:, None]) & (
        doc_rows[:, None] <= token_positions[None, :]
    )
    decay_gap = jnp.where(allowed[None], cumulative[:, :, None] - cumulative[:, None, :], 0.0)
    decay_mat = jnp.where(allowed[None], jnp.exp(decay_gap), 0.0)
    scores = jnp.einsum("thd,shd->hts", query_heads, key_heads, preferred_element_type=jnp.float32)
    key_float = key_heads.astype(jnp.float32)
    value_float = value_heads.astype(jnp.float32)
    inner_part = jnp.einsum("hts,shd->thd", scores * decay_mat, value_float, precision=HIGHEST)
    keep_mask = (doc_rows == doc_rows[-1]).astype(jnp.float32)
    tail_weight = jnp.exp(totals[:, None] - cumulative) * keep_mask[None, :]
    weighted_keys = key_float * jnp.transpose(tail_weight)[:, :, None]
    fresh_state = jnp.einsum("shd,she->hde", weighted_keys, value_float, precision=HIGHEST)
    carry_on = (doc_rows[-1] < first_place).astype(jnp.float32)
    factor = jnp.exp(totals) * carry_on
    read_mask = (doc_rows < first_place).astype(jnp.float32)[:, None] * jnp.transpose(
        jnp.exp(cumulative)
    )
    return (inner_part, fresh_state, factor, read_mask)


def combine_states(earlier, later_part):
    return (earlier[0] * later_part[0], later_part[0][:, None, None] * earlier[1] + later_part[1])


def lightning_part(query_lin, key_lin, value_lin, log_decay, doc_start):
    span_len = query_lin.shape[0]
    head_count = log_decay.shape[0]
    first_place = lax.axis_index("seq") * span_len
    query_heads = query_lin.reshape(span_len, head_count, DH)
    key_heads = key_lin.reshape(span_len, head_count, DH)
    value_heads = value_lin.reshape(span_len, head_count, DH)
    inner_part, fresh_state, factor, read_mask = span_terms(
        query_heads, key_heads, value_heads, log_decay, doc_start, first_place
    )
    identity = (jnp.ones((head_count,), jnp.float32), jnp.zeros((head_count, DH, DH), jnp.float32))
    unused, carried = prefix((factor, fresh_state), "seq", combine_states, identity)
    outer_part = (
        jnp.einsum("thd,hde->the", query_heads.astype(jnp.float32), carried, precision=HIGHEST)
        * read_mask[:, :, None]
    )
    mixed_out = inner_part + outer_part
    normed = mixed_out * lax.rsqrt(jnp.mean(mixed_out * mixed_out, axis=-1, keepdims=True) + 1e-06)
    return normed.astype(jnp.bfloat16).reshape(span_len, head_count * DH)


def softmax_part(query_soft, key_soft, value_soft, doc_start):
    queries, keys_local, values_local = (
        lax.all_to_all(query_soft, "head", split_axis=1, concat_axis=0, tiled=True),
        lax.all_to_all(key_soft, "head", split_axis=1, concat_axis=0, tiled=True),
        lax.all_to_all(value_soft, "head", split_axis=1, concat_axis=0, tiled=True),
    )
    span_len = queries.shape[0]
    kv_count = keys_local.shape[1] // DH
    group_size = queries.shape[1] // keys_local.shape[1]
    first_place = lax.axis_index("seq") * span_len
    query_places = first_place + jnp.arange(span_len, dtype=jnp.int32)
    query_heads = queries.reshape(span_len, kv_count, group_size, DH)
    score_scale = DH ** (-0.5)
    start_state = (
        jnp.full((span_len, kv_count, group_size), masked_score, jnp.float32),
        jnp.zeros((span_len, kv_count, group_size), jnp.float32),
        jnp.zeros((span_len, kv_count, group_size, DH), jnp.float32),
    )
    key_piece = lax.all_gather(keys_local, "seq", axis=0, tiled=True)
    value_piece = lax.all_gather(values_local, "seq", axis=0, tiled=True)
    piece_rows = key_piece.shape[0]
    block_rows = max(
        (divisor for divisor in range(1, min(piece_rows, 1024) + 1) if piece_rows % divisor == 0)
    )
    block_count = piece_rows // block_rows
    key_parts = key_piece.reshape(block_count, block_rows, kv_count, DH)
    value_parts = value_piece.reshape(block_count, block_rows, kv_count, DH)
    begin_rows = jnp.int32(0) + block_rows * jnp.arange(block_count, dtype=jnp.int32)

    def absorb_block(running, slices):
        key_block, value_block, begin_row = slices
        running_max, norm_sum, accum_out = running
        token_positions = begin_row + jnp.arange(block_rows, dtype=jnp.int32)
        allowed = (token_positions[None, :] <= query_places[:, None]) & (
            doc_start[:, None] <= token_positions[None, :]
        )
        allowed = allowed[:, None, None, :]
        scores = (
            jnp.einsum("tkgd,skd->tkgs", query_heads, key_block, preferred_element_type=jnp.float32)
            * score_scale
        )
        new_max = jnp.maximum(
            running_max, jnp.max(jnp.where(allowed, scores, masked_score), axis=-1)
        )
        raw_weight = jnp.where(allowed, jnp.exp(scores - new_max[..., None]), 0.0)
        shrink = jnp.exp(running_max - new_max)
        norm_sum = norm_sum * shrink + jnp.sum(raw_weight, axis=-1)
        accum_out = accum_out * shrink[..., None] + jnp.einsum(
            "tkgs,skd->tkgd",
            raw_weight.astype(jnp.bfloat16),
            value_block,
            preferred_element_type=jnp.float32,
        )
        running = (new_max, norm_sum, accum_out)
        return (running, None)

    final_state, unused = lax.scan(absorb_block, start_state, (key_parts, value_parts, begin_rows))
    running_max, norm_sum, accum_out = final_state
    soft_out = (
        (accum_out / norm_sum[..., None])
        .astype(jnp.bfloat16)
        .reshape(span_len, kv_count * group_size * DH)
    )
    soft_lse = jnp.transpose(
        (running_max + jnp.log(norm_sum)).reshape(span_len, kv_count * group_size)
    )
    return (soft_out, soft_lse)


MESH = pl.DeviceIdType.MESH
NT = (((1,), (1,)), ((), ()))


TN = (((0,), (0,)), ((), ()))


def fused_kernel(
    n, m, q_in, k_in, v_in, ld_in, qs_in, ks_in, vs_in, doc_in,
    lin_out, soft_out, lse_out,
    lin_all, theirs_v, ld_v, doc_v, fresh, fresh_x, state_f, state, got, sums, sums_got,
    inner, lin_v, qs, kv, soft_v, lse_v, bias, part_o, part_m, part_l,
    loc_sem, pair_s, pair_r, kv1_s, kv1_r, qs_s, qs_r, kv2_s, kvb_r, fwd_s,
    got_s, got_r, sums_s, sums_r, out_s, out_r, go_xy, go_z, far_in,
):
    span, heads = doc_in.shape[1], ld_in.shape[0]
    rows = qs_in.shape[0]
    chips, group, chunk = n // 2, heads // 2, 2 * span
    width = group * DH
    reach = chips * span
    bf16, f32 = jnp.bfloat16, jnp.float32
    me, hd = lax.axis_index("seq"), lax.axis_index("head")
    chip, core = me // 2, lax.rem(me, 2)
    other = 1 - core
    sibling = {"seq": 2 * chip + other}
    first = chip * chunk
    head_peers = [j + jnp.where(j >= hd, 1, 0) for j in range(m - 1)]

    def cols(index, size=DH):
        return pl.ds(pl.multiple_of(index * size, size), size)

    def own_rows(index, count):
        return pl.ds(pl.multiple_of(index * count, count), count)

    def greet(semaphore, device):
        pl.semaphore_signal(semaphore, inc=1, device_id=device, device_id_type=MESH)

    def remote(src, dst, send, recv, device):
        return pltpu.make_async_remote_copy(
            src_ref=src, dst_ref=dst, send_sem=send, recv_sem=recv,
            device_id=device, device_id_type=MESH,
        )

    barrier = pltpu.get_barrier_semaphore()
    for peer in head_peers:
        greet(barrier, {"seq": 2 * chip + 1, "head": peer})
    early = hd < m // 2
    late = jnp.logical_not(early)

    @pl.when((core == 1) & early)
    def _():
        greet(barrier, {"seq": me - 1})

    @pl.when((core == 0) & late)
    def _():
        greet(barrier, {"seq": me + 1})

    for source, targets in ((0, (1,)), (1, (0, 2, 3)), (2, (3,))):
        for target in targets:

            @pl.when(chip == target)
            def _():
                greet(barrier, {"seq": 2 * source})

    my_cols, their_cols = cols(core, width), cols(other, width)
    here = own_rows(core, span)
    kv_rows = own_rows(chip * m + hd, rows)
    loads = [
        pltpu.make_async_copy(ld_in, ld_v.at[core], loc_sem.at[0]),
        pltpu.make_async_copy(doc_in, doc_v.at[core], loc_sem.at[1]),
        pltpu.make_async_copy(k_in.at[:, their_cols], theirs_v.at[0], loc_sem.at[2]),
        pltpu.make_async_copy(v_in.at[:, their_cols], theirs_v.at[1], loc_sem.at[3]),
        pltpu.make_async_copy(k_in.at[:, my_cols], lin_all.at[1, here, :], loc_sem.at[4]),
        pltpu.make_async_copy(v_in.at[:, my_cols], lin_all.at[2, here, :], loc_sem.at[5]),
        pltpu.make_async_copy(q_in.at[:, my_cols], lin_all.at[0, here, :], loc_sem.at[6]),
        pltpu.make_async_copy(ks_in.at[:, cols(hd)], kv.at[core, 0, kv_rows, :], loc_sem.at[7]),
        pltpu.make_async_copy(vs_in.at[:, cols(hd)], kv.at[core, 1, kv_rows, :], loc_sem.at[8]),
        pltpu.make_async_copy(
            qs_in.at[:, cols(hd, heads * DH)], qs.at[own_rows(hd, rows), :], loc_sem.at[9]
        ),
    ]
    for load in loads:
        load.start()

    pair = [
        remote(fresh_x.at[0:2], fresh.at[core, 0:2], pair_s.at[0], pair_r.at[0], sibling),
        remote(fresh_x.at[2:4], fresh.at[core, 2:4], pair_s.at[1], pair_r.at[1], sibling),
        remote(ld_in, ld_v.at[core], pair_s.at[2], pair_r.at[2], sibling),
        remote(doc_in, doc_v.at[core], pair_s.at[3], pair_r.at[3], sibling),
        remote(theirs_v.at[0], lin_all.at[1, here, :], pair_s.at[4], pair_r.at[4], sibling),
        remote(theirs_v.at[1], lin_all.at[2, here, :], pair_s.at[5], pair_r.at[5], sibling),
        remote(q_in.at[:, their_cols], lin_all.at[0, here, :], pair_s.at[6], pair_r.at[6], sibling),
    ]
    kv1, qsc = [], []
    for j, peer in enumerate(head_peers):
        for which, src in enumerate((ks_in, vs_in)):
            kv1.append(
                remote(
                    src.at[:, cols(peer)], kv.at[core, which, kv_rows, :],
                    kv1_s.at[which, j], kv1_r.at[which, hd], {"head": peer},
                )
            )
        qsc.append(
            remote(
                qs_in.at[:, cols(peer, heads * DH)], qs.at[own_rows(hd, rows), :],
                qs_s.at[j], qs_r.at[hd], {"head": peer},
            )
        )

    def kv_block(parity, place):
        return kv.at[parity, :, own_rows(place, span), :]

    def kv_to(target):
        mine = kv_block(core, chip)
        return remote(
            mine, mine, kv2_s.at[target], kvb_r.at[core, chip], {"seq": 2 * target + core}
        )

    def kv_pass(place):
        block = kv_block(core, place)
        return remote(block, block, fwd_s.at[place], kvb_r.at[core, place], sibling)

    def kv_from(parity, place):
        block = kv_block(parity, place)
        return remote(block, block, fwd_s.at[0], kvb_r.at[parity, place], sibling)

    def state_to(i, target):
        return remote(
            state.at[i], got.at[chip, i], got_s.at[target, i], got_r.at[chip, i],
            {"seq": 2 * target + core},
        )

    def state_from(source, i):
        there = got.at[source, i]
        return remote(there, there, got_s.at[0, i], got_r.at[source, i], sibling)

    def sums_to(target):
        return remote(
            sums, sums_got.at[chip], sums_s.at[target], sums_r.at[chip],
            {"seq": 2 * target + core},
        )

    def sums_from(source):
        there = sums_got.at[source]
        return remote(there, there, sums_s.at[0], sums_r.at[source], sibling)

    def send_over_z():
        for copy in kv1 + qsc:
            copy.start()

    n_z = 2 * (m - 1)
    n_xy = jnp.where(chip == 1, 6, 2)

    def told(semaphore):
        pl.semaphore_wait(semaphore, 1)

    @pl.when(late)
    def _():
        @pl.when(core == 1)
        def _():
            pl.semaphore_wait(barrier, n_z + 1)
            greet(go_z, sibling)

        @pl.when(core == 0)
        def _():
            told(go_z)

        send_over_z()
        for copy in pair[2:4]:
            copy.start()

    def iota(shape, dim):
        return lax.broadcasted_iota(jnp.int32, shape, dim)

    def running(values):
        size = values.shape[1]
        upper = jnp.where(iota((size, size), 0) <= iota((size, size), 1), 1.0, 0.0).astype(bf16)
        high = values.astype(bf16)
        rest = values - high.astype(f32)
        middle = rest.astype(bf16)
        low = (rest - middle.astype(f32)).astype(bf16)
        return sum(
            jnp.dot(term, upper, preferred_element_type=f32) for term in (low, middle, high)
        )

    def mine_of(values):
        return jnp.where(core == 0, values[:group], values[group:])

    def theirs_of(values):
        return jnp.where(core == 0, values[group:], values[:group])

    def key_value(keys, values, weight):
        values = values.astype(f32) * weight
        high = values.astype(bf16)
        low = (values - high.astype(f32)).astype(bf16)
        both = lax.dot_general(
            keys, jnp.concatenate([high, low], axis=1), TN, preferred_element_type=f32
        )
        return both[:, :DH] + both[:, DH:]

    for load in loads[:6]:
        load.wait()
    decay = ld_v[core]
    doc_own = doc_v[core]
    summed = running(decay)
    total = jnp.sum(decay, axis=1, keepdims=True)
    weight = jnp.where(doc_own == doc_own[:, span - 1 : span], jnp.exp(total - summed), 0.0)
    weight = jnp.transpose(jnp.concatenate([theirs_of(weight), mine_of(weight)], axis=0))
    for i in range(group):
        part = slice(i * DH, (i + 1) * DH)
        fresh_x[i] = key_value(theirs_v[0, :, part], theirs_v[1, :, part], weight[:, i : i + 1])

    @pl.when(early)
    def _():
        @pl.when(core == 0)
        def _():
            pl.semaphore_wait(barrier, jnp.where(chip == 3, 1, n_xy + 1))
            greet(go_xy, sibling)

        @pl.when(core == 1)
        def _():
            told(go_xy)

        for copy in pair[2:4]:
            copy.start()

    for copy in pair[:2] + pair[4:]:
        copy.start()
    for i in range(group):
        part = slice(i * DH, (i + 1) * DH)
        fresh[core, i] = key_value(
            lin_all[1, here, part], lin_all[2, here, part], weight[:, group + i : group + i + 1]
        )

    @pl.when(late)
    def _():
        @pl.when(core == 0)
        def _():
            @pl.when(chip < chips - 1)
            def _():
                pl.semaphore_wait(barrier, n_xy)

            greet(go_xy, sibling)

        @pl.when(core == 1)
        def _():
            told(go_xy)

    @pl.when((chip == 1) & (core == 0))
    def _():
        greet(far_in, {"seq": 0})
        greet(far_in, {"seq": 1})

    for copy in pair[:4]:
        copy.wait_recv()
    both_decays = jnp.concatenate([ld_v[0], ld_v[1]], axis=1)
    cum = mine_of(running(both_decays))
    second = mine_of(jnp.sum(both_decays[:, span:], axis=1, keepdims=True))
    doc_row = jnp.concatenate([doc_v[0], doc_v[1]], axis=1).astype(f32)
    doc_last = doc_row[:, chunk - 1 : chunk]
    first_f = first.astype(f32)
    sums[...] = jnp.concatenate(
        [jnp.broadcast_to(cum[:, chunk - 1 : chunk], (group, DH)), jnp.zeros((8 - group, DH), f32)],
        axis=0,
    )
    joined = jnp.where(doc_last < first_f + span, jnp.exp(second), 0.0)
    for i in range(group):
        merged = joined[i : i + 1] * fresh[0, i] + fresh[1, i]
        state_f[i] = merged
        state[i] = merged.astype(bf16)
    tree = group // 2

    @pl.when(chip == 0)
    def _():
        for i in range(tree):
            state_to(i, 1).start()
        told(far_in)
        for i in range(tree, group):
            for target in (3, 2, 1):
                state_to(i, target).start()

    @pl.when(chip == 1)
    def _():
        for target in (3, 2):
            sums_to(target).start()
            for i in range(tree, group):
                state_to(i, target).start()

    @pl.when(chip == 2)
    def _():
        sums_to(3).start()
        for i in range(group):
            state_to(i, 3).start()

    @pl.when(early)
    def _():
        @pl.when(core == 1)
        def _():
            pl.semaphore_wait(barrier, n_z)
            greet(go_z, sibling)

        @pl.when(core == 0)
        def _():
            told(go_z)

        send_over_z()

    square = (chunk, chunk)
    at_row, at_col = iota(square, 0), iota(square, 1)
    eye, tri = at_row == at_col, at_row >= at_col
    doc_col = jnp.sum(jnp.where(eye, doc_row, 0.0), axis=1, keepdims=True)
    is_open = tri & (at_col + first >= doc_col.astype(jnp.int32))
    columns = jnp.transpose(jnp.concatenate([cum, jnp.exp(cum)], axis=0))
    loads[6].wait()
    for copy in pair[4:]:
        copy.wait_recv()
    for i in range(group):
        part = slice(i * DH, (i + 1) * DH)
        values = lin_all[2, :, part]
        score = lax.dot_general(
            lin_all[0, :, part], lin_all[1, :, part], NT, preferred_element_type=f32
        )
        mix = jnp.where(is_open, score * jnp.exp(columns[:, i : i + 1] - cum[i : i + 1]), 0.0)
        high = mix.astype(bf16)
        low = (mix - high.astype(f32)).astype(bf16)
        inner[i] = jnp.dot(
            jnp.concatenate([high, low], axis=1), jnp.concatenate([values, values], axis=0),
            preferred_element_type=f32,
        )

    back = [
        remote(
            lin_v.at[own_rows(other, span), pl.ds(half * tree * DH, tree * DH)],
            lin_out.at[:, cols(core * 2 + half, tree * DH)],
            out_s.at[half], out_r.at[half], sibling,
        )
        for half in range(2)
    ]
    own_out = [
        pltpu.make_async_copy(
            lin_v.at[here, pl.ds(half * tree * DH, tree * DH)],
            lin_out.at[:, cols(core * 2 + half, tree * DH)],
            loc_sem.at[10 + half],
        )
        for half in range(2)
    ]

    def finish(i):
        out = inner[i]
        normed = out * lax.rsqrt(jnp.mean(out * out, axis=1, keepdims=True) + 1e-06)
        lin_v[:, i * DH : (i + 1) * DH] = normed.astype(bf16)

    @pl.when(chip == 0)
    def _():
        for i in range(group):
            finish(i)
        for copy in back + own_out:
            copy.start()

    for place in range(chips):
        for parity in range(2):

            @pl.when(2 * place + parity > me)
            def _():
                kv[parity, :, place * span : (place + 1) * span, :] = jnp.zeros(
                    (2, span, DH), kv.dtype
                )

    eye_s = iota((span, span), 0) == iota((span, span), 1)
    own_doc = jnp.sum(jnp.where(eye_s, doc_own.astype(f32), 0.0), axis=1, keepdims=True)
    query_at = me * span + iota((span, reach), 0)
    slot = iota((span, reach), 1)
    for side in range(2):
        parity = core if side == 0 else other
        key_at = slot + (slot // span + parity) * span
        open_s = (key_at <= query_at) & (key_at >= own_doc.astype(jnp.int32))
        half = jnp.where(open_s, 0.0, masked_score)
        bias[side, 0:span, :] = half
        bias[side, span : 2 * span, :] = half

    for load in loads[7:9]:
        load.wait()
    for peer in head_peers:
        for which in range(2):
            there = kv.at[core, which, own_rows(chip * m + peer, rows), :]
            remote(
                there, there, kv1_s.at[which, 0], kv1_r.at[which, peer], {"head": peer}
            ).wait_recv()
    for target in (3, 2, 1):
        pl.when(chip < target)(kv_to(target).start)
    pl.when(core == 0)(kv_pass(chip).start)

    @pl.when(chip == 1)
    def _():
        linked = jnp.where(doc_last < first_f, 1.0, 0.0)
        for i in range(tree):
            state_from(0, i).wait_recv()
            factor = jnp.exp(sums[i : i + 1, 0:1]) * linked
            state[i] = (state_f[i] + factor * got[0, i].astype(f32)).astype(bf16)
            for target in (3, 2):
                state_to(i, target).start()

    def read(i, source, gap):
        known = doc_col < ((source + 1) * chunk)
        scale = columns[:, group + i : group + i + 1] * jnp.exp(gap)
        carried = jnp.dot(
            lin_all[0, :, i * DH : (i + 1) * DH], got[source, i], preferred_element_type=f32
        )
        inner[i] += jnp.where(known, scale, 0.0) * carried

    none = jnp.zeros((1, 1), f32)

    @pl.when(chip == 2)
    def _():
        sums_from(1).wait_recv()

    @pl.when(chip == 3)
    def _():
        sums_from(1).wait_recv()
        sums_from(2).wait_recv()

    def read_half(half):
        members = range(half * tree, (half + 1) * tree)
        for i in members:
            line = slice(i, i + 1)

            @pl.when(chip == 1)
            def _():
                if half:
                    state_from(0, i).wait_recv()
                read(i, 0, none)

            @pl.when(chip == 2)
            def _():
                if half:
                    state_from(0, i).wait_recv()
                    read(i, 0, sums_got[1, line, 0:1])
                state_from(1, i).wait_recv()
                read(i, 1, none)

            @pl.when(chip == 3)
            def _():
                if half:
                    state_from(0, i).wait_recv()
                    read(i, 0, sums_got[1, line, 0:1] + sums_got[2, line, 0:1])
                state_from(2, i).wait_recv()
                read(i, 2, none)
                state_from(1, i).wait_recv()
                read(i, 1, sums_got[2, line, 0:1])

        @pl.when(chip > 0)
        def _():
            for i in members:
                finish(i)
            back[half].start()
            own_out[half].start()

    read_half(1)
    for place in range(chips - 1):

        @pl.when(place < chip)
        def _():
            kv_from(core, place).wait_recv()
            kv_pass(place).start()

    loads[9].wait()
    for peer in head_peers:
        there = qs.at[own_rows(peer, rows), :]
        remote(there, there, qs_s.at[0], qs_r.at[peer], {"head": peer}).wait_recv()

    def attend(i, side, parity):
        queries = jnp.concatenate(
            [qs[:, g * DH : (g + 1) * DH] for g in (2 * i, 2 * i + 1)], axis=0
        )
        score = lax.dot_general(queries, kv[parity, 0], NT, preferred_element_type=f32)
        score = score * DH ** (-0.5) + bias[side]
        top = jnp.max(score, axis=1, keepdims=True)
        weight = jnp.exp(score - top)
        total = jnp.sum(weight, axis=1, keepdims=True)
        out = jnp.dot(weight.astype(bf16), kv[parity, 1], preferred_element_type=f32)
        return top, total, out

    for i in range(heads // 2):
        part_m[i], part_l[i], part_o[i] = attend(i, 0, core)
    read_half(0)
    for place in range(chips):
        pl.when(place < chip + core)(kv_from(other, place).wait_recv)

    for i in range(heads // 2):
        top_b, total_b, out_b = attend(i, 1, other)
        top_a, total_a = part_m[i], part_l[i]
        top = jnp.maximum(top_a, top_b)
        scale_a, scale_b = jnp.exp(top_a - top), jnp.exp(top_b - top)
        total = total_a * scale_a + total_b * scale_b
        out = ((part_o[i] * scale_a + out_b * scale_b) / total).astype(bf16)
        lse = top + jnp.log(total)
        for b in range(2):
            g = 2 * i + b
            part = slice(b * span, (b + 1) * span)
            soft_v[:, g * DH : (g + 1) * DH] = out[part]
            lse_v[g : g + 1, :] = jnp.sum(
                jnp.where(eye_s, lse[part], 0.0), axis=0, keepdims=True
            )
    stores = [
        pltpu.make_async_copy(soft_v, soft_out, loc_sem.at[12]),
        pltpu.make_async_copy(lse_v, lse_out, loc_sem.at[13]),
    ]
    for store in stores:
        store.start()

    for copy in pair + kv1 + qsc:
        copy.wait_send()
    for target in (3, 2, 1):
        pl.when(chip < target)(kv_to(target).wait_send)
    pl.when(core == 0)(kv_pass(chip).wait_send)
    for place in range(chips - 1):
        pl.when(place < chip)(kv_pass(place).wait_send)

    @pl.when(chip == 0)
    def _():
        for i in range(group):
            for target in (3, 2, 1) if i >= tree else (1,):
                state_to(i, target).wait_send()

    @pl.when(chip == 1)
    def _():
        for target in (3, 2):
            sums_to(target).wait_send()
            for i in range(group):
                state_to(i, target).wait_send()

    @pl.when(chip == 2)
    def _():
        sums_to(3).wait_send()
        for i in range(group):
            state_to(i, 3).wait_send()

    for copy in own_out + stores:
        copy.wait()
    for half in (1, 0):
        back[half].wait_send()
        there = lin_out.at[:, cols(other * 2 + half, tree * DH)]
        remote(there, there, out_s.at[half], out_r.at[half], sibling).wait_recv()


def fused(n, m, query_lin, key_lin, value_lin, log_decay, query_soft, key_soft, value_soft, doc_start):
    span, heads = query_lin.shape[0], log_decay.shape[0]
    rows = query_soft.shape[0]
    chips, chunk, group = n // 2, 2 * span, heads // 2
    bf16, f32 = jnp.bfloat16, jnp.float32
    any_spec = pl.BlockSpec(memory_space=pl.ANY)
    hbm_spec = pl.BlockSpec(memory_space=pltpu.HBM)
    dma = pltpu.SemaphoreType.DMA
    regular = pltpu.SemaphoreType.REGULAR
    results = pl.pallas_call(
        functools.partial(fused_kernel, n, m),
        out_shape=(
            jax.ShapeDtypeStruct((span, heads * DH), bf16),
            jax.ShapeDtypeStruct((span, heads * DH), bf16),
            jax.ShapeDtypeStruct((heads, span), f32),
        ),
        in_specs=[any_spec] * 8,
        out_specs=(any_spec,) * 3,
        scratch_shapes=[
            pltpu.VMEM((3, chunk, group * DH), bf16),
            pltpu.VMEM((2, span, group * DH), bf16),
            pltpu.VMEM((2, heads, span), f32),
            pltpu.VMEM((2, 1, span), jnp.int32),
            pltpu.VMEM((2, group, DH, DH), f32),
            pltpu.VMEM((group, DH, DH), f32),
            pltpu.VMEM((group, DH, DH), f32),
            pltpu.VMEM((group, DH, DH), bf16),
            pltpu.VMEM((chips - 1, group, DH, DH), bf16),
            pltpu.VMEM((8, DH), f32),
            pltpu.VMEM((chips - 1, 8, DH), f32),
            pltpu.VMEM((group, chunk, DH), f32),
            pltpu.VMEM((chunk, group * DH), bf16),
            pltpu.VMEM((span, heads * DH), bf16),
            pltpu.VMEM((2, 2, chips * span, DH), bf16),
            pltpu.VMEM((span, heads * DH), bf16),
            pltpu.VMEM((heads, span), f32),
            pltpu.VMEM((2, 2 * span, chips * span), f32),
            pltpu.VMEM((heads // 2, chunk, DH), f32),
            pltpu.VMEM((heads // 2, chunk, 1), f32),
            pltpu.VMEM((heads // 2, chunk, 1), f32),
            dma((14,)),
            dma((7,)), dma((7,)),
            dma((2, m - 1)), dma((2, m)), dma((m - 1,)), dma((m,)),
            dma((chips,)), dma((2, chips)), dma((chips,)),
            dma((chips, group)), dma((chips - 1, group)), dma((chips,)), dma((chips - 1,)),
            dma((2,)), dma((2,)), regular, regular, regular,
        ],
        compiler_params=pltpu.CompilerParams(
            collective_id=0, has_side_effects=True, vmem_limit_bytes=32 * 1024 * 1024
        ),
    )(*(pltpu.with_memory_space_constraint(x, pltpu.HBM) for x in (
        query_lin, key_lin, value_lin, log_decay, query_soft, key_soft, value_soft,
        doc_start.reshape(1, span),
    )))
    return pl.pallas_call(
        store_kernel,
        out_shape=tuple(jax.ShapeDtypeStruct(part.shape, part.dtype) for part in results),
        in_specs=[any_spec] * 3,
        out_specs=(hbm_spec,) * 3,
        scratch_shapes=[dma((3,))],
    )(*(pltpu.with_memory_space_constraint(part, pltpu.VMEM) for part in results))


def store_kernel(a, b, c, a_out, b_out, c_out, sem):
    copies = [
        pltpu.make_async_copy(src, dst, sem.at[i])
        for i, (src, dst) in enumerate(((a, a_out), (b, b_out), (c, c_out)))
    ]
    for copy in copies:
        copy.start()
    for copy in copies:
        copy.wait()


def per_device(
    query_lin, key_lin, value_lin, log_decay, query_soft, key_soft, value_soft, doc_start
):
    n, m = lax.axis_size("seq"), lax.axis_size("head")
    span, heads = query_lin.shape[0], log_decay.shape[0]
    if heads == n == 8 and m == 4 and span == DH // 2 and key_soft.shape[1] == m * DH:
        return fused(
            n, m, query_lin, key_lin, value_lin, log_decay,
            query_soft, key_soft, value_soft, doc_start,
        )
    lin_out = lightning_part(query_lin, key_lin, value_lin, log_decay, doc_start)
    soft_out, soft_lse = softmax_part(query_soft, key_soft, value_soft, doc_start)
    return (lin_out, soft_out, soft_lse)


def solution(mesh):
    return jax.shard_map(
        per_device,
        mesh=mesh,
        in_specs=(
            P("seq", "head"),
            P("seq", "head"),
            P("seq", "head"),
            P("head", "seq"),
            P(("seq", "head"), None),
            P(("seq", "head"), None),
            P(("seq", "head"), None),
            P("seq"),
        ),
        out_specs=(P("seq", "head"), P("seq", "head"), P("head", "seq")),
        check_vma=False,
    )
```

```python
import functools

import jax
import jax.numpy as jnp
from jax import lax
from jax.experimental import pallas as pl
from jax.experimental.pallas import tpu as pltpu
from jax.sharding import PartitionSpec as P


DH = 128


HIGHEST = lax.Precision.HIGHEST
masked_score = -1e30


def prefix(array, axis, combine, identity):
    size, here = (lax.axis_size(axis), lax.axis_index(axis))
    everything = jax.tree.map(lambda part: lax.all_gather(part, axis), array)
    start = jax.tree.map(
        lambda part, zero: jnp.broadcast_to(jnp.asarray(zero, part.dtype), part.shape),
        array,
        identity,
    )

    def lap(k, before):
        reached = k < here
        new = combine(before, jax.tree.map(lambda part: part[k], everything))
        return jax.tree.map(lambda a, b: jnp.where(reached, a, b), new, before)

    return lax.fori_loop(0, size, lap, start)


def span_terms(query_heads, key_heads, value_heads, decay_rows, doc_rows, first_place):
    span_len = query_heads.shape[0]
    places = jnp.arange(span_len, dtype=jnp.int32)
    not_later = places[None, :] <= places[:, None]
    cumulative = jnp.sum(jnp.where(not_later[None], decay_rows[:, None, :], 0.0), axis=2)
    totals = cumulative[:, -1]
    token_positions = first_place + jnp.arange(span_len, dtype=jnp.int32)
    allowed = (token_positions[None, :] <= token_positions[:, None]) & (
        doc_rows[:, None] <= token_positions[None, :]
    )
    decay_gap = jnp.where(allowed[None], cumulative[:, :, None] - cumulative[:, None, :], 0.0)
    decay_mat = jnp.where(allowed[None], jnp.exp(decay_gap), 0.0)
    scores = jnp.einsum("thd,shd->hts", query_heads, key_heads, preferred_element_type=jnp.float32)
    key_float = key_heads.astype(jnp.float32)
    value_float = value_heads.astype(jnp.float32)
    inner_part = jnp.einsum("hts,shd->thd", scores * decay_mat, value_float, precision=HIGHEST)
    keep_mask = (doc_rows == doc_rows[-1]).astype(jnp.float32)
    tail_weight = jnp.exp(totals[:, None] - cumulative) * keep_mask[None, :]
    weighted_keys = key_float * jnp.transpose(tail_weight)[:, :, None]
    fresh_state = jnp.einsum("shd,she->hde", weighted_keys, value_float, precision=HIGHEST)
    carry_on = (doc_rows[-1] < first_place).astype(jnp.float32)
    factor = jnp.exp(totals) * carry_on
    read_mask = (doc_rows < first_place).astype(jnp.float32)[:, None] * jnp.transpose(
        jnp.exp(cumulative)
    )
    return (inner_part, fresh_state, factor, read_mask)


def combine_states(earlier, later_part):
    return (earlier[0] * later_part[0], later_part[0][:, None, None] * earlier[1] + later_part[1])


def lightning_part(query_lin, key_lin, value_lin, log_decay, doc_start):
    span_len = query_lin.shape[0]
    head_count = log_decay.shape[0]
    first_place = lax.axis_index("seq") * span_len
    query_heads = query_lin.reshape(span_len, head_count, DH)
    key_heads = key_lin.reshape(span_len, head_count, DH)
    value_heads = value_lin.reshape(span_len, head_count, DH)
    inner_part, fresh_state, factor, read_mask = span_terms(
        query_heads, key_heads, value_heads, log_decay, doc_start, first_place
    )
    identity = (jnp.ones((head_count,), jnp.float32), jnp.zeros((head_count, DH, DH), jnp.float32))
    unused, carried = prefix((factor, fresh_state), "seq", combine_states, identity)
    outer_part = (
        jnp.einsum("thd,hde->the", query_heads.astype(jnp.float32), carried, precision=HIGHEST)
        * read_mask[:, :, None]
    )
    mixed_out = inner_part + outer_part
    normed = mixed_out * lax.rsqrt(jnp.mean(mixed_out * mixed_out, axis=-1, keepdims=True) + 1e-06)
    return normed.astype(jnp.bfloat16).reshape(span_len, head_count * DH)


def softmax_part(query_soft, key_soft, value_soft, doc_start):
    queries, keys_local, values_local = (
        lax.all_to_all(query_soft, "head", split_axis=1, concat_axis=0, tiled=True),
        lax.all_to_all(key_soft, "head", split_axis=1, concat_axis=0, tiled=True),
        lax.all_to_all(value_soft, "head", split_axis=1, concat_axis=0, tiled=True),
    )
    span_len = queries.shape[0]
    kv_count = keys_local.shape[1] // DH
    group_size = queries.shape[1] // keys_local.shape[1]
    first_place = lax.axis_index("seq") * span_len
    query_places = first_place + jnp.arange(span_len, dtype=jnp.int32)
    query_heads = queries.reshape(span_len, kv_count, group_size, DH)
    score_scale = DH ** (-0.5)
    start_state = (
        jnp.full((span_len, kv_count, group_size), masked_score, jnp.float32),
        jnp.zeros((span_len, kv_count, group_size), jnp.float32),
        jnp.zeros((span_len, kv_count, group_size, DH), jnp.float32),
    )
    key_piece = lax.all_gather(keys_local, "seq", axis=0, tiled=True)
    value_piece = lax.all_gather(values_local, "seq", axis=0, tiled=True)
    piece_rows = key_piece.shape[0]
    block_rows = max(
        (divisor for divisor in range(1, min(piece_rows, 1024) + 1) if piece_rows % divisor == 0)
    )
    block_count = piece_rows // block_rows
    key_parts = key_piece.reshape(block_count, block_rows, kv_count, DH)
    value_parts = value_piece.reshape(block_count, block_rows, kv_count, DH)
    begin_rows = jnp.int32(0) + block_rows * jnp.arange(block_count, dtype=jnp.int32)

    def absorb_block(running, slices):
        key_block, value_block, begin_row = slices
        running_max, norm_sum, accum_out = running
        token_positions = begin_row + jnp.arange(block_rows, dtype=jnp.int32)
        allowed = (token_positions[None, :] <= query_places[:, None]) & (
            doc_start[:, None] <= token_positions[None, :]
        )
        allowed = allowed[:, None, None, :]
        scores = (
            jnp.einsum("tkgd,skd->tkgs", query_heads, key_block, preferred_element_type=jnp.float32)
            * score_scale
        )
        new_max = jnp.maximum(
            running_max, jnp.max(jnp.where(allowed, scores, masked_score), axis=-1)
        )
        raw_weight = jnp.where(allowed, jnp.exp(scores - new_max[..., None]), 0.0)
        shrink = jnp.exp(running_max - new_max)
        norm_sum = norm_sum * shrink + jnp.sum(raw_weight, axis=-1)
        accum_out = accum_out * shrink[..., None] + jnp.einsum(
            "tkgs,skd->tkgd",
            raw_weight.astype(jnp.bfloat16),
            value_block,
            preferred_element_type=jnp.float32,
        )
        running = (new_max, norm_sum, accum_out)
        return (running, None)

    final_state, unused = lax.scan(absorb_block, start_state, (key_parts, value_parts, begin_rows))
    running_max, norm_sum, accum_out = final_state
    soft_out = (
        (accum_out / norm_sum[..., None])
        .astype(jnp.bfloat16)
        .reshape(span_len, kv_count * group_size * DH)
    )
    soft_lse = jnp.transpose(
        (running_max + jnp.log(norm_sum)).reshape(span_len, kv_count * group_size)
    )
    return (soft_out, soft_lse)


MESH = pl.DeviceIdType.MESH
NT = (((1,), (1,)), ((), ()))


TN = (((0,), (0,)), ((), ()))


def fused_kernel(
    n, m, q_in, k_in, v_in, ld_in, qs_in, ks_in, vs_in, doc_in,
    lin_out, soft_out, lse_out,
    lin_all, theirs_v, ld_v, doc_v, fresh, fresh_x, state_f, state, got, sums, sums_got,
    inner, lin_v, qs, q_all, kv, soft_v, lse_v, shut_own, shut_past, top_v, total_v, out_v,
    loc_sem, pair_s, pair_r, kv1_s, kv1_r, qs_s, qs_r, kv2_s, kvb_r, fwd_s,
    got_s, got_r, sums_s, sums_r, out_s, out_r, go_xy, go_z, far_in,
):
    span, heads = doc_in.shape[1], ld_in.shape[0]
    rows = qs_in.shape[0]
    chips, group, chunk = n // 2, heads // 2, 2 * span
    width = group * DH
    reach = chips * span
    bf16, f32 = jnp.bfloat16, jnp.float32
    me, hd = lax.axis_index("seq"), lax.axis_index("head")
    chip, core = me // 2, lax.rem(me, 2)
    other = 1 - core
    sibling = {"seq": 2 * chip + other}
    first = chip * chunk
    head_peers = [j + jnp.where(j >= hd, 1, 0) for j in range(m - 1)]

    def cols(index, size=DH):
        return pl.ds(pl.multiple_of(index * size, size), size)

    def own_rows(index, count):
        return pl.ds(pl.multiple_of(index * count, count), count)

    def greet(semaphore, device):
        pl.semaphore_signal(semaphore, inc=1, device_id=device, device_id_type=MESH)

    def remote(src, dst, send, recv, device):
        return pltpu.make_async_remote_copy(
            src_ref=src, dst_ref=dst, send_sem=send, recv_sem=recv,
            device_id=device, device_id_type=MESH,
        )

    barrier = pltpu.get_barrier_semaphore()
    for peer in head_peers:
        greet(barrier, {"seq": 2 * chip + 1, "head": peer})
    early = hd < m - 1
    late = jnp.logical_not(early)

    @pl.when((core == 1) & early)
    def _():
        greet(barrier, {"seq": me - 1})

    @pl.when((core == 0) & late)
    def _():
        greet(barrier, {"seq": me + 1})

    for source, targets in ((0, (1,)), (1, (0, 2, 3)), (2, (3,))):
        for target in targets:

            @pl.when(chip == target)
            def _():
                greet(barrier, {"seq": 2 * source})

    my_cols, their_cols = cols(core, width), cols(other, width)
    here = own_rows(core, span)
    kv_rows = own_rows(chip * m + hd, rows)
    loads = [
        pltpu.make_async_copy(ld_in, ld_v.at[core], loc_sem.at[0]),
        pltpu.make_async_copy(doc_in, doc_v.at[core], loc_sem.at[1]),
        pltpu.make_async_copy(k_in.at[:, their_cols], theirs_v.at[0], loc_sem.at[2]),
        pltpu.make_async_copy(v_in.at[:, their_cols], theirs_v.at[1], loc_sem.at[3]),
        pltpu.make_async_copy(k_in.at[:, my_cols], lin_all.at[1, here, :], loc_sem.at[4]),
        pltpu.make_async_copy(v_in.at[:, my_cols], lin_all.at[2, here, :], loc_sem.at[5]),
        pltpu.make_async_copy(q_in.at[:, my_cols], lin_all.at[0, here, :], loc_sem.at[6]),
        pltpu.make_async_copy(ks_in.at[:, cols(hd)], kv.at[core, 0, kv_rows, :], loc_sem.at[7]),
        pltpu.make_async_copy(vs_in.at[:, cols(hd)], kv.at[core, 1, kv_rows, :], loc_sem.at[8]),
        pltpu.make_async_copy(
            qs_in.at[:, cols(hd, heads * DH)], qs.at[own_rows(hd, rows), :], loc_sem.at[9]
        ),
    ]
    for load in loads:
        load.start()

    pair = [
        remote(fresh_x.at[0:2], fresh.at[core, 0:2], pair_s.at[0], pair_r.at[0], sibling),
        remote(fresh_x.at[2:4], fresh.at[core, 2:4], pair_s.at[1], pair_r.at[1], sibling),
        remote(ld_in, ld_v.at[core], pair_s.at[2], pair_r.at[2], sibling),
        remote(doc_in, doc_v.at[core], pair_s.at[3], pair_r.at[3], sibling),
        remote(theirs_v.at[0], lin_all.at[1, here, :], pair_s.at[4], pair_r.at[4], sibling),
        remote(theirs_v.at[1], lin_all.at[2, here, :], pair_s.at[5], pair_r.at[5], sibling),
        remote(q_in.at[:, their_cols], lin_all.at[0, here, :], pair_s.at[6], pair_r.at[6], sibling),
    ]
    kv1, qsc = [], []
    for j, peer in enumerate(head_peers):
        for which, src in enumerate((ks_in, vs_in)):
            kv1.append(
                remote(
                    src.at[:, cols(peer)], kv.at[core, which, kv_rows, :],
                    kv1_s.at[which, j], kv1_r.at[which, hd], {"head": peer},
                )
            )
        qsc.append(
            remote(
                qs_in.at[:, cols(peer, heads * DH)], qs.at[own_rows(hd, rows), :],
                qs_s.at[j], qs_r.at[hd], {"head": peer},
            )
        )

    def kv_block(parity, place):
        return kv.at[parity, :, own_rows(place, span), :]

    def kv_to(target):
        mine = kv_block(core, chip)
        return remote(
            mine, mine, kv2_s.at[target], kvb_r.at[core, chip], {"seq": 2 * target + core}
        )

    def kv_pass(place):
        block = kv_block(core, place)
        return remote(block, block, fwd_s.at[place], kvb_r.at[core, place], sibling)

    def kv_from(parity, place):
        block = kv_block(parity, place)
        return remote(block, block, fwd_s.at[0], kvb_r.at[parity, place], sibling)

    def state_to(i, target):
        return remote(
            state.at[i], got.at[chip, i], got_s.at[target, i], got_r.at[chip, i],
            {"seq": 2 * target + core},
        )

    def state_from(source, i):
        there = got.at[source, i]
        return remote(there, there, got_s.at[0, i], got_r.at[source, i], sibling)

    def sums_to(target):
        return remote(
            sums, sums_got.at[chip], sums_s.at[target], sums_r.at[chip],
            {"seq": 2 * target + core},
        )

    def sums_from(source):
        there = sums_got.at[source]
        return remote(there, there, sums_s.at[0], sums_r.at[source], sibling)

    def send_over_z():
        for copy in kv1 + qsc:
            copy.start()

    n_z = 2 * (m - 1)
    n_xy = jnp.where(chip == 1, 6, 2)

    def told(semaphore):
        pl.semaphore_wait(semaphore, 1)

    @pl.when(late)
    def _():
        @pl.when(core == 1)
        def _():
            pl.semaphore_wait(barrier, n_z + 1)
            greet(go_z, sibling)

        @pl.when(core == 0)
        def _():
            told(go_z)

        send_over_z()
        for copy in pair[2:4]:
            copy.start()

    def iota(shape, dim):
        return lax.broadcasted_iota(jnp.int32, shape, dim)

    def running(values):
        size = values.shape[1]
        upper = jnp.where(iota((size, size), 0) <= iota((size, size), 1), 1.0, 0.0).astype(bf16)
        high = values.astype(bf16)
        rest = values - high.astype(f32)
        middle = rest.astype(bf16)
        low = (rest - middle.astype(f32)).astype(bf16)
        return sum(
            jnp.dot(term, upper, preferred_element_type=f32) for term in (low, middle, high)
        )

    def mine_of(values):
        return jnp.where(core == 0, values[:group], values[group:])

    def theirs_of(values):
        return jnp.where(core == 0, values[group:], values[:group])

    def key_value(keys, values, weight):
        values = values.astype(f32) * weight
        high = values.astype(bf16)
        low = (values - high.astype(f32)).astype(bf16)
        both = lax.dot_general(
            keys, jnp.concatenate([high, low], axis=1), TN, preferred_element_type=f32
        )
        return both[:, :DH] + both[:, DH:]

    for load in loads[:6]:
        load.wait()
    decay = ld_v[core]
    doc_own = doc_v[core]
    summed = running(decay)
    total = jnp.sum(decay, axis=1, keepdims=True)
    weight = jnp.where(doc_own == doc_own[:, span - 1 : span], jnp.exp(total - summed), 0.0)
    weight = jnp.transpose(jnp.concatenate([theirs_of(weight), mine_of(weight)], axis=0))
    for i in range(group):
        part = slice(i * DH, (i + 1) * DH)
        fresh_x[i] = key_value(theirs_v[0, :, part], theirs_v[1, :, part], weight[:, i : i + 1])

    @pl.when(early)
    def _():
        @pl.when(core == 0)
        def _():
            pl.semaphore_wait(barrier, jnp.where(chip == 3, 1, n_xy + 1))
            greet(go_xy, sibling)

        @pl.when(core == 1)
        def _():
            told(go_xy)

        for copy in pair[2:4]:
            copy.start()

    for copy in pair[:2] + pair[4:]:
        copy.start()
    for i in range(group):
        part = slice(i * DH, (i + 1) * DH)
        fresh[core, i] = key_value(
            lin_all[1, here, part], lin_all[2, here, part], weight[:, group + i : group + i + 1]
        )

    @pl.when(late)
    def _():
        @pl.when(core == 0)
        def _():
            @pl.when(chip < chips - 1)
            def _():
                pl.semaphore_wait(barrier, n_xy)

            greet(go_xy, sibling)

        @pl.when(core == 1)
        def _():
            told(go_xy)

    @pl.when((chip == 1) & (core == 0))
    def _():
        greet(far_in, {"seq": 0})
        greet(far_in, {"seq": 1})

    @pl.when(early & (hd > 0))
    def _():
        @pl.when(core == 1)
        def _():
            pl.semaphore_wait(barrier, n_z)
            greet(go_z, sibling)

        @pl.when(core == 0)
        def _():
            told(go_z)

        send_over_z()

    for copy in pair[:4]:
        copy.wait_recv()
    both_decays = jnp.concatenate([ld_v[0], ld_v[1]], axis=1)
    cum = mine_of(running(both_decays))
    second = mine_of(jnp.sum(both_decays[:, span:], axis=1, keepdims=True))
    doc_row = jnp.concatenate([doc_v[0], doc_v[1]], axis=1).astype(f32)
    doc_last = doc_row[:, chunk - 1 : chunk]
    first_f = first.astype(f32)
    sums[...] = jnp.concatenate(
        [jnp.broadcast_to(cum[:, chunk - 1 : chunk], (group, DH)), jnp.zeros((8 - group, DH), f32)],
        axis=0,
    )
    joined = jnp.where(doc_last < first_f + span, jnp.exp(second), 0.0)
    for i in range(group):
        merged = joined[i : i + 1] * fresh[0, i] + fresh[1, i]
        state_f[i] = merged
        state[i] = merged.astype(bf16)
    tree, side_heads = 2, group // 2

    @pl.when(chip == 0)
    def _():
        for i in range(tree):
            state_to(i, 1).start()
        told(far_in)
        for i in range(tree, group):
            state_to(i, 2).start()

    @pl.when(chip == 1)
    def _():
        for target in (3, 2):
            sums_to(target).start()
        for i in range(tree, group):
            state_to(i, 3).start()

    @pl.when(chip == 2)
    def _():
        sums_to(3).start()
        for i in range(tree):
            state_to(i, 3).start()

    @pl.when(hd == 0)
    def _():
        @pl.when(core == 1)
        def _():
            pl.semaphore_wait(barrier, n_z)
            greet(go_z, sibling)

        @pl.when(core == 0)
        def _():
            told(go_z)

        send_over_z()

    square = (chunk, chunk)
    at_row, at_col = iota(square, 0), iota(square, 1)
    eye, tri = at_row == at_col, at_row >= at_col
    doc_col = jnp.sum(jnp.where(eye, doc_row, 0.0), axis=1, keepdims=True)
    is_open = tri & (at_col + first >= doc_col.astype(jnp.int32))
    columns = jnp.transpose(jnp.concatenate([cum, jnp.exp(cum)], axis=0))
    loads[6].wait()
    for copy in pair[4:]:
        copy.wait_recv()
    for i in range(group):
        part = slice(i * DH, (i + 1) * DH)
        values = lin_all[2, :, part]
        score = lax.dot_general(
            lin_all[0, :, part], lin_all[1, :, part], NT, preferred_element_type=f32
        )
        mix = jnp.where(is_open, score * jnp.exp(columns[:, i : i + 1] - cum[i : i + 1]), 0.0)
        high = mix.astype(bf16)
        low = (mix - high.astype(f32)).astype(bf16)
        inner[i] = jnp.dot(
            jnp.concatenate([high, low], axis=1), jnp.concatenate([values, values], axis=0),
            preferred_element_type=f32,
        )

    @pl.when(chip < 2)
    def _():
        for i in range(tree, group):
            pl.when(chip == 0)(state_to(i, 1).start)
            pl.when(chip == 1)(state_to(i, 2).start)

    back = [
        remote(
            lin_v.at[own_rows(other, span), pl.ds(half * side_heads * DH, side_heads * DH)],
            lin_out.at[:, cols(core * 2 + half, side_heads * DH)],
            out_s.at[half], out_r.at[half], sibling,
        )
        for half in range(2)
    ]
    own_out = [
        pltpu.make_async_copy(
            lin_v.at[here, pl.ds(half * side_heads * DH, side_heads * DH)],
            lin_out.at[:, cols(core * 2 + half, side_heads * DH)],
            loc_sem.at[10 + half],
        )
        for half in range(2)
    ]

    def finish(i):
        out = inner[i]
        normed = out * lax.rsqrt(jnp.mean(out * out, axis=1, keepdims=True) + 1e-06)
        lin_v[:, i * DH : (i + 1) * DH] = normed.astype(bf16)

    @pl.when(chip == 0)
    def _():
        for i in range(group):
            finish(i)
        for copy in back + own_out:
            copy.start()

    for place in range(chips):
        for parity in range(2):

            @pl.when(2 * place + parity > me)
            def _():
                kv[parity, :, place * span : (place + 1) * span, :] = jnp.zeros(
                    (2, span, DH), kv.dtype
                )

    def masked(is_on):
        half = jnp.where(is_on, 0.0, masked_score)
        return jnp.concatenate([half, half], axis=1)

    query_at = me * span + iota((chunk, span), 1)
    key_at = first + iota((chunk, span), 0)
    shut_own[...] = masked((key_at <= query_at) & (key_at >= doc_own))
    past = reach - span
    slot = iota((past, span), 0)
    for side, parity in enumerate((core, other)):
        key_at = slot + (slot // span + parity) * span
        shut_past[side] = masked((slot < chip * span) & (key_at >= doc_own))

    @pl.when(chip == 2)
    def _():
        sums_from(1).wait_recv()
        linked = jnp.where(doc_last < chunk, 1.0, 0.0)
        for i in range(tree, group):
            state_from(0, i).wait_recv()
            factor = jnp.exp(sums_got[1, i : i + 1, 0:1] + sums[i : i + 1, 0:1]) * linked
            state[i] = (state_f[i] + factor * got[0, i].astype(f32)).astype(bf16)
            state_to(i, 3).start()

    @pl.when(chip == 1)
    def _():
        linked = jnp.where(doc_last < first_f, 1.0, 0.0)
        for i in range(tree):
            state_from(0, i).wait_recv()
            factor = jnp.exp(sums[i : i + 1, 0:1]) * linked
            state[i] = (state_f[i] + factor * got[0, i].astype(f32)).astype(bf16)
            for target in (3, 2):
                state_to(i, target).start()

    def read(i, source, gap):
        known = doc_col < ((source + 1) * chunk)
        scale = columns[:, group + i : group + i + 1] * jnp.exp(gap)
        carried = jnp.dot(
            lin_all[0, :, i * DH : (i + 1) * DH], got[source, i], preferred_element_type=f32
        )
        inner[i] += jnp.where(known, scale, 0.0) * carried

    none = jnp.zeros((1, 1), f32)

    @pl.when(chip == 3)
    def _():
        sums_from(1).wait_recv()
        sums_from(2).wait_recv()

    def read_half(half):
        members = range(half * side_heads, (half + 1) * side_heads)
        for i in members:
            line = slice(i, i + 1)

            @pl.when(chip == 1)
            def _():
                if i >= tree:
                    state_from(0, i).wait_recv()
                read(i, 0, none)

            @pl.when(chip == 2)
            def _():
                if i >= tree:
                    read(i, 0, sums_got[1, line, 0:1])
                state_from(1, i).wait_recv()
                read(i, 1, none)

            @pl.when(chip == 3)
            def _():
                state_from(2, i).wait_recv()
                read(i, 2, none)
                state_from(1, i).wait_recv()
                read(i, 1, sums_got[2, line, 0:1])

        @pl.when(chip > 0)
        def _():
            for i in members:
                finish(i)
            back[half].start()
            own_out[half].start()

    def attend(keys, values, shut, going):
        score = lax.dot_general(keys, q_all[...], NT, preferred_element_type=f32)
        score = score * DH ** (-0.5) + jnp.concatenate([shut] * (heads // 2), axis=1)
        top = jnp.max(score, axis=0, keepdims=True)
        if going:
            top = jnp.maximum(top, top_v[...])
        weight = jnp.exp(score - top)
        total = jnp.sum(weight, axis=0, keepdims=True)
        out = lax.dot_general(values, weight.astype(bf16), TN, preferred_element_type=f32)
        if going:
            shrink = jnp.exp(top_v[...] - top)
            total += total_v[...] * shrink
            out += out_v[...] * shrink
        top_v[...], total_v[...], out_v[...] = top, total, out

    for load in loads[7:9]:
        load.wait()
    for peer in head_peers:
        for which in range(2):
            there = kv.at[core, which, own_rows(chip * m + peer, rows), :]
            remote(
                there, there, kv1_s.at[which, 0], kv1_r.at[which, peer], {"head": peer}
            ).wait_recv()
    for target in (3, 2, 1):
        pl.when(chip < target)(kv_to(target).start)
    pl.when(core == 0)(kv_pass(chip).start)

    loads[9].wait()
    for peer in head_peers:
        there = qs.at[own_rows(peer, rows), :]
        remote(there, there, qs_s.at[0], qs_r.at[peer], {"head": peer}).wait_recv()
    for g in range(heads):
        q_all[g * span : (g + 1) * span, :] = qs[:, g * DH : (g + 1) * DH]
    pl.when(core == 1)(kv_from(0, chip).wait_recv)
    own_keys, own_values = (
        jnp.concatenate([kv[p, which, own_rows(chip, span), :] for p in range(2)], axis=0)
        for which in range(2)
    )
    attend(own_keys, own_values, shut_own[...], False)
    read_half(1)
    for place in range(chips - 1):

        @pl.when(place < chip)
        def _():
            kv_from(core, place).wait_recv()
            kv_pass(place).start()

    read_half(0)

    @pl.when(chip > 0)
    def _():
        attend(kv[core, 0, :past, :], kv[core, 1, :past, :], shut_past[0], True)
        for place in range(chips - 1):
            pl.when(place < chip)(kv_from(other, place).wait_recv)
        attend(kv[other, 0, :past, :], kv[other, 1, :past, :], shut_past[1], True)

    result = out_v[...] * (1.0 / total_v[...])
    lse = top_v[...] + jnp.log(total_v[...])
    for i in range(heads // 2):
        both_heads = jnp.transpose(result[:, i * DH : (i + 1) * DH]).astype(bf16)
        for b in range(2):
            g = 2 * i + b
            soft_v[:, g * DH : (g + 1) * DH] = both_heads[b * span : (b + 1) * span]
            lse_v[g : g + 1, :] = lse[:, g * span : (g + 1) * span]
    stores = [
        pltpu.make_async_copy(soft_v, soft_out, loc_sem.at[12]),
        pltpu.make_async_copy(lse_v, lse_out, loc_sem.at[13]),
    ]
    for store in stores:
        store.start()

    for copy in pair + kv1 + qsc:
        copy.wait_send()
    for target in (3, 2, 1):
        pl.when(chip < target)(kv_to(target).wait_send)
    pl.when(core == 0)(kv_pass(chip).wait_send)
    for place in range(chips - 1):
        pl.when(place < chip)(kv_pass(place).wait_send)

    @pl.when(chip == 0)
    def _():
        for i in range(group):
            for target in (2, 1) if i >= tree else (1,):
                state_to(i, target).wait_send()

    @pl.when(chip == 1)
    def _():
        for target in (3, 2):
            sums_to(target).wait_send()
            for i in range(group):
                state_to(i, target).wait_send()

    @pl.when(chip == 2)
    def _():
        sums_to(3).wait_send()
        for i in range(group):
            state_to(i, 3).wait_send()

    for copy in own_out + stores:
        copy.wait()
    for half in (1, 0):
        back[half].wait_send()
        there = lin_out.at[:, cols(other * 2 + half, side_heads * DH)]
        remote(there, there, out_s.at[half], out_r.at[half], sibling).wait_recv()


def fused(n, m, query_lin, key_lin, value_lin, log_decay, query_soft, key_soft, value_soft, doc_start):
    span, heads = query_lin.shape[0], log_decay.shape[0]
    rows = query_soft.shape[0]
    chips, chunk, group = n // 2, 2 * span, heads // 2
    bf16, f32 = jnp.bfloat16, jnp.float32
    any_spec = pl.BlockSpec(memory_space=pl.ANY)
    hbm_spec = pl.BlockSpec(memory_space=pltpu.HBM)
    dma = pltpu.SemaphoreType.DMA
    regular = pltpu.SemaphoreType.REGULAR
    results = pl.pallas_call(
        functools.partial(fused_kernel, n, m),
        out_shape=(
            jax.ShapeDtypeStruct((span, heads * DH), bf16),
            jax.ShapeDtypeStruct((span, heads * DH), bf16),
            jax.ShapeDtypeStruct((heads, span), f32),
        ),
        in_specs=[any_spec] * 8,
        out_specs=(any_spec,) * 3,
        scratch_shapes=[
            pltpu.VMEM((3, chunk, group * DH), bf16),
            pltpu.VMEM((2, span, group * DH), bf16),
            pltpu.VMEM((2, heads, span), f32),
            pltpu.VMEM((2, 1, span), jnp.int32),
            pltpu.VMEM((2, group, DH, DH), f32),
            pltpu.VMEM((group, DH, DH), f32),
            pltpu.VMEM((group, DH, DH), f32),
            pltpu.VMEM((group, DH, DH), bf16),
            pltpu.VMEM((chips - 1, group, DH, DH), bf16),
            pltpu.VMEM((8, DH), f32),
            pltpu.VMEM((chips - 1, 8, DH), f32),
            pltpu.VMEM((group, chunk, DH), f32),
            pltpu.VMEM((chunk, group * DH), bf16),
            pltpu.VMEM((span, heads * DH), bf16),
            pltpu.VMEM((heads * span, DH), bf16),
            pltpu.VMEM((2, 2, chips * span, DH), bf16),
            pltpu.VMEM((span, heads * DH), bf16),
            pltpu.VMEM((heads, span), f32),
            pltpu.VMEM((chunk, 2 * span), f32),
            pltpu.VMEM((2, (chips - 1) * span, 2 * span), f32),
            pltpu.VMEM((1, heads * span), f32),
            pltpu.VMEM((1, heads * span), f32),
            pltpu.VMEM((DH, heads * span), f32),
            dma((14,)),
            dma((7,)), dma((7,)),
            dma((2, m - 1)), dma((2, m)), dma((m - 1,)), dma((m,)),
            dma((chips,)), dma((2, chips)), dma((chips,)),
            dma((chips, group)), dma((chips - 1, group)), dma((chips,)), dma((chips - 1,)),
            dma((2,)), dma((2,)), regular, regular, regular,
        ],
        compiler_params=pltpu.CompilerParams(
            collective_id=0, has_side_effects=True, vmem_limit_bytes=32 * 1024 * 1024
        ),
    )(*(pltpu.with_memory_space_constraint(x, pltpu.HBM) for x in (
        query_lin, key_lin, value_lin, log_decay, query_soft, key_soft, value_soft,
        doc_start.reshape(1, span),
    )))
    return pl.pallas_call(
        store_kernel,
        out_shape=tuple(jax.ShapeDtypeStruct(part.shape, part.dtype) for part in results),
        in_specs=[any_spec] * 3,
        out_specs=(hbm_spec,) * 3,
        scratch_shapes=[dma((3,))],
    )(*(pltpu.with_memory_space_constraint(part, pltpu.VMEM) for part in results))


def store_kernel(a, b, c, a_out, b_out, c_out, sem):
    copies = [
        pltpu.make_async_copy(src, dst, sem.at[i])
        for i, (src, dst) in enumerate(((a, a_out), (b, b_out), (c, c_out)))
    ]
    for copy in copies:
        copy.start()
    for copy in copies:
        copy.wait()


def per_device(
    query_lin, key_lin, value_lin, log_decay, query_soft, key_soft, value_soft, doc_start
):
    n, m = lax.axis_size("seq"), lax.axis_size("head")
    span, heads = query_lin.shape[0], log_decay.shape[0]
    if heads == n == 8 and m == 4 and span == DH // 2 and key_soft.shape[1] == m * DH:
        return fused(
            n, m, query_lin, key_lin, value_lin, log_decay,
            query_soft, key_soft, value_soft, doc_start,
        )
    lin_out = lightning_part(query_lin, key_lin, value_lin, log_decay, doc_start)
    soft_out, soft_lse = softmax_part(query_soft, key_soft, value_soft, doc_start)
    return (lin_out, soft_out, soft_lse)


def solution(mesh):
    return jax.shard_map(
        per_device,
        mesh=mesh,
        in_specs=(
            P("seq", "head"),
            P("seq", "head"),
            P("seq", "head"),
            P("head", "seq"),
            P(("seq", "head"), None),
            P(("seq", "head"), None),
            P(("seq", "head"), None),
            P("seq"),
        ),
        out_specs=(P("seq", "head"), P("seq", "head"), P("head", "seq")),
        check_vma=False,
    )
```

```python
import functools

import jax
import jax.numpy as jnp
from jax import lax
from jax.experimental import pallas as pl
from jax.experimental.pallas import tpu as pltpu
from jax.sharding import PartitionSpec as P


DH = 128


HIGHEST = lax.Precision.HIGHEST
masked_score = -1e30


def prefix(array, axis, combine, identity):
    size, here = (lax.axis_size(axis), lax.axis_index(axis))
    everything = jax.tree.map(lambda part: lax.all_gather(part, axis), array)
    start = jax.tree.map(
        lambda part, zero: jnp.broadcast_to(jnp.asarray(zero, part.dtype), part.shape),
        array,
        identity,
    )

    def lap(k, before):
        reached = k < here
        new = combine(before, jax.tree.map(lambda part: part[k], everything))
        return jax.tree.map(lambda a, b: jnp.where(reached, a, b), new, before)

    return lax.fori_loop(0, size, lap, start)


def span_terms(query_heads, key_heads, value_heads, decay_rows, doc_rows, first_place):
    span_len = query_heads.shape[0]
    places = jnp.arange(span_len, dtype=jnp.int32)
    not_later = places[None, :] <= places[:, None]
    cumulative = jnp.sum(jnp.where(not_later[None], decay_rows[:, None, :], 0.0), axis=2)
    totals = cumulative[:, -1]
    token_positions = first_place + jnp.arange(span_len, dtype=jnp.int32)
    allowed = (token_positions[None, :] <= token_positions[:, None]) & (
        doc_rows[:, None] <= token_positions[None, :]
    )
    decay_gap = jnp.where(allowed[None], cumulative[:, :, None] - cumulative[:, None, :], 0.0)
    decay_mat = jnp.where(allowed[None], jnp.exp(decay_gap), 0.0)
    scores = jnp.einsum("thd,shd->hts", query_heads, key_heads, preferred_element_type=jnp.float32)
    key_float = key_heads.astype(jnp.float32)
    value_float = value_heads.astype(jnp.float32)
    inner_part = jnp.einsum("hts,shd->thd", scores * decay_mat, value_float, precision=HIGHEST)
    keep_mask = (doc_rows == doc_rows[-1]).astype(jnp.float32)
    tail_weight = jnp.exp(totals[:, None] - cumulative) * keep_mask[None, :]
    weighted_keys = key_float * jnp.transpose(tail_weight)[:, :, None]
    fresh_state = jnp.einsum("shd,she->hde", weighted_keys, value_float, precision=HIGHEST)
    carry_on = (doc_rows[-1] < first_place).astype(jnp.float32)
    factor = jnp.exp(totals) * carry_on
    read_mask = (doc_rows < first_place).astype(jnp.float32)[:, None] * jnp.transpose(
        jnp.exp(cumulative)
    )
    return (inner_part, fresh_state, factor, read_mask)


def combine_states(earlier, later_part):
    return (earlier[0] * later_part[0], later_part[0][:, None, None] * earlier[1] + later_part[1])


def lightning_part(query_lin, key_lin, value_lin, log_decay, doc_start):
    span_len = query_lin.shape[0]
    head_count = log_decay.shape[0]
    first_place = lax.axis_index("seq") * span_len
    query_heads = query_lin.reshape(span_len, head_count, DH)
    key_heads = key_lin.reshape(span_len, head_count, DH)
    value_heads = value_lin.reshape(span_len, head_count, DH)
    inner_part, fresh_state, factor, read_mask = span_terms(
        query_heads, key_heads, value_heads, log_decay, doc_start, first_place
    )
    identity = (jnp.ones((head_count,), jnp.float32), jnp.zeros((head_count, DH, DH), jnp.float32))
    unused, carried = prefix((factor, fresh_state), "seq", combine_states, identity)
    outer_part = (
        jnp.einsum("thd,hde->the", query_heads.astype(jnp.float32), carried, precision=HIGHEST)
        * read_mask[:, :, None]
    )
    mixed_out = inner_part + outer_part
    normed = mixed_out * lax.rsqrt(jnp.mean(mixed_out * mixed_out, axis=-1, keepdims=True) + 1e-06)
    return normed.astype(jnp.bfloat16).reshape(span_len, head_count * DH)


def softmax_part(query_soft, key_soft, value_soft, doc_start):
    queries, keys_local, values_local = (
        lax.all_to_all(query_soft, "head", split_axis=1, concat_axis=0, tiled=True),
        lax.all_to_all(key_soft, "head", split_axis=1, concat_axis=0, tiled=True),
        lax.all_to_all(value_soft, "head", split_axis=1, concat_axis=0, tiled=True),
    )
    span_len = queries.shape[0]
    kv_count = keys_local.shape[1] // DH
    group_size = queries.shape[1] // keys_local.shape[1]
    first_place = lax.axis_index("seq") * span_len
    query_places = first_place + jnp.arange(span_len, dtype=jnp.int32)
    query_heads = queries.reshape(span_len, kv_count, group_size, DH)
    score_scale = DH ** (-0.5)
    start_state = (
        jnp.full((span_len, kv_count, group_size), masked_score, jnp.float32),
        jnp.zeros((span_len, kv_count, group_size), jnp.float32),
        jnp.zeros((span_len, kv_count, group_size, DH), jnp.float32),
    )
    key_piece = lax.all_gather(keys_local, "seq", axis=0, tiled=True)
    value_piece = lax.all_gather(values_local, "seq", axis=0, tiled=True)
    piece_rows = key_piece.shape[0]
    block_rows = max(
        (divisor for divisor in range(1, min(piece_rows, 1024) + 1) if piece_rows % divisor == 0)
    )
    block_count = piece_rows // block_rows
    key_parts = key_piece.reshape(block_count, block_rows, kv_count, DH)
    value_parts = value_piece.reshape(block_count, block_rows, kv_count, DH)
    begin_rows = jnp.int32(0) + block_rows * jnp.arange(block_count, dtype=jnp.int32)

    def absorb_block(running, slices):
        key_block, value_block, begin_row = slices
        running_max, norm_sum, accum_out = running
        token_positions = begin_row + jnp.arange(block_rows, dtype=jnp.int32)
        allowed = (token_positions[None, :] <= query_places[:, None]) & (
            doc_start[:, None] <= token_positions[None, :]
        )
        allowed = allowed[:, None, None, :]
        scores = (
            jnp.einsum("tkgd,skd->tkgs", query_heads, key_block, preferred_element_type=jnp.float32)
            * score_scale
        )
        new_max = jnp.maximum(
            running_max, jnp.max(jnp.where(allowed, scores, masked_score), axis=-1)
        )
        raw_weight = jnp.where(allowed, jnp.exp(scores - new_max[..., None]), 0.0)
        shrink = jnp.exp(running_max - new_max)
        norm_sum = norm_sum * shrink + jnp.sum(raw_weight, axis=-1)
        accum_out = accum_out * shrink[..., None] + jnp.einsum(
            "tkgs,skd->tkgd",
            raw_weight.astype(jnp.bfloat16),
            value_block,
            preferred_element_type=jnp.float32,
        )
        running = (new_max, norm_sum, accum_out)
        return (running, None)

    final_state, unused = lax.scan(absorb_block, start_state, (key_parts, value_parts, begin_rows))
    running_max, norm_sum, accum_out = final_state
    soft_out = (
        (accum_out / norm_sum[..., None])
        .astype(jnp.bfloat16)
        .reshape(span_len, kv_count * group_size * DH)
    )
    soft_lse = jnp.transpose(
        (running_max + jnp.log(norm_sum)).reshape(span_len, kv_count * group_size)
    )
    return (soft_out, soft_lse)


MESH = pl.DeviceIdType.MESH
NT = (((1,), (1,)), ((), ()))


TN = (((0,), (0,)), ((), ()))


def fused_kernel(
    n, m, q_in, k_in, v_in, ld_in, qs_in, ks_in, vs_in, doc_in,
    lin_out, soft_out, lse_out,
    lin_all, theirs_v, ld_v, doc_v, fresh, fresh_x, state_f, state, got, sums, sums_got,
    inner, lin_v, qs, q_all, kv, soft_v, lse_v, shut_own, shut_past, top_v, total_v, out_v,
    loc_sem, pair_s, pair_r, kv1_s, kv1_r, qs_s, qs_r, kv2_s, kvb_r, fwd_s,
    got_s, got_r, sums_s, sums_r, out_s, out_r, go_xy, go_z, far_in,
):
    span, heads = doc_in.shape[1], ld_in.shape[0]
    rows = qs_in.shape[0]
    chips, group, chunk = n // 2, heads // 2, 2 * span
    width = group * DH
    reach = chips * span
    bf16, f32 = jnp.bfloat16, jnp.float32
    me, hd = lax.axis_index("seq"), lax.axis_index("head")
    chip, core = me // 2, lax.rem(me, 2)
    other = 1 - core
    sibling = {"seq": 2 * chip + other}
    first = chip * chunk
    head_peers = [j + jnp.where(j >= hd, 1, 0) for j in range(m - 1)]

    def cols(index, size=DH):
        return pl.ds(pl.multiple_of(index * size, size), size)

    def own_rows(index, count):
        return pl.ds(pl.multiple_of(index * count, count), count)

    def greet(semaphore, device):
        pl.semaphore_signal(semaphore, inc=1, device_id=device, device_id_type=MESH)

    def remote(src, dst, send, recv, device):
        return pltpu.make_async_remote_copy(
            src_ref=src, dst_ref=dst, send_sem=send, recv_sem=recv,
            device_id=device, device_id_type=MESH,
        )

    barrier = pltpu.get_barrier_semaphore()
    for peer in head_peers:
        greet(barrier, {"seq": 2 * chip + 1, "head": peer})
    early = hd < m - 1
    late = jnp.logical_not(early)

    @pl.when((core == 1) & early)
    def _():
        greet(barrier, {"seq": me - 1})

    @pl.when((core == 0) & late)
    def _():
        greet(barrier, {"seq": me + 1})

    for source, targets in ((0, (1,)), (1, (0, 2, 3)), (2, (3,))):
        for target in targets:

            @pl.when(chip == target)
            def _():
                greet(barrier, {"seq": 2 * source})

    my_cols, their_cols = cols(core, width), cols(other, width)
    here = own_rows(core, span)
    kv_rows = own_rows(chip * m + hd, rows)
    loads = [
        pltpu.make_async_copy(ld_in, ld_v.at[core], loc_sem.at[0]),
        pltpu.make_async_copy(doc_in, doc_v.at[core], loc_sem.at[1]),
        pltpu.make_async_copy(k_in.at[:, their_cols], theirs_v.at[0], loc_sem.at[2]),
        pltpu.make_async_copy(v_in.at[:, their_cols], theirs_v.at[1], loc_sem.at[3]),
        pltpu.make_async_copy(k_in.at[:, my_cols], lin_all.at[1, here, :], loc_sem.at[4]),
        pltpu.make_async_copy(v_in.at[:, my_cols], lin_all.at[2, here, :], loc_sem.at[5]),
        pltpu.make_async_copy(q_in.at[:, my_cols], lin_all.at[0, here, :], loc_sem.at[6]),
        pltpu.make_async_copy(ks_in.at[:, cols(hd)], kv.at[core, 0, kv_rows, :], loc_sem.at[7]),
        pltpu.make_async_copy(vs_in.at[:, cols(hd)], kv.at[core, 1, kv_rows, :], loc_sem.at[8]),
        pltpu.make_async_copy(
            qs_in.at[:, cols(hd, heads * DH)], qs.at[own_rows(hd, rows), :], loc_sem.at[9]
        ),
    ]
    for load in loads:
        load.start()

    pair = [
        remote(fresh_x.at[0:2], fresh.at[core, 0:2], pair_s.at[0], pair_r.at[0], sibling),
        remote(fresh_x.at[2:4], fresh.at[core, 2:4], pair_s.at[1], pair_r.at[1], sibling),
        remote(ld_in, ld_v.at[core], pair_s.at[2], pair_r.at[2], sibling),
        remote(doc_in, doc_v.at[core], pair_s.at[3], pair_r.at[3], sibling),
        remote(theirs_v.at[0], lin_all.at[1, here, :], pair_s.at[4], pair_r.at[4], sibling),
        remote(theirs_v.at[1], lin_all.at[2, here, :], pair_s.at[5], pair_r.at[5], sibling),
        remote(q_in.at[:, their_cols], lin_all.at[0, here, :], pair_s.at[6], pair_r.at[6], sibling),
    ]
    kv1, qsc = [], []
    for j, peer in enumerate(head_peers):
        for which, src in enumerate((ks_in, vs_in)):
            kv1.append(
                remote(
                    src.at[:, cols(peer)], kv.at[core, which, kv_rows, :],
                    kv1_s.at[which, j], kv1_r.at[which, hd], {"head": peer},
                )
            )
        qsc.append(
            remote(
                qs_in.at[:, cols(peer, heads * DH)], qs.at[own_rows(hd, rows), :],
                qs_s.at[j], qs_r.at[hd], {"head": peer},
            )
        )

    def kv_block(parity, place):
        return kv.at[parity, :, own_rows(place, span), :]

    def kv_to(target):
        mine = kv_block(core, chip)
        return remote(
            mine, mine, kv2_s.at[target], kvb_r.at[core, chip], {"seq": 2 * target + 1}
        )

    def kv_own():
        mine = kv_block(0, chip)
        return remote(mine, mine, fwd_s.at[chip], kvb_r.at[0, chip], sibling)

    def kv_pass(place):
        both = kv.at[:, :, own_rows(place, span), :]
        return remote(both, both, fwd_s.at[place], kvb_r.at[0, place], sibling)

    def kv_from(parity, place):
        block = kv_block(parity, place)
        return remote(block, block, fwd_s.at[0], kvb_r.at[parity, place], sibling)

    def state_to(i, target):
        return remote(
            state.at[i], got.at[chip, i], got_s.at[target, i], got_r.at[chip, i],
            {"seq": 2 * target + core},
        )

    def state_on(i):
        held = got.at[1, i]
        return remote(held, held, got_s.at[2, i], got_r.at[1, i], {"seq": 4 + core})

    def state_from(source, i):
        there = got.at[source, i]
        return remote(there, there, got_s.at[0, i], got_r.at[source, i], sibling)

    def sums_to(target):
        return remote(
            sums, sums_got.at[chip], sums_s.at[target], sums_r.at[chip],
            {"seq": 2 * target + core},
        )

    def sums_from(source):
        there = sums_got.at[source]
        return remote(there, there, sums_s.at[0], sums_r.at[source], sibling)

    def send_over_z():
        for copy in kv1 + qsc:
            copy.start()

    n_z = 2 * (m - 1)
    n_xy = jnp.where(chip == 1, 6, 2)

    def told(semaphore):
        pl.semaphore_wait(semaphore, 1)

    @pl.when(late)
    def _():
        @pl.when(core == 1)
        def _():
            pl.semaphore_wait(barrier, n_z + 1)
            greet(go_z, sibling)

        @pl.when(core == 0)
        def _():
            told(go_z)

        send_over_z()
        for copy in pair[2:4]:
            copy.start()

    def iota(shape, dim):
        return lax.broadcasted_iota(jnp.int32, shape, dim)

    def running(values):
        size = values.shape[1]
        upper = jnp.where(iota((size, size), 0) <= iota((size, size), 1), 1.0, 0.0).astype(bf16)
        high = values.astype(bf16)
        rest = values - high.astype(f32)
        middle = rest.astype(bf16)
        low = (rest - middle.astype(f32)).astype(bf16)
        return sum(
            jnp.dot(term, upper, preferred_element_type=f32) for term in (low, middle, high)
        )

    def mine_of(values):
        return jnp.where(core == 0, values[:group], values[group:])

    def theirs_of(values):
        return jnp.where(core == 0, values[group:], values[:group])

    def key_value(keys, values, weight):
        values = values.astype(f32) * weight
        high = values.astype(bf16)
        low = (values - high.astype(f32)).astype(bf16)
        both = lax.dot_general(
            keys, jnp.concatenate([high, low], axis=1), TN, preferred_element_type=f32
        )
        return both[:, :DH] + both[:, DH:]

    for load in loads[:6]:
        load.wait()
    decay = ld_v[core]
    doc_own = doc_v[core]
    summed = running(decay)
    total = jnp.sum(decay, axis=1, keepdims=True)
    weight = jnp.where(doc_own == doc_own[:, span - 1 : span], jnp.exp(total - summed), 0.0)
    weight = jnp.transpose(jnp.concatenate([theirs_of(weight), mine_of(weight)], axis=0))
    for i in range(group):
        part = slice(i * DH, (i + 1) * DH)
        fresh_x[i] = key_value(theirs_v[0, :, part], theirs_v[1, :, part], weight[:, i : i + 1])

    @pl.when(early)
    def _():
        @pl.when(core == 0)
        def _():
            pl.semaphore_wait(barrier, jnp.where(chip == 3, 1, n_xy + 1))
            greet(go_xy, sibling)

        @pl.when(core == 1)
        def _():
            told(go_xy)

        for copy in pair[2:4]:
            copy.start()

    for copy in pair[:2] + pair[4:]:
        copy.start()
    for i in range(group):
        part = slice(i * DH, (i + 1) * DH)
        fresh[core, i] = key_value(
            lin_all[1, here, part], lin_all[2, here, part], weight[:, group + i : group + i + 1]
        )

    @pl.when(late)
    def _():
        @pl.when(core == 0)
        def _():
            @pl.when(chip < chips - 1)
            def _():
                pl.semaphore_wait(barrier, n_xy)

            greet(go_xy, sibling)

        @pl.when(core == 1)
        def _():
            told(go_xy)

    @pl.when((chip == 1) & (core == 0))
    def _():
        greet(far_in, {"seq": 0})
        greet(far_in, {"seq": 1})

    @pl.when(early & (hd > 0))
    def _():
        @pl.when(core == 1)
        def _():
            pl.semaphore_wait(barrier, n_z)
            greet(go_z, sibling)

        @pl.when(core == 0)
        def _():
            told(go_z)

        send_over_z()

    for copy in pair[:4]:
        copy.wait_recv()
    both_decays = jnp.concatenate([ld_v[0], ld_v[1]], axis=1)
    cum = mine_of(running(both_decays))
    second = mine_of(jnp.sum(both_decays[:, span:], axis=1, keepdims=True))
    doc_row = jnp.concatenate([doc_v[0], doc_v[1]], axis=1).astype(f32)
    doc_last = doc_row[:, chunk - 1 : chunk]
    first_f = first.astype(f32)
    sums[...] = jnp.concatenate(
        [jnp.broadcast_to(cum[:, chunk - 1 : chunk], (group, DH)), jnp.zeros((8 - group, DH), f32)],
        axis=0,
    )
    joined = jnp.where(doc_last < first_f + span, jnp.exp(second), 0.0)
    for i in range(group):
        merged = joined[i : i + 1] * fresh[0, i] + fresh[1, i]
        state_f[i] = merged
        state[i] = merged.astype(bf16)
    tree, side_heads = 2, group // 2

    @pl.when(chip == 0)
    def _():
        for i in range(tree):
            state_to(i, 1).start()
        told(far_in)
        for i in range(tree, group):
            state_to(i, 2).start()

    @pl.when(chip == 1)
    def _():
        for target in (3, 2):
            sums_to(target).start()
        for i in range(tree, group):
            state_to(i, 3).start()

    @pl.when(chip == 2)
    def _():
        sums_to(3).start()
        for i in range(tree):
            state_to(i, 3).start()

    @pl.when(hd == 0)
    def _():
        @pl.when(core == 1)
        def _():
            pl.semaphore_wait(barrier, n_z)
            greet(go_z, sibling)

        @pl.when(core == 0)
        def _():
            told(go_z)

        send_over_z()

    square = (chunk, chunk)
    at_row, at_col = iota(square, 0), iota(square, 1)
    eye, tri = at_row == at_col, at_row >= at_col
    doc_col = jnp.sum(jnp.where(eye, doc_row, 0.0), axis=1, keepdims=True)
    is_open = tri & (at_col + first >= doc_col.astype(jnp.int32))
    columns = jnp.transpose(jnp.concatenate([cum, jnp.exp(cum)], axis=0))
    loads[6].wait()
    for copy in pair[4:]:
        copy.wait_recv()
    for i in range(group):
        part = slice(i * DH, (i + 1) * DH)
        values = lin_all[2, :, part]
        score = lax.dot_general(
            lin_all[0, :, part], lin_all[1, :, part], NT, preferred_element_type=f32
        )
        mix = jnp.where(is_open, score * jnp.exp(columns[:, i : i + 1] - cum[i : i + 1]), 0.0)
        high = mix.astype(bf16)
        low = (mix - high.astype(f32)).astype(bf16)
        inner[i] = jnp.dot(
            jnp.concatenate([high, low], axis=1), jnp.concatenate([values, values], axis=0),
            preferred_element_type=f32,
        )

    @pl.when(chip == 0)
    def _():
        for i in range(tree, group):
            state_to(i, 1).start()

    back = [
        remote(
            lin_v.at[own_rows(other, span), pl.ds(half * side_heads * DH, side_heads * DH)],
            lin_out.at[:, cols(core * 2 + half, side_heads * DH)],
            out_s.at[half], out_r.at[half], sibling,
        )
        for half in range(2)
    ]
    own_out = [
        pltpu.make_async_copy(
            lin_v.at[here, pl.ds(half * side_heads * DH, side_heads * DH)],
            lin_out.at[:, cols(core * 2 + half, side_heads * DH)],
            loc_sem.at[10 + half],
        )
        for half in range(2)
    ]

    def finish(i):
        out = inner[i]
        normed = out * lax.rsqrt(jnp.mean(out * out, axis=1, keepdims=True) + 1e-06)
        lin_v[:, i * DH : (i + 1) * DH] = normed.astype(bf16)

    @pl.when(chip == 0)
    def _():
        for i in range(group):
            finish(i)
        for copy in back + own_out:
            copy.start()

    for place in range(chips):
        for parity in range(2):

            @pl.when(2 * place + parity > me)
            def _():
                kv[parity, :, place * span : (place + 1) * span, :] = jnp.zeros(
                    (2, span, DH), kv.dtype
                )

    def masked(is_on):
        half = jnp.where(is_on, 0.0, masked_score)
        return jnp.concatenate([half, half], axis=1)

    query_at = me * span + iota((chunk, span), 1)
    key_at = first + iota((chunk, span), 0)
    shut_own[...] = masked((key_at <= query_at) & (key_at >= doc_own))
    past = reach - span
    slot = iota((past, span), 0)
    for parity in range(2):
        key_at = slot + (slot // span + parity) * span
        shut_past[parity] = masked((slot < chip * span) & (key_at >= doc_own))

    @pl.when(chip == 3)
    def _():
        for i in range(tree, group):
            state_from(1, i).wait_recv()
            state_on(i).start()

    @pl.when(chip == 2)
    def _():
        sums_from(1).wait_recv()
        linked = jnp.where(doc_last < chunk, 1.0, 0.0)
        for i in range(tree, group):
            state_from(0, i).wait_recv()
            factor = jnp.exp(sums_got[1, i : i + 1, 0:1] + sums[i : i + 1, 0:1]) * linked
            state[i] = (state_f[i] + factor * got[0, i].astype(f32)).astype(bf16)
            state_to(i, 3).start()

    @pl.when(chip == 1)
    def _():
        linked = jnp.where(doc_last < first_f, 1.0, 0.0)
        for i in range(tree):
            state_from(0, i).wait_recv()
            factor = jnp.exp(sums[i : i + 1, 0:1]) * linked
            state[i] = (state_f[i] + factor * got[0, i].astype(f32)).astype(bf16)
            for target in (3, 2):
                state_to(i, target).start()

    def read(i, source, gap):
        known = doc_col < ((source + 1) * chunk)
        scale = columns[:, group + i : group + i + 1] * jnp.exp(gap)
        carried = jnp.dot(
            lin_all[0, :, i * DH : (i + 1) * DH], got[source, i], preferred_element_type=f32
        )
        inner[i] += jnp.where(known, scale, 0.0) * carried

    none = jnp.zeros((1, 1), f32)

    @pl.when(chip == 3)
    def _():
        sums_from(1).wait_recv()
        sums_from(2).wait_recv()

    def read_half(half):
        members = range(half * side_heads, (half + 1) * side_heads)
        for i in members:
            line = slice(i, i + 1)

            @pl.when(chip == 1)
            def _():
                if i >= tree:
                    state_from(0, i).wait_recv()
                read(i, 0, none)

            @pl.when(chip == 2)
            def _():
                if i >= tree:
                    read(i, 0, sums_got[1, line, 0:1])
                state_from(1, i).wait_recv()
                read(i, 1, none)

            @pl.when(chip == 3)
            def _():
                state_from(2, i).wait_recv()
                read(i, 2, none)
                if i < tree:
                    state_from(1, i).wait_recv()
                read(i, 1, sums_got[2, line, 0:1])

        @pl.when(chip > 0)
        def _():
            for i in members:
                finish(i)
            back[half].start()
            own_out[half].start()

    def attend(keys, values, shut, going):
        score = lax.dot_general(keys, q_all[...], NT, preferred_element_type=f32)
        score = score * DH ** (-0.5) + jnp.concatenate([shut] * (heads // 2), axis=1)
        top = jnp.max(score, axis=0, keepdims=True)
        if going:
            top = jnp.maximum(top, top_v[...])
        weight = jnp.exp(score - top)
        total = jnp.sum(weight, axis=0, keepdims=True)
        out = lax.dot_general(values, weight.astype(bf16), TN, preferred_element_type=f32)
        if going:
            shrink = jnp.exp(top_v[...] - top)
            total += total_v[...] * shrink
            out += out_v[...] * shrink
        top_v[...], total_v[...], out_v[...] = top, total, out

    for load in loads[7:9]:
        load.wait()
    for peer in head_peers:
        for which in range(2):
            there = kv.at[core, which, own_rows(chip * m + peer, rows), :]
            remote(
                there, there, kv1_s.at[which, 0], kv1_r.at[which, peer], {"head": peer}
            ).wait_recv()
    for target in (3, 2, 1):
        pl.when(chip < target)(kv_to(target).start)
    pl.when(core == 0)(kv_own().start)

    loads[9].wait()
    for peer in head_peers:
        there = qs.at[own_rows(peer, rows), :]
        remote(there, there, qs_s.at[0], qs_r.at[peer], {"head": peer}).wait_recv()
    for g in range(heads):
        q_all[g * span : (g + 1) * span, :] = qs[:, g * DH : (g + 1) * DH]
    pl.when(core == 1)(kv_from(0, chip).wait_recv)
    own_keys, own_values = (
        jnp.concatenate([kv[p, which, own_rows(chip, span), :] for p in range(2)], axis=0)
        for which in range(2)
    )
    attend(own_keys, own_values, shut_own[...], False)
    read_half(1)
    for place in range(chips - 1):

        @pl.when((place < chip) & (core == 1))
        def _():
            kv_from(0, place).wait_recv()
            kv_from(1, place).wait_recv()
            kv_pass(place).start()

    read_half(0)

    @pl.when(chip > 0)
    def _():
        for place in range(chips - 1):
            pl.when((place < chip) & (core == 0))(kv_pass(place).wait_recv)
        for parity in range(2):
            attend(kv[parity, 0, :past, :], kv[parity, 1, :past, :], shut_past[parity], True)

    result = out_v[...] * (1.0 / total_v[...])
    lse = top_v[...] + jnp.log(total_v[...])
    for i in range(heads // 2):
        both_heads = jnp.transpose(result[:, i * DH : (i + 1) * DH]).astype(bf16)
        for b in range(2):
            g = 2 * i + b
            soft_v[:, g * DH : (g + 1) * DH] = both_heads[b * span : (b + 1) * span]
            lse_v[g : g + 1, :] = lse[:, g * span : (g + 1) * span]
    stores = [
        pltpu.make_async_copy(soft_v, soft_out, loc_sem.at[12]),
        pltpu.make_async_copy(lse_v, lse_out, loc_sem.at[13]),
    ]
    for store in stores:
        store.start()

    for copy in pair + kv1 + qsc:
        copy.wait_send()
    for target in (3, 2, 1):
        pl.when(chip < target)(kv_to(target).wait_send)
    pl.when(core == 0)(kv_own().wait_send)
    for place in range(chips - 1):
        pl.when((place < chip) & (core == 1))(kv_pass(place).wait_send)

    @pl.when(chip == 0)
    def _():
        for i in range(group):
            for target in (2, 1) if i >= tree else (1,):
                state_to(i, target).wait_send()

    @pl.when(chip == 1)
    def _():
        for target in (3, 2):
            sums_to(target).wait_send()
            for i in range(group if target == 3 else tree):
                state_to(i, target).wait_send()

    @pl.when(chip == 3)
    def _():
        for i in range(tree, group):
            state_on(i).wait_send()

    @pl.when(chip == 2)
    def _():
        sums_to(3).wait_send()
        for i in range(group):
            state_to(i, 3).wait_send()

    for copy in own_out + stores:
        copy.wait()
    for half in (1, 0):
        back[half].wait_send()
        there = lin_out.at[:, cols(other * 2 + half, side_heads * DH)]
        remote(there, there, out_s.at[half], out_r.at[half], sibling).wait_recv()


def fused(n, m, query_lin, key_lin, value_lin, log_decay, query_soft, key_soft, value_soft, doc_start):
    span, heads = query_lin.shape[0], log_decay.shape[0]
    rows = query_soft.shape[0]
    chips, chunk, group = n // 2, 2 * span, heads // 2
    bf16, f32 = jnp.bfloat16, jnp.float32
    any_spec = pl.BlockSpec(memory_space=pl.ANY)
    hbm_spec = pl.BlockSpec(memory_space=pltpu.HBM)
    dma = pltpu.SemaphoreType.DMA
    regular = pltpu.SemaphoreType.REGULAR
    results = pl.pallas_call(
        functools.partial(fused_kernel, n, m),
        out_shape=(
            jax.ShapeDtypeStruct((span, heads * DH), bf16),
            jax.ShapeDtypeStruct((span, heads * DH), bf16),
            jax.ShapeDtypeStruct((heads, span), f32),
        ),
        in_specs=[any_spec] * 8,
        out_specs=(any_spec,) * 3,
        scratch_shapes=[
            pltpu.VMEM((3, chunk, group * DH), bf16),
            pltpu.VMEM((2, span, group * DH), bf16),
            pltpu.VMEM((2, heads, span), f32),
            pltpu.VMEM((2, 1, span), jnp.int32),
            pltpu.VMEM((2, group, DH, DH), f32),
            pltpu.VMEM((group, DH, DH), f32),
            pltpu.VMEM((group, DH, DH), f32),
            pltpu.VMEM((group, DH, DH), bf16),
            pltpu.VMEM((chips - 1, group, DH, DH), bf16),
            pltpu.VMEM((8, DH), f32),
            pltpu.VMEM((chips - 1, 8, DH), f32),
            pltpu.VMEM((group, chunk, DH), f32),
            pltpu.VMEM((chunk, group * DH), bf16),
            pltpu.VMEM((span, heads * DH), bf16),
            pltpu.VMEM((heads * span, DH), bf16),
            pltpu.VMEM((2, 2, chips * span, DH), bf16),
            pltpu.VMEM((span, heads * DH), bf16),
            pltpu.VMEM((heads, span), f32),
            pltpu.VMEM((chunk, 2 * span), f32),
            pltpu.VMEM((2, (chips - 1) * span, 2 * span), f32),
            pltpu.VMEM((1, heads * span), f32),
            pltpu.VMEM((1, heads * span), f32),
            pltpu.VMEM((DH, heads * span), f32),
            dma((14,)),
            dma((7,)), dma((7,)),
            dma((2, m - 1)), dma((2, m)), dma((m - 1,)), dma((m,)),
            dma((chips,)), dma((2, chips)), dma((chips,)),
            dma((chips, group)), dma((chips - 1, group)), dma((chips,)), dma((chips - 1,)),
            dma((2,)), dma((2,)), regular, regular, regular,
        ],
        compiler_params=pltpu.CompilerParams(
            collective_id=0, has_side_effects=True, vmem_limit_bytes=32 * 1024 * 1024
        ),
    )(*(pltpu.with_memory_space_constraint(x, pltpu.HBM) for x in (
        query_lin, key_lin, value_lin, log_decay, query_soft, key_soft, value_soft,
        doc_start.reshape(1, span),
    )))
    return pl.pallas_call(
        store_kernel,
        out_shape=tuple(jax.ShapeDtypeStruct(part.shape, part.dtype) for part in results),
        in_specs=[any_spec] * 3,
        out_specs=(hbm_spec,) * 3,
        scratch_shapes=[dma((3,))],
    )(*(pltpu.with_memory_space_constraint(part, pltpu.VMEM) for part in results))


def store_kernel(a, b, c, a_out, b_out, c_out, sem):
    copies = [
        pltpu.make_async_copy(src, dst, sem.at[i])
        for i, (src, dst) in enumerate(((a, a_out), (b, b_out), (c, c_out)))
    ]
    for copy in copies:
        copy.start()
    for copy in copies:
        copy.wait()


def per_device(
    query_lin, key_lin, value_lin, log_decay, query_soft, key_soft, value_soft, doc_start
):
    n, m = lax.axis_size("seq"), lax.axis_size("head")
    span, heads = query_lin.shape[0], log_decay.shape[0]
    if heads == n == 8 and m == 4 and span == DH // 2 and key_soft.shape[1] == m * DH:
        return fused(
            n, m, query_lin, key_lin, value_lin, log_decay,
            query_soft, key_soft, value_soft, doc_start,
        )
    lin_out = lightning_part(query_lin, key_lin, value_lin, log_decay, doc_start)
    soft_out, soft_lse = softmax_part(query_soft, key_soft, value_soft, doc_start)
    return (lin_out, soft_out, soft_lse)


def solution(mesh):
    return jax.shard_map(
        per_device,
        mesh=mesh,
        in_specs=(
            P("seq", "head"),
            P("seq", "head"),
            P("seq", "head"),
            P("head", "seq"),
            P(("seq", "head"), None),
            P(("seq", "head"), None),
            P(("seq", "head"), None),
            P("seq"),
        ),
        out_specs=(P("seq", "head"), P("seq", "head"), P("head", "seq")),
        check_vma=False,
    )
```

```python
import functools

import jax
import jax.numpy as jnp
from jax import lax
from jax.experimental import pallas as pl
from jax.experimental.pallas import tpu as pltpu
from jax.sharding import PartitionSpec as P


DH = 128


HIGHEST = lax.Precision.HIGHEST
masked_score = -1e30


def prefix(array, axis, combine, identity):
    size, here = (lax.axis_size(axis), lax.axis_index(axis))
    everything = jax.tree.map(lambda part: lax.all_gather(part, axis), array)
    start = jax.tree.map(
        lambda part, zero: jnp.broadcast_to(jnp.asarray(zero, part.dtype), part.shape),
        array,
        identity,
    )

    def lap(k, before):
        reached = k < here
        new = combine(before, jax.tree.map(lambda part: part[k], everything))
        return jax.tree.map(lambda a, b: jnp.where(reached, a, b), new, before)

    return lax.fori_loop(0, size, lap, start)


def span_terms(query_heads, key_heads, value_heads, decay_rows, doc_rows, first_place):
    span_len = query_heads.shape[0]
    places = jnp.arange(span_len, dtype=jnp.int32)
    not_later = places[None, :] <= places[:, None]
    cumulative = jnp.sum(jnp.where(not_later[None], decay_rows[:, None, :], 0.0), axis=2)
    totals = cumulative[:, -1]
    token_positions = first_place + jnp.arange(span_len, dtype=jnp.int32)
    allowed = (token_positions[None, :] <= token_positions[:, None]) & (
        doc_rows[:, None] <= token_positions[None, :]
    )
    decay_gap = jnp.where(allowed[None], cumulative[:, :, None] - cumulative[:, None, :], 0.0)
    decay_mat = jnp.where(allowed[None], jnp.exp(decay_gap), 0.0)
    scores = jnp.einsum("thd,shd->hts", query_heads, key_heads, preferred_element_type=jnp.float32)
    key_float = key_heads.astype(jnp.float32)
    value_float = value_heads.astype(jnp.float32)
    inner_part = jnp.einsum("hts,shd->thd", scores * decay_mat, value_float, precision=HIGHEST)
    keep_mask = (doc_rows == doc_rows[-1]).astype(jnp.float32)
    tail_weight = jnp.exp(totals[:, None] - cumulative) * keep_mask[None, :]
    weighted_keys = key_float * jnp.transpose(tail_weight)[:, :, None]
    fresh_state = jnp.einsum("shd,she->hde", weighted_keys, value_float, precision=HIGHEST)
    carry_on = (doc_rows[-1] < first_place).astype(jnp.float32)
    factor = jnp.exp(totals) * carry_on
    read_mask = (doc_rows < first_place).astype(jnp.float32)[:, None] * jnp.transpose(
        jnp.exp(cumulative)
    )
    return (inner_part, fresh_state, factor, read_mask)


def combine_states(earlier, later_part):
    return (earlier[0] * later_part[0], later_part[0][:, None, None] * earlier[1] + later_part[1])


def lightning_part(query_lin, key_lin, value_lin, log_decay, doc_start):
    span_len = query_lin.shape[0]
    head_count = log_decay.shape[0]
    first_place = lax.axis_index("seq") * span_len
    query_heads = query_lin.reshape(span_len, head_count, DH)
    key_heads = key_lin.reshape(span_len, head_count, DH)
    value_heads = value_lin.reshape(span_len, head_count, DH)
    inner_part, fresh_state, factor, read_mask = span_terms(
        query_heads, key_heads, value_heads, log_decay, doc_start, first_place
    )
    identity = (jnp.ones((head_count,), jnp.float32), jnp.zeros((head_count, DH, DH), jnp.float32))
    unused, carried = prefix((factor, fresh_state), "seq", combine_states, identity)
    outer_part = (
        jnp.einsum("thd,hde->the", query_heads.astype(jnp.float32), carried, precision=HIGHEST)
        * read_mask[:, :, None]
    )
    mixed_out = inner_part + outer_part
    normed = mixed_out * lax.rsqrt(jnp.mean(mixed_out * mixed_out, axis=-1, keepdims=True) + 1e-06)
    return normed.astype(jnp.bfloat16).reshape(span_len, head_count * DH)


def softmax_part(query_soft, key_soft, value_soft, doc_start):
    queries, keys_local, values_local = (
        lax.all_to_all(query_soft, "head", split_axis=1, concat_axis=0, tiled=True),
        lax.all_to_all(key_soft, "head", split_axis=1, concat_axis=0, tiled=True),
        lax.all_to_all(value_soft, "head", split_axis=1, concat_axis=0, tiled=True),
    )
    span_len = queries.shape[0]
    kv_count = keys_local.shape[1] // DH
    group_size = queries.shape[1] // keys_local.shape[1]
    first_place = lax.axis_index("seq") * span_len
    query_places = first_place + jnp.arange(span_len, dtype=jnp.int32)
    query_heads = queries.reshape(span_len, kv_count, group_size, DH)
    score_scale = DH ** (-0.5)
    start_state = (
        jnp.full((span_len, kv_count, group_size), masked_score, jnp.float32),
        jnp.zeros((span_len, kv_count, group_size), jnp.float32),
        jnp.zeros((span_len, kv_count, group_size, DH), jnp.float32),
    )
    key_piece = lax.all_gather(keys_local, "seq", axis=0, tiled=True)
    value_piece = lax.all_gather(values_local, "seq", axis=0, tiled=True)
    piece_rows = key_piece.shape[0]
    block_rows = max(
        (divisor for divisor in range(1, min(piece_rows, 1024) + 1) if piece_rows % divisor == 0)
    )
    block_count = piece_rows // block_rows
    key_parts = key_piece.reshape(block_count, block_rows, kv_count, DH)
    value_parts = value_piece.reshape(block_count, block_rows, kv_count, DH)
    begin_rows = jnp.int32(0) + block_rows * jnp.arange(block_count, dtype=jnp.int32)

    def absorb_block(running, slices):
        key_block, value_block, begin_row = slices
        running_max, norm_sum, accum_out = running
        token_positions = begin_row + jnp.arange(block_rows, dtype=jnp.int32)
        allowed = (token_positions[None, :] <= query_places[:, None]) & (
            doc_start[:, None] <= token_positions[None, :]
        )
        allowed = allowed[:, None, None, :]
        scores = (
            jnp.einsum("tkgd,skd->tkgs", query_heads, key_block, preferred_element_type=jnp.float32)
            * score_scale
        )
        new_max = jnp.maximum(
            running_max, jnp.max(jnp.where(allowed, scores, masked_score), axis=-1)
        )
        raw_weight = jnp.where(allowed, jnp.exp(scores - new_max[..., None]), 0.0)
        shrink = jnp.exp(running_max - new_max)
        norm_sum = norm_sum * shrink + jnp.sum(raw_weight, axis=-1)
        accum_out = accum_out * shrink[..., None] + jnp.einsum(
            "tkgs,skd->tkgd",
            raw_weight.astype(jnp.bfloat16),
            value_block,
            preferred_element_type=jnp.float32,
        )
        running = (new_max, norm_sum, accum_out)
        return (running, None)

    final_state, unused = lax.scan(absorb_block, start_state, (key_parts, value_parts, begin_rows))
    running_max, norm_sum, accum_out = final_state
    soft_out = (
        (accum_out / norm_sum[..., None])
        .astype(jnp.bfloat16)
        .reshape(span_len, kv_count * group_size * DH)
    )
    soft_lse = jnp.transpose(
        (running_max + jnp.log(norm_sum)).reshape(span_len, kv_count * group_size)
    )
    return (soft_out, soft_lse)


MESH = pl.DeviceIdType.MESH
NT = (((1,), (1,)), ((), ()))


TN = (((0,), (0,)), ((), ()))


def fused_kernel(
    n, m, q_in, k_in, v_in, ld_in, qs_in, ks_in, vs_in, doc_in,
    lin_out, soft_out, lse_out,
    lin_all, theirs_v, ld_v, doc_v, fresh, fresh_x, state_f, state, state_x, got, sums, sums_got,
    inner, lin_v, qs, q_all, kv, shut_own, shut_past, top_v, total_v, out_v,
    loc_sem, pair_s, pair_r, kv1_s, kv1_r, qs_s, qs_r, kv2_s, kvb_r, fwd_s,
    got_s, got_r, sums_s, sums_r, out_s, out_r, go_xy, go_z, far_in,
):
    span, heads = doc_in.shape[1], ld_in.shape[0]
    rows = qs_in.shape[0]
    chips, group, chunk = n // 2, heads // 2, 2 * span
    width = group * DH
    reach = chips * span
    bf16, f32 = jnp.bfloat16, jnp.float32
    me, hd = lax.axis_index("seq"), lax.axis_index("head")
    chip, core = me // 2, lax.rem(me, 2)
    other = 1 - core
    sibling = {"seq": 2 * chip + other}
    first = chip * chunk
    head_peers = [j + jnp.where(j >= hd, 1, 0) for j in range(m - 1)]

    def cols(index, size=DH):
        return pl.ds(pl.multiple_of(index * size, size), size)

    def own_rows(index, count):
        return pl.ds(pl.multiple_of(index * count, count), count)

    def greet(semaphore, device):
        pl.semaphore_signal(semaphore, inc=1, device_id=device, device_id_type=MESH)

    def remote(src, dst, send, recv, device):
        return pltpu.make_async_remote_copy(
            src_ref=src, dst_ref=dst, send_sem=send, recv_sem=recv,
            device_id=device, device_id_type=MESH,
        )

    barrier = pltpu.get_barrier_semaphore()
    for peer in head_peers:
        greet(barrier, {"seq": 2 * chip + 1, "head": peer})
    early = hd < m - 1
    late = jnp.logical_not(early)

    @pl.when((core == 1) & early)
    def _():
        greet(barrier, {"seq": me - 1})

    @pl.when((core == 0) & late)
    def _():
        greet(barrier, {"seq": me + 1})

    for source, targets in ((0, (1,)), (1, (0, 2, 3)), (2, (3,))):
        for target in targets:

            @pl.when(chip == target)
            def _():
                greet(barrier, {"seq": 2 * source})

    my_cols, their_cols = cols(core, width), cols(other, width)
    here = own_rows(core, span)
    kv_rows = own_rows(chip * m + hd, rows)
    loads = [
        pltpu.make_async_copy(ld_in, ld_v.at[core], loc_sem.at[0]),
        pltpu.make_async_copy(doc_in, doc_v.at[core], loc_sem.at[1]),
        pltpu.make_async_copy(k_in.at[:, their_cols], theirs_v.at[0], loc_sem.at[2]),
        pltpu.make_async_copy(v_in.at[:, their_cols], theirs_v.at[1], loc_sem.at[3]),
        pltpu.make_async_copy(k_in.at[:, my_cols], lin_all.at[1, here, :], loc_sem.at[4]),
        pltpu.make_async_copy(v_in.at[:, my_cols], lin_all.at[2, here, :], loc_sem.at[5]),
        pltpu.make_async_copy(q_in.at[:, my_cols], lin_all.at[0, here, :], loc_sem.at[6]),
        pltpu.make_async_copy(ks_in.at[:, cols(hd)], kv.at[core, 0, kv_rows, :], loc_sem.at[7]),
        pltpu.make_async_copy(vs_in.at[:, cols(hd)], kv.at[core, 1, kv_rows, :], loc_sem.at[8]),
        pltpu.make_async_copy(
            qs_in.at[:, cols(hd, heads * DH)], qs.at[own_rows(hd, rows), :], loc_sem.at[9]
        ),
    ]
    for load in loads:
        load.start()

    pair = [
        remote(fresh_x.at[0:2], fresh.at[core, 0:2], pair_s.at[0], pair_r.at[0], sibling),
        remote(fresh_x.at[2:4], fresh.at[core, 2:4], pair_s.at[1], pair_r.at[1], sibling),
        remote(ld_in, ld_v.at[core], pair_s.at[2], pair_r.at[2], sibling),
        remote(doc_in, doc_v.at[core], pair_s.at[3], pair_r.at[3], sibling),
        remote(theirs_v.at[0], lin_all.at[1, here, :], pair_s.at[4], pair_r.at[4], sibling),
        remote(theirs_v.at[1], lin_all.at[2, here, :], pair_s.at[5], pair_r.at[5], sibling),
        remote(q_in.at[:, their_cols], lin_all.at[0, here, :], pair_s.at[6], pair_r.at[6], sibling),
    ]
    kv1, qsc = [], []
    for j, peer in enumerate(head_peers):
        for which, src in enumerate((ks_in, vs_in)):
            kv1.append(
                remote(
                    src.at[:, cols(peer)], kv.at[core, which, kv_rows, :],
                    kv1_s.at[which, j], kv1_r.at[which, hd], {"head": peer},
                )
            )
        qsc.append(
            remote(
                qs_in.at[:, cols(peer, heads * DH)], qs.at[own_rows(hd, rows), :],
                qs_s.at[j], qs_r.at[hd], {"head": peer},
            )
        )

    def kv_block(parity, place):
        return kv.at[parity, :, own_rows(place, span), :]

    def kv_to(target):
        mine = kv_block(core, chip)
        return remote(
            mine, mine, kv2_s.at[target], kvb_r.at[core, chip], {"seq": 2 * target + 1}
        )

    def kv_own():
        mine = kv_block(0, chip)
        return remote(mine, mine, fwd_s.at[chip], kvb_r.at[0, chip], sibling)

    def kv_pass(place):
        both = kv.at[:, :, own_rows(place, span), :]
        return remote(both, both, fwd_s.at[place], kvb_r.at[0, place], sibling)

    def kv_from(parity, place):
        block = kv_block(parity, place)
        return remote(block, block, fwd_s.at[0], kvb_r.at[parity, place], sibling)

    def state_to(i, target):
        return remote(
            state.at[i], got.at[chip, i], got_s.at[target, i], got_r.at[chip, i],
            {"seq": 2 * target + core},
        )

    def alone_to():
        return remote(
            state_x, got.at[1, 1], got_s.at[2, 1], got_r.at[1, 1], {"seq": 4 + core}
        )

    def state_on(i):
        held = got.at[1, i]
        return remote(held, held, got_s.at[2, i], got_r.at[1, i], {"seq": 4 + core})

    def state_from(source, i):
        there = got.at[source, i]
        return remote(there, there, got_s.at[0, i], got_r.at[source, i], sibling)

    def sums_to(target):
        return remote(
            sums, sums_got.at[chip], sums_s.at[target], sums_r.at[chip],
            {"seq": 2 * target + core},
        )

    def sums_from(source):
        there = sums_got.at[source]
        return remote(there, there, sums_s.at[0], sums_r.at[source], sibling)

    def send_over_z():
        for copy in kv1 + qsc:
            copy.start()

    n_z = 2 * (m - 1)
    n_xy = jnp.where(chip == 1, 6, 2)

    def told(semaphore):
        pl.semaphore_wait(semaphore, 1)

    @pl.when(late)
    def _():
        @pl.when(core == 1)
        def _():
            pl.semaphore_wait(barrier, n_z + 1)
            greet(go_z, sibling)

        @pl.when(core == 0)
        def _():
            told(go_z)

        send_over_z()
        for copy in pair[2:4]:
            copy.start()

    def iota(shape, dim):
        return lax.broadcasted_iota(jnp.int32, shape, dim)

    def running(values):
        size = values.shape[1]
        upper = jnp.where(iota((size, size), 0) <= iota((size, size), 1), 1.0, 0.0).astype(bf16)
        high = values.astype(bf16)
        rest = values - high.astype(f32)
        middle = rest.astype(bf16)
        low = (rest - middle.astype(f32)).astype(bf16)
        return sum(
            jnp.dot(term, upper, preferred_element_type=f32) for term in (low, middle, high)
        )

    def mine_of(values):
        return jnp.where(core == 0, values[:group], values[group:])

    def theirs_of(values):
        return jnp.where(core == 0, values[group:], values[:group])

    def key_value(keys, values, weight):
        values = values.astype(f32) * weight
        high = values.astype(bf16)
        low = (values - high.astype(f32)).astype(bf16)
        both = lax.dot_general(
            keys, jnp.concatenate([high, low], axis=1), TN, preferred_element_type=f32
        )
        return both[:, :DH] + both[:, DH:]

    for load in loads[:6]:
        load.wait()
    decay = ld_v[core]
    doc_own = doc_v[core]
    summed = running(decay)
    total = jnp.sum(decay, axis=1, keepdims=True)
    weight = jnp.where(doc_own == doc_own[:, span - 1 : span], jnp.exp(total - summed), 0.0)
    weight = jnp.transpose(jnp.concatenate([theirs_of(weight), mine_of(weight)], axis=0))
    for i in range(group):
        part = slice(i * DH, (i + 1) * DH)
        fresh_x[i] = key_value(theirs_v[0, :, part], theirs_v[1, :, part], weight[:, i : i + 1])

    @pl.when(early)
    def _():
        @pl.when(core == 0)
        def _():
            pl.semaphore_wait(barrier, jnp.where(chip == 3, 1, n_xy + 1))
            greet(go_xy, sibling)

        @pl.when(core == 1)
        def _():
            told(go_xy)

        for copy in pair[2:4]:
            copy.start()

    for copy in pair[:2] + pair[4:]:
        copy.start()
    for i in range(group):
        part = slice(i * DH, (i + 1) * DH)
        fresh[core, i] = key_value(
            lin_all[1, here, part], lin_all[2, here, part], weight[:, group + i : group + i + 1]
        )

    @pl.when(late)
    def _():
        @pl.when(core == 0)
        def _():
            @pl.when(chip < chips - 1)
            def _():
                pl.semaphore_wait(barrier, n_xy)

            greet(go_xy, sibling)

        @pl.when(core == 1)
        def _():
            told(go_xy)

    @pl.when((chip == 1) & (core == 0))
    def _():
        greet(far_in, {"seq": 0})
        greet(far_in, {"seq": 1})

    @pl.when(early & (hd > 0))
    def _():
        @pl.when(core == 1)
        def _():
            pl.semaphore_wait(barrier, n_z)
            greet(go_z, sibling)

        @pl.when(core == 0)
        def _():
            told(go_z)

        send_over_z()

    for copy in pair[:4]:
        copy.wait_recv()
    both_decays = jnp.concatenate([ld_v[0], ld_v[1]], axis=1)
    cum = mine_of(running(both_decays))
    second = mine_of(jnp.sum(both_decays[:, span:], axis=1, keepdims=True))
    doc_row = jnp.concatenate([doc_v[0], doc_v[1]], axis=1).astype(f32)
    doc_last = doc_row[:, chunk - 1 : chunk]
    first_f = first.astype(f32)
    sums[...] = jnp.concatenate(
        [jnp.broadcast_to(cum[:, chunk - 1 : chunk], (group, DH)), jnp.zeros((8 - group, DH), f32)],
        axis=0,
    )
    joined = jnp.where(doc_last < first_f + span, jnp.exp(second), 0.0)
    for i in range(group):
        merged = joined[i : i + 1] * fresh[0, i] + fresh[1, i]
        state_f[i] = merged
        state[i] = merged.astype(bf16)
    tree, side_heads = 2, group // 2

    @pl.when(chip == 0)
    def _():
        for i in range(tree):
            state_to(i, 1).start()
        told(far_in)
        for i in range(tree, group):
            state_to(i, 2).start()

    @pl.when(chip == 1)
    def _():
        for target in (3, 2):
            sums_to(target).start()
        for i in range(tree, group):
            state_to(i, 3).start()
        state_x[...] = state[1]

    @pl.when(chip == 2)
    def _():
        sums_to(3).start()
        for i in range(tree):
            state_to(i, 3).start()

    @pl.when(hd == 0)
    def _():
        @pl.when(core == 1)
        def _():
            pl.semaphore_wait(barrier, n_z)
            greet(go_z, sibling)

        @pl.when(core == 0)
        def _():
            told(go_z)

        send_over_z()

    square = (chunk, chunk)
    at_row, at_col = iota(square, 0), iota(square, 1)
    eye, tri = at_row == at_col, at_row >= at_col
    doc_col = jnp.sum(jnp.where(eye, doc_row, 0.0), axis=1, keepdims=True)
    is_open = tri & (at_col + first >= doc_col.astype(jnp.int32))
    columns = jnp.transpose(jnp.concatenate([cum, jnp.exp(cum)], axis=0))
    loads[6].wait()
    for copy in pair[4:]:
        copy.wait_recv()
    for i in range(group):
        part = slice(i * DH, (i + 1) * DH)
        values = lin_all[2, :, part]
        score = lax.dot_general(
            lin_all[0, :, part], lin_all[1, :, part], NT, preferred_element_type=f32
        )
        mix = jnp.where(is_open, score * jnp.exp(columns[:, i : i + 1] - cum[i : i + 1]), 0.0)
        high = mix.astype(bf16)
        low = (mix - high.astype(f32)).astype(bf16)
        inner[i] = jnp.dot(
            jnp.concatenate([high, low], axis=1), jnp.concatenate([values, values], axis=0),
            preferred_element_type=f32,
        )

    @pl.when(chip == 0)
    def _():
        for i in range(1, tree):
            state_to(i, 2).start()
        for i in range(tree, group):
            state_to(i, 1).start()

    pl.when(chip == 1)(alone_to().start)

    back = [
        remote(
            lin_v.at[own_rows(other, span), pl.ds(half * side_heads * DH, side_heads * DH)],
            lin_out.at[:, cols(core * 2 + half, side_heads * DH)],
            out_s.at[half], out_r.at[half], sibling,
        )
        for half in range(2)
    ]
    own_out = [
        pltpu.make_async_copy(
            lin_v.at[here, pl.ds(half * side_heads * DH, side_heads * DH)],
            lin_out.at[:, cols(core * 2 + half, side_heads * DH)],
            loc_sem.at[10 + half],
        )
        for half in range(2)
    ]

    def finish(i):
        out = inner[i]
        normed = out * lax.rsqrt(jnp.mean(out * out, axis=1, keepdims=True) + 1e-06)
        lin_v[:, i * DH : (i + 1) * DH] = normed.astype(bf16)

    @pl.when(chip == 0)
    def _():
        for i in range(group):
            finish(i)
        for copy in back + own_out:
            copy.start()

    for place in range(chips):
        for parity in range(2):

            @pl.when(2 * place + parity > me)
            def _():
                kv[parity, :, place * span : (place + 1) * span, :] = jnp.zeros(
                    (2, span, DH), kv.dtype
                )

    def masked(is_on):
        half = jnp.where(is_on, 0.0, masked_score)
        return jnp.concatenate([half, half], axis=1)

    query_at = me * span + iota((chunk, span), 1)
    key_at = first + iota((chunk, span), 0)
    shut_own[...] = masked((key_at <= query_at) & (key_at >= doc_own))
    past = reach - span
    slot = iota((past, span), 0)
    for parity in range(2):
        key_at = slot + (slot // span + parity) * span
        shut_past[parity] = masked((slot < chip * span) & (key_at >= doc_own))

    @pl.when(chip == 3)
    def _():
        for i in range(tree, group):
            state_from(1, i).wait_recv()
            state_on(i).start()

    @pl.when(chip == 2)
    def _():
        sums_from(1).wait_recv()
        linked = jnp.where(doc_last < chunk, 1.0, 0.0)
        for i in range(tree, group):
            state_from(0, i).wait_recv()
            factor = jnp.exp(sums_got[1, i : i + 1, 0:1] + sums[i : i + 1, 0:1]) * linked
            state[i] = (state_f[i] + factor * got[0, i].astype(f32)).astype(bf16)
            state_to(i, 3).start()

    @pl.when(chip == 1)
    def _():
        linked = jnp.where(doc_last < first_f, 1.0, 0.0)
        for i in range(tree):
            state_from(0, i).wait_recv()
            factor = jnp.exp(sums[i : i + 1, 0:1]) * linked
            state[i] = (state_f[i] + factor * got[0, i].astype(f32)).astype(bf16)
            for target in (3, 2) if i == 0 else (3,):
                state_to(i, target).start()

    def read(i, source, gap):
        known = doc_col < ((source + 1) * chunk)
        scale = columns[:, group + i : group + i + 1] * jnp.exp(gap)
        carried = jnp.dot(
            lin_all[0, :, i * DH : (i + 1) * DH], got[source, i], preferred_element_type=f32
        )
        inner[i] += jnp.where(known, scale, 0.0) * carried

    none = jnp.zeros((1, 1), f32)

    @pl.when(chip == 3)
    def _():
        sums_from(1).wait_recv()
        sums_from(2).wait_recv()

    def read_half(half, last):
        members = range(half * side_heads, (half + 1) * side_heads)
        for i in members:
            line = slice(i, i + 1)

            if not last:

                @pl.when(chip == 1)
                def _():
                    if i >= tree:
                        state_from(0, i).wait_recv()
                    read(i, 0, none)

            if not last:

                @pl.when(chip == 2)
                def _():
                    if 0 < i < tree:
                        state_from(0, i).wait_recv()
                    if i:
                        read(i, 0, sums_got[1, line, 0:1])
                    state_from(1, i).wait_recv()
                    read(i, 1, none)

            if last:

                @pl.when(chip == 3)
                def _():
                    state_from(2, i).wait_recv()
                    read(i, 2, none)
                    if i < tree:
                        state_from(1, i).wait_recv()
                    read(i, 1, sums_got[2, line, 0:1])

        @pl.when(chip == 3 if last else (chip > 0) & (chip < 3))
        def _():
            for i in members:
                finish(i)
            back[half].start()
            own_out[half].start()

    def attend(keys, values, shut, going):
        score = lax.dot_general(keys, q_all[...], NT, preferred_element_type=f32)
        score = score * DH ** (-0.5) + jnp.concatenate([shut] * (heads // 2), axis=1)
        top = jnp.max(score, axis=0, keepdims=True)
        if going:
            top = jnp.maximum(top, top_v[...])
        weight = jnp.exp(score - top)
        total = jnp.sum(weight, axis=0, keepdims=True)
        out = lax.dot_general(values, weight.astype(bf16), TN, preferred_element_type=f32)
        if going:
            shrink = jnp.exp(top_v[...] - top)
            total += total_v[...] * shrink
            out += out_v[...] * shrink
        top_v[...], total_v[...], out_v[...] = top, total, out

    for load in loads[7:9]:
        load.wait()
    for peer in head_peers:
        for which in range(2):
            there = kv.at[core, which, own_rows(chip * m + peer, rows), :]
            remote(
                there, there, kv1_s.at[which, 0], kv1_r.at[which, peer], {"head": peer}
            ).wait_recv()
    for target in (3, 2, 1):
        pl.when(chip < target)(kv_to(target).start)
    pl.when(core == 0)(kv_own().start)

    loads[9].wait()
    for peer in head_peers:
        there = qs.at[own_rows(peer, rows), :]
        remote(there, there, qs_s.at[0], qs_r.at[peer], {"head": peer}).wait_recv()
    for g in range(heads):
        q_all[g * span : (g + 1) * span, :] = qs[:, g * DH : (g + 1) * DH]
    pl.when(core == 1)(kv_from(0, chip).wait_recv)
    own_keys, own_values = (
        jnp.concatenate([kv[p, which, own_rows(chip, span), :] for p in range(2)], axis=0)
        for which in range(2)
    )
    attend(own_keys, own_values, shut_own[...], False)
    read_half(1, False)
    read_half(0, True)
    for place in range(chips - 1):

        @pl.when((place < chip) & (core == 1))
        def _():
            kv_from(0, place).wait_recv()
            kv_from(1, place).wait_recv()
            kv_pass(place).start()

    read_half(0, False)
    read_half(1, True)

    @pl.when(chip > 0)
    def _():
        for place in range(chips - 1):
            pl.when((place < chip) & (core == 0))(kv_pass(place).wait_recv)
        for parity in range(2):
            attend(kv[parity, 0, :past, :], kv[parity, 1, :past, :], shut_past[parity], True)

    result = out_v[...] * (1.0 / total_v[...])
    lse = top_v[...] + jnp.log(total_v[...])
    for i in range(heads // 2):
        both_heads = jnp.transpose(result[:, i * DH : (i + 1) * DH].astype(bf16))
        for b in range(2):
            g = 2 * i + b
            soft_out[:, g * DH : (g + 1) * DH] = both_heads[b * span : (b + 1) * span]
            lse_out[g : g + 1, :] = lse[:, g * span : (g + 1) * span]

    for copy in pair + kv1 + qsc:
        copy.wait_send()
    for target in (3, 2, 1):
        pl.when(chip < target)(kv_to(target).wait_send)
    pl.when(core == 0)(kv_own().wait_send)
    for place in range(chips - 1):
        pl.when((place < chip) & (core == 1))(kv_pass(place).wait_send)

    @pl.when(chip == 0)
    def _():
        for i in range(group):
            for target in (2, 1) if i else (1,):
                state_to(i, target).wait_send()

    @pl.when(chip == 1)
    def _():
        for target in (3, 2):
            sums_to(target).wait_send()
            for i in range(group if target == 3 else 1):
                state_to(i, target).wait_send()
        alone_to().wait_send()

    @pl.when(chip == 3)
    def _():
        for i in range(tree, group):
            state_on(i).wait_send()

    @pl.when(chip == 2)
    def _():
        sums_to(3).wait_send()
        for i in range(group):
            state_to(i, 3).wait_send()

    for copy in own_out:
        copy.wait()
    for half in (1, 0):
        back[half].wait_send()
        there = lin_out.at[:, cols(other * 2 + half, side_heads * DH)]
        remote(there, there, out_s.at[half], out_r.at[half], sibling).wait_recv()


def fused(n, m, query_lin, key_lin, value_lin, log_decay, query_soft, key_soft, value_soft, doc_start):
    span, heads = query_lin.shape[0], log_decay.shape[0]
    rows = query_soft.shape[0]
    chips, chunk, group = n // 2, 2 * span, heads // 2
    bf16, f32 = jnp.bfloat16, jnp.float32
    any_spec = pl.BlockSpec(memory_space=pl.ANY)
    hbm_spec = pl.BlockSpec(memory_space=pltpu.HBM)
    dma = pltpu.SemaphoreType.DMA
    regular = pltpu.SemaphoreType.REGULAR
    results = pl.pallas_call(
        functools.partial(fused_kernel, n, m),
        out_shape=(
            jax.ShapeDtypeStruct((span, heads * DH), bf16),
            jax.ShapeDtypeStruct((span, heads * DH), bf16),
            jax.ShapeDtypeStruct((heads, span), f32),
        ),
        in_specs=[any_spec] * 8,
        out_specs=(any_spec,) + (pl.BlockSpec(memory_space=pltpu.VMEM),) * 2,
        scratch_shapes=[
            pltpu.VMEM((3, chunk, group * DH), bf16),
            pltpu.VMEM((2, span, group * DH), bf16),
            pltpu.VMEM((2, heads, span), f32),
            pltpu.VMEM((2, 1, span), jnp.int32),
            pltpu.VMEM((2, group, DH, DH), f32),
            pltpu.VMEM((group, DH, DH), f32),
            pltpu.VMEM((group, DH, DH), f32),
            pltpu.VMEM((group, DH, DH), bf16),
            pltpu.VMEM((DH, DH), bf16),
            pltpu.VMEM((chips - 1, group, DH, DH), bf16),
            pltpu.VMEM((8, DH), f32),
            pltpu.VMEM((chips - 1, 8, DH), f32),
            pltpu.VMEM((group, chunk, DH), f32),
            pltpu.VMEM((chunk, group * DH), bf16),
            pltpu.VMEM((span, heads * DH), bf16),
            pltpu.VMEM((heads * span, DH), bf16),
            pltpu.VMEM((2, 2, chips * span, DH), bf16),
            pltpu.VMEM((chunk, 2 * span), f32),
            pltpu.VMEM((2, (chips - 1) * span, 2 * span), f32),
            pltpu.VMEM((1, heads * span), f32),
            pltpu.VMEM((1, heads * span), f32),
            pltpu.VMEM((DH, heads * span), f32),
            dma((14,)),
            dma((7,)), dma((7,)),
            dma((2, m - 1)), dma((2, m)), dma((m - 1,)), dma((m,)),
            dma((chips,)), dma((2, chips)), dma((chips,)),
            dma((chips, group)), dma((chips - 1, group)), dma((chips,)), dma((chips - 1,)),
            dma((2,)), dma((2,)), regular, regular, regular,
        ],
        compiler_params=pltpu.CompilerParams(
            collective_id=0, has_side_effects=True, vmem_limit_bytes=32 * 1024 * 1024
        ),
    )(*(pltpu.with_memory_space_constraint(x, pltpu.HBM) for x in (
        query_lin, key_lin, value_lin, log_decay, query_soft, key_soft, value_soft,
        doc_start.reshape(1, span),
    )))
    return pl.pallas_call(
        store_kernel,
        out_shape=tuple(jax.ShapeDtypeStruct(part.shape, part.dtype) for part in results),
        in_specs=[any_spec] * 3,
        out_specs=(hbm_spec,) * 3,
        scratch_shapes=[dma((3,))],
    )(*(pltpu.with_memory_space_constraint(part, pltpu.VMEM) for part in results))


def store_kernel(a, b, c, a_out, b_out, c_out, sem):
    copies = [
        pltpu.make_async_copy(src, dst, sem.at[i])
        for i, (src, dst) in enumerate(((a, a_out), (b, b_out), (c, c_out)))
    ]
    for copy in copies:
        copy.start()
    for copy in copies:
        copy.wait()


def per_device(
    query_lin, key_lin, value_lin, log_decay, query_soft, key_soft, value_soft, doc_start
):
    n, m = lax.axis_size("seq"), lax.axis_size("head")
    span, heads = query_lin.shape[0], log_decay.shape[0]
    if heads == n == 8 and m == 4 and span == DH // 2 and key_soft.shape[1] == m * DH:
        return fused(
            n, m, query_lin, key_lin, value_lin, log_decay,
            query_soft, key_soft, value_soft, doc_start,
        )
    lin_out = lightning_part(query_lin, key_lin, value_lin, log_decay, doc_start)
    soft_out, soft_lse = softmax_part(query_soft, key_soft, value_soft, doc_start)
    return (lin_out, soft_out, soft_lse)


def solution(mesh):
    return jax.shard_map(
        per_device,
        mesh=mesh,
        in_specs=(
            P("seq", "head"),
            P("seq", "head"),
            P("seq", "head"),
            P("head", "seq"),
            P(("seq", "head"), None),
            P(("seq", "head"), None),
            P(("seq", "head"), None),
            P("seq"),
        ),
        out_specs=(P("seq", "head"), P("seq", "head"), P("head", "seq")),
        check_vma=False,
    )
```

```python
import functools

import jax
import jax.numpy as jnp
from jax import lax
from jax.experimental import pallas as pl
from jax.experimental.pallas import tpu as pltpu
from jax.sharding import PartitionSpec as P


DH = 128


HIGHEST = lax.Precision.HIGHEST
masked_score = -1e30


def prefix(array, axis, combine, identity):
    size, here = (lax.axis_size(axis), lax.axis_index(axis))
    everything = jax.tree.map(lambda part: lax.all_gather(part, axis), array)
    start = jax.tree.map(
        lambda part, zero: jnp.broadcast_to(jnp.asarray(zero, part.dtype), part.shape),
        array,
        identity,
    )

    def lap(k, before):
        reached = k < here
        new = combine(before, jax.tree.map(lambda part: part[k], everything))
        return jax.tree.map(lambda a, b: jnp.where(reached, a, b), new, before)

    return lax.fori_loop(0, size, lap, start)


def span_terms(query_heads, key_heads, value_heads, decay_rows, doc_rows, first_place):
    span_len = query_heads.shape[0]
    places = jnp.arange(span_len, dtype=jnp.int32)
    not_later = places[None, :] <= places[:, None]
    cumulative = jnp.sum(jnp.where(not_later[None], decay_rows[:, None, :], 0.0), axis=2)
    totals = cumulative[:, -1]
    token_positions = first_place + jnp.arange(span_len, dtype=jnp.int32)
    allowed = (token_positions[None, :] <= token_positions[:, None]) & (
        doc_rows[:, None] <= token_positions[None, :]
    )
    decay_gap = jnp.where(allowed[None], cumulative[:, :, None] - cumulative[:, None, :], 0.0)
    decay_mat = jnp.where(allowed[None], jnp.exp(decay_gap), 0.0)
    scores = jnp.einsum("thd,shd->hts", query_heads, key_heads, preferred_element_type=jnp.float32)
    key_float = key_heads.astype(jnp.float32)
    value_float = value_heads.astype(jnp.float32)
    inner_part = jnp.einsum("hts,shd->thd", scores * decay_mat, value_float, precision=HIGHEST)
    keep_mask = (doc_rows == doc_rows[-1]).astype(jnp.float32)
    tail_weight = jnp.exp(totals[:, None] - cumulative) * keep_mask[None, :]
    weighted_keys = key_float * jnp.transpose(tail_weight)[:, :, None]
    fresh_state = jnp.einsum("shd,she->hde", weighted_keys, value_float, precision=HIGHEST)
    carry_on = (doc_rows[-1] < first_place).astype(jnp.float32)
    factor = jnp.exp(totals) * carry_on
    read_mask = (doc_rows < first_place).astype(jnp.float32)[:, None] * jnp.transpose(
        jnp.exp(cumulative)
    )
    return (inner_part, fresh_state, factor, read_mask)


def combine_states(earlier, later_part):
    return (earlier[0] * later_part[0], later_part[0][:, None, None] * earlier[1] + later_part[1])


def lightning_part(query_lin, key_lin, value_lin, log_decay, doc_start):
    span_len = query_lin.shape[0]
    head_count = log_decay.shape[0]
    first_place = lax.axis_index("seq") * span_len
    query_heads = query_lin.reshape(span_len, head_count, DH)
    key_heads = key_lin.reshape(span_len, head_count, DH)
    value_heads = value_lin.reshape(span_len, head_count, DH)
    inner_part, fresh_state, factor, read_mask = span_terms(
        query_heads, key_heads, value_heads, log_decay, doc_start, first_place
    )
    identity = (jnp.ones((head_count,), jnp.float32), jnp.zeros((head_count, DH, DH), jnp.float32))
    unused, carried = prefix((factor, fresh_state), "seq", combine_states, identity)
    outer_part = (
        jnp.einsum("thd,hde->the", query_heads.astype(jnp.float32), carried, precision=HIGHEST)
        * read_mask[:, :, None]
    )
    mixed_out = inner_part + outer_part
    normed = mixed_out * lax.rsqrt(jnp.mean(mixed_out * mixed_out, axis=-1, keepdims=True) + 1e-06)
    return normed.astype(jnp.bfloat16).reshape(span_len, head_count * DH)


def softmax_part(query_soft, key_soft, value_soft, doc_start):
    queries, keys_local, values_local = (
        lax.all_to_all(query_soft, "head", split_axis=1, concat_axis=0, tiled=True),
        lax.all_to_all(key_soft, "head", split_axis=1, concat_axis=0, tiled=True),
        lax.all_to_all(value_soft, "head", split_axis=1, concat_axis=0, tiled=True),
    )
    span_len = queries.shape[0]
    kv_count = keys_local.shape[1] // DH
    group_size = queries.shape[1] // keys_local.shape[1]
    first_place = lax.axis_index("seq") * span_len
    query_places = first_place + jnp.arange(span_len, dtype=jnp.int32)
    query_heads = queries.reshape(span_len, kv_count, group_size, DH)
    score_scale = DH ** (-0.5)
    start_state = (
        jnp.full((span_len, kv_count, group_size), masked_score, jnp.float32),
        jnp.zeros((span_len, kv_count, group_size), jnp.float32),
        jnp.zeros((span_len, kv_count, group_size, DH), jnp.float32),
    )
    key_piece = lax.all_gather(keys_local, "seq", axis=0, tiled=True)
    value_piece = lax.all_gather(values_local, "seq", axis=0, tiled=True)
    piece_rows = key_piece.shape[0]
    block_rows = max(
        (divisor for divisor in range(1, min(piece_rows, 1024) + 1) if piece_rows % divisor == 0)
    )
    block_count = piece_rows // block_rows
    key_parts = key_piece.reshape(block_count, block_rows, kv_count, DH)
    value_parts = value_piece.reshape(block_count, block_rows, kv_count, DH)
    begin_rows = jnp.int32(0) + block_rows * jnp.arange(block_count, dtype=jnp.int32)

    def absorb_block(running, slices):
        key_block, value_block, begin_row = slices
        running_max, norm_sum, accum_out = running
        token_positions = begin_row + jnp.arange(block_rows, dtype=jnp.int32)
        allowed = (token_positions[None, :] <= query_places[:, None]) & (
            doc_start[:, None] <= token_positions[None, :]
        )
        allowed = allowed[:, None, None, :]
        scores = (
            jnp.einsum("tkgd,skd->tkgs", query_heads, key_block, preferred_element_type=jnp.float32)
            * score_scale
        )
        new_max = jnp.maximum(
            running_max, jnp.max(jnp.where(allowed, scores, masked_score), axis=-1)
        )
        raw_weight = jnp.where(allowed, jnp.exp(scores - new_max[..., None]), 0.0)
        shrink = jnp.exp(running_max - new_max)
        norm_sum = norm_sum * shrink + jnp.sum(raw_weight, axis=-1)
        accum_out = accum_out * shrink[..., None] + jnp.einsum(
            "tkgs,skd->tkgd",
            raw_weight.astype(jnp.bfloat16),
            value_block,
            preferred_element_type=jnp.float32,
        )
        running = (new_max, norm_sum, accum_out)
        return (running, None)

    final_state, unused = lax.scan(absorb_block, start_state, (key_parts, value_parts, begin_rows))
    running_max, norm_sum, accum_out = final_state
    soft_out = (
        (accum_out / norm_sum[..., None])
        .astype(jnp.bfloat16)
        .reshape(span_len, kv_count * group_size * DH)
    )
    soft_lse = jnp.transpose(
        (running_max + jnp.log(norm_sum)).reshape(span_len, kv_count * group_size)
    )
    return (soft_out, soft_lse)


MESH = pl.DeviceIdType.MESH
NT = (((1,), (1,)), ((), ()))


TN = (((0,), (0,)), ((), ()))


def fused_kernel(
    n, m, q_in, k_in, v_in, ld_in, qs_in, ks_in, vs_in, doc_in,
    lin_out, soft_out, lse_out,
    lin_all, theirs_v, ld_v, doc_v, fresh, fresh_x, state_f, state, state_x, got, sums, sums_got,
    inner, lin_v, qs, q_all, kv, shut_own, shut_past, top_v, total_v, out_v,
    loc_sem, pair_s, pair_r, kv1_s, kv1_r, qs_s, qs_r, kv2_s, kvb_r, fwd_s,
    got_s, got_r, sums_s, sums_r, out_s, out_r, go_xy, go_z, far_in,
):
    span, heads = doc_in.shape[1], ld_in.shape[0]
    rows = qs_in.shape[0]
    chips, group, chunk = n // 2, heads // 2, 2 * span
    width = group * DH
    reach = chips * span
    bf16, f32 = jnp.bfloat16, jnp.float32
    me, hd = lax.axis_index("seq"), lax.axis_index("head")
    chip, core = me // 2, lax.rem(me, 2)
    other = 1 - core
    sibling = {"seq": 2 * chip + other}
    first = chip * chunk
    head_peers = [j + jnp.where(j >= hd, 1, 0) for j in range(m - 1)]

    def cols(index, size=DH):
        return pl.ds(pl.multiple_of(index * size, size), size)

    def own_rows(index, count):
        return pl.ds(pl.multiple_of(index * count, count), count)

    def greet(semaphore, device):
        pl.semaphore_signal(semaphore, inc=1, device_id=device, device_id_type=MESH)

    def remote(src, dst, send, recv, device):
        return pltpu.make_async_remote_copy(
            src_ref=src, dst_ref=dst, send_sem=send, recv_sem=recv,
            device_id=device, device_id_type=MESH,
        )

    barrier = pltpu.get_barrier_semaphore()
    for peer in head_peers:
        greet(barrier, {"seq": 2 * chip + 1, "head": peer})
    early = hd < m - 1
    late = jnp.logical_not(early)

    @pl.when((core == 1) & early)
    def _():
        greet(barrier, {"seq": me - 1})

    @pl.when((core == 0) & late)
    def _():
        greet(barrier, {"seq": me + 1})

    for source, targets in ((0, (1,)), (1, (0, 2, 3)), (2, (3,))):
        for target in targets:

            @pl.when(chip == target)
            def _():
                greet(barrier, {"seq": 2 * source})

    my_cols, their_cols = cols(core, width), cols(other, width)
    here = own_rows(core, span)
    kv_rows = own_rows(chip * m + hd, rows)
    loads = [
        pltpu.make_async_copy(ld_in, ld_v.at[core], loc_sem.at[0]),
        pltpu.make_async_copy(doc_in, doc_v.at[core], loc_sem.at[1]),
        pltpu.make_async_copy(k_in.at[:, their_cols], theirs_v.at[0], loc_sem.at[2]),
        pltpu.make_async_copy(v_in.at[:, their_cols], theirs_v.at[1], loc_sem.at[3]),
        pltpu.make_async_copy(k_in.at[:, my_cols], lin_all.at[1, here, :], loc_sem.at[4]),
        pltpu.make_async_copy(v_in.at[:, my_cols], lin_all.at[2, here, :], loc_sem.at[5]),
        pltpu.make_async_copy(q_in.at[:, my_cols], lin_all.at[0, here, :], loc_sem.at[6]),
        pltpu.make_async_copy(ks_in.at[:, cols(hd)], kv.at[core, 0, kv_rows, :], loc_sem.at[7]),
        pltpu.make_async_copy(vs_in.at[:, cols(hd)], kv.at[core, 1, kv_rows, :], loc_sem.at[8]),
        pltpu.make_async_copy(
            qs_in.at[:, cols(hd, heads * DH)], qs.at[own_rows(hd, rows), :], loc_sem.at[9]
        ),
    ]
    for load in loads:
        load.start()

    pair = [
        remote(fresh_x.at[0:2], fresh.at[core, 0:2], pair_s.at[0], pair_r.at[0], sibling),
        remote(fresh_x.at[2:4], fresh.at[core, 2:4], pair_s.at[1], pair_r.at[1], sibling),
        remote(ld_in, ld_v.at[core], pair_s.at[2], pair_r.at[2], sibling),
        remote(doc_in, doc_v.at[core], pair_s.at[3], pair_r.at[3], sibling),
        remote(theirs_v.at[0], lin_all.at[1, here, :], pair_s.at[4], pair_r.at[4], sibling),
        remote(theirs_v.at[1], lin_all.at[2, here, :], pair_s.at[5], pair_r.at[5], sibling),
        remote(q_in.at[:, their_cols], lin_all.at[0, here, :], pair_s.at[6], pair_r.at[6], sibling),
    ]
    kv1, qsc = [], []
    for j, peer in enumerate(head_peers):
        for which, src in enumerate((ks_in, vs_in)):
            kv1.append(
                remote(
                    src.at[:, cols(peer)], kv.at[core, which, kv_rows, :],
                    kv1_s.at[which, j], kv1_r.at[which, hd], {"head": peer},
                )
            )
        qsc.append(
            remote(
                qs_in.at[:, cols(peer, heads * DH)], qs.at[own_rows(hd, rows), :],
                qs_s.at[j], qs_r.at[hd], {"head": peer},
            )
        )

    def kv_block(parity, place):
        return kv.at[parity, :, own_rows(place, span), :]

    def kv_to(target):
        mine = kv_block(core, chip)
        return remote(
            mine, mine, kv2_s.at[target], kvb_r.at[core, chip], {"seq": 2 * target + 1}
        )

    def kv_own():
        mine = kv_block(0, chip)
        return remote(mine, mine, fwd_s.at[chip], kvb_r.at[0, chip], sibling)

    def kv_pass(place):
        both = kv.at[:, :, own_rows(place, span), :]
        return remote(both, both, fwd_s.at[place], kvb_r.at[0, place], sibling)

    def kv_from(parity, place):
        block = kv_block(parity, place)
        return remote(block, block, fwd_s.at[0], kvb_r.at[parity, place], sibling)

    def state_to(i, target):
        return remote(
            state.at[i], got.at[chip, i], got_s.at[target, i], got_r.at[chip, i],
            {"seq": 2 * target + core},
        )

    def alone_to(i):
        return remote(
            state_x.at[i], got.at[1, i], got_s.at[0, i], got_r.at[1, i], {"seq": core}
        )

    def join_to(i):
        return remote(
            state_x.at[i], got.at[1, i], got_s.at[2, i], got_r.at[1, i], {"seq": 4 + core}
        )

    def state_on(i):
        held = got.at[1, i]
        return remote(held, held, got_s.at[2, i], got_r.at[1, i], {"seq": 4 + core})

    def state_from(source, i):
        there = got.at[source, i]
        return remote(there, there, got_s.at[0, i], got_r.at[source, i], sibling)

    def sums_to(target):
        return remote(
            sums, sums_got.at[chip], sums_s.at[target], sums_r.at[chip],
            {"seq": 2 * target + core},
        )

    def sums_from(source):
        there = sums_got.at[source]
        return remote(there, there, sums_s.at[0], sums_r.at[source], sibling)

    def send_over_z():
        for copy in kv1 + qsc:
            copy.start()

    n_z = 2 * (m - 1)
    n_xy = jnp.where(chip == 1, 6, 2)

    def told(semaphore):
        pl.semaphore_wait(semaphore, 1)

    @pl.when(late)
    def _():
        @pl.when(core == 1)
        def _():
            pl.semaphore_wait(barrier, n_z + 1)
            greet(go_z, sibling)

        @pl.when(core == 0)
        def _():
            told(go_z)

        send_over_z()
        for copy in pair[2:4]:
            copy.start()

    def iota(shape, dim):
        return lax.broadcasted_iota(jnp.int32, shape, dim)

    def running(values):
        size = values.shape[1]
        upper = jnp.where(iota((size, size), 0) <= iota((size, size), 1), 1.0, 0.0).astype(bf16)
        high = values.astype(bf16)
        rest = values - high.astype(f32)
        middle = rest.astype(bf16)
        low = (rest - middle.astype(f32)).astype(bf16)
        return sum(
            jnp.dot(term, upper, preferred_element_type=f32) for term in (low, middle, high)
        )

    def mine_of(values):
        return jnp.where(core == 0, values[:group], values[group:])

    def theirs_of(values):
        return jnp.where(core == 0, values[group:], values[:group])

    def key_value(keys, values, weight):
        values = values.astype(f32) * weight
        high = values.astype(bf16)
        low = (values - high.astype(f32)).astype(bf16)
        both = lax.dot_general(
            keys, jnp.concatenate([high, low], axis=1), TN, preferred_element_type=f32
        )
        return both[:, :DH] + both[:, DH:]

    for load in loads[:6]:
        load.wait()
    decay = ld_v[core]
    doc_own = doc_v[core]
    summed = running(decay)
    total = jnp.sum(decay, axis=1, keepdims=True)
    weight = jnp.where(doc_own == doc_own[:, span - 1 : span], jnp.exp(total - summed), 0.0)
    weight = jnp.transpose(jnp.concatenate([theirs_of(weight), mine_of(weight)], axis=0))
    for i in range(group):
        part = slice(i * DH, (i + 1) * DH)
        fresh_x[i] = key_value(theirs_v[0, :, part], theirs_v[1, :, part], weight[:, i : i + 1])

    @pl.when(early)
    def _():
        @pl.when(core == 0)
        def _():
            pl.semaphore_wait(barrier, jnp.where(chip == 3, 1, n_xy + 1))
            greet(go_xy, sibling)

        @pl.when(core == 1)
        def _():
            told(go_xy)

        for copy in pair[2:4]:
            copy.start()

    for copy in pair[:2] + pair[4:]:
        copy.start()
    for i in range(group):
        part = slice(i * DH, (i + 1) * DH)
        fresh[core, i] = key_value(
            lin_all[1, here, part], lin_all[2, here, part], weight[:, group + i : group + i + 1]
        )

    @pl.when(late)
    def _():
        @pl.when(core == 0)
        def _():
            @pl.when(chip < chips - 1)
            def _():
                pl.semaphore_wait(barrier, n_xy)

            greet(go_xy, sibling)

        @pl.when(core == 1)
        def _():
            told(go_xy)

    @pl.when((chip == 1) & (core == 0))
    def _():
        greet(far_in, {"seq": 0})
        greet(far_in, {"seq": 1})

    @pl.when(early & (hd > 0))
    def _():
        @pl.when(core == 1)
        def _():
            pl.semaphore_wait(barrier, n_z)
            greet(go_z, sibling)

        @pl.when(core == 0)
        def _():
            told(go_z)

        send_over_z()

    for copy in pair[:4]:
        copy.wait_recv()
    both_decays = jnp.concatenate([ld_v[0], ld_v[1]], axis=1)
    cum = mine_of(running(both_decays))
    second = mine_of(jnp.sum(both_decays[:, span:], axis=1, keepdims=True))
    doc_row = jnp.concatenate([doc_v[0], doc_v[1]], axis=1).astype(f32)
    doc_last = doc_row[:, chunk - 1 : chunk]
    first_f = first.astype(f32)
    sums[...] = jnp.concatenate(
        [
            jnp.broadcast_to(rows_of, (group, DH))
            for rows_of in (
                cum[:, chunk - 1 : chunk],
                jnp.where(doc_last < first_f, jnp.exp(cum[:, chunk - 1 : chunk]), 0.0),
            )
        ],
        axis=0,
    )
    joined = jnp.where(doc_last < first_f + span, jnp.exp(second), 0.0)
    for i in range(group):
        merged = joined[i : i + 1] * fresh[0, i] + fresh[1, i]
        state_f[i] = merged
        state[i] = merged.astype(bf16)
    tree, side_heads = 2, group // 2

    @pl.when(chip == 0)
    def _():
        state_to(0, 1).start()
        told(far_in)
        for i in range(tree, group):
            state_to(i, 2).start()

    @pl.when(chip == 1)
    def _():
        for target in (0, 3, 2):
            sums_to(target).start()
        for i in range(tree, group):
            state_to(i, 3).start()
        for i in range(tree):
            state_x[i] = state[i]
            alone_to(i).start()

    @pl.when(chip == 2)
    def _():
        sums_to(3).start()
        for i in range(tree):
            state_to(i, 3).start()

    @pl.when(hd == 0)
    def _():
        @pl.when(core == 1)
        def _():
            pl.semaphore_wait(barrier, n_z)
            greet(go_z, sibling)

        @pl.when(core == 0)
        def _():
            told(go_z)

        send_over_z()

    square = (chunk, chunk)
    at_row, at_col = iota(square, 0), iota(square, 1)
    eye, tri = at_row == at_col, at_row >= at_col
    doc_col = jnp.sum(jnp.where(eye, doc_row, 0.0), axis=1, keepdims=True)
    is_open = tri & (at_col + first >= doc_col.astype(jnp.int32))
    columns = jnp.transpose(jnp.concatenate([cum, jnp.exp(cum)], axis=0))
    loads[6].wait()
    for copy in pair[4:]:
        copy.wait_recv()
    for i in range(group):
        part = slice(i * DH, (i + 1) * DH)
        values = lin_all[2, :, part]
        score = lax.dot_general(
            lin_all[0, :, part], lin_all[1, :, part], NT, preferred_element_type=f32
        )
        mix = jnp.where(is_open, score * jnp.exp(columns[:, i : i + 1] - cum[i : i + 1]), 0.0)
        high = mix.astype(bf16)
        low = (mix - high.astype(f32)).astype(bf16)
        inner[i] = jnp.dot(
            jnp.concatenate([high, low], axis=1), jnp.concatenate([values, values], axis=0),
            preferred_element_type=f32,
        )

    @pl.when(chip == 0)
    def _():
        for i in range(1, group):
            state_to(i, 1).start()

    back = [
        remote(
            lin_v.at[own_rows(other, span), pl.ds(half * side_heads * DH, side_heads * DH)],
            lin_out.at[:, cols(core * 2 + half, side_heads * DH)],
            out_s.at[half], out_r.at[half], sibling,
        )
        for half in range(2)
    ]
    def finish(i):
        out = inner[i]
        normed = out * lax.rsqrt(jnp.mean(out * out, axis=1, keepdims=True) + 1e-06)
        normed = normed.astype(bf16)
        lin_v[:, i * DH : (i + 1) * DH] = normed
        lin_out[:, cols(group * core + i)] = jnp.where(core == 0, normed[:span], normed[span:])

    @pl.when(chip == 0)
    def _():
        for i in range(group):
            finish(i)
        for copy in back:
            copy.start()

    for place in range(chips):
        for parity in range(2):

            @pl.when(2 * place + parity > me)
            def _():
                kv[parity, :, place * span : (place + 1) * span, :] = jnp.zeros(
                    (2, span, DH), kv.dtype
                )

    def masked(is_on):
        half = jnp.where(is_on, 0.0, masked_score)
        return jnp.concatenate([half, half], axis=1)

    query_at = me * span + iota((chunk, span), 1)
    key_at = first + iota((chunk, span), 0)
    shut_own[...] = masked((key_at <= query_at) & (key_at >= doc_own))
    past = reach - span
    slot = iota((past, span), 0)
    for parity in range(2):
        key_at = slot + (slot // span + parity) * span
        shut_past[parity] = masked((slot < chip * span) & (key_at >= doc_own))

    @pl.when(chip == 3)
    def _():
        for i in range(tree, group):
            state_from(1, i).wait_recv()
            state_on(i).start()

    @pl.when(chip == 2)
    def _():
        sums_from(1).wait_recv()
        linked = jnp.where(doc_last < chunk, 1.0, 0.0)
        for i in range(tree, group):
            state_from(0, i).wait_recv()
            factor = jnp.exp(sums_got[1, i : i + 1, 0:1] + sums[i : i + 1, 0:1]) * linked
            state[i] = (state_f[i] + factor * got[0, i].astype(f32)).astype(bf16)
            state_to(i, 3).start()

    @pl.when((chip == 1) & (hd == 0))
    def _():
        linked = jnp.where(doc_last < first_f, 1.0, 0.0)
        for i in range(tree):
            state_from(0, i).wait_recv()
            factor = jnp.exp(sums[i : i + 1, 0:1]) * linked
            state[i] = (state_f[i] + factor * got[0, i].astype(f32)).astype(bf16)
            state_to(i, 3).start()

    def read(i, source, gap):
        known = doc_col < ((source + 1) * chunk)
        scale = columns[:, group + i : group + i + 1] * jnp.exp(gap)
        carried = jnp.dot(
            lin_all[0, :, i * DH : (i + 1) * DH], got[source, i], preferred_element_type=f32
        )
        inner[i] += jnp.where(known, scale, 0.0) * carried

    none = jnp.zeros((1, 1), f32)

    @pl.when(chip == 3)
    def _():
        sums_from(1).wait_recv()
        sums_from(2).wait_recv()

    def read_half(half, last):
        members = range(half * side_heads, (half + 1) * side_heads)
        for i in members:
            line = slice(i, i + 1)

            if not last:

                @pl.when(chip == 1)
                def _():
                    if i >= tree:
                        state_from(0, i).wait_recv()
                    read(i, 0, none)

            if not last:

                @pl.when(chip == 2)
                def _():
                    if i >= tree:
                        read(i, 0, sums_got[1, line, 0:1])
                    state_from(1, i).wait_recv()
                    read(i, 1, none)

            if last:

                @pl.when(chip == 3)
                def _():
                    state_from(2, i).wait_recv()
                    read(i, 2, none)
                    if i < tree:
                        state_from(1, i).wait_recv()
                    read(i, 1, sums_got[2, line, 0:1])

        @pl.when(chip == 3 if last else (chip > 0) & (chip < 3))
        def _():
            for i in members:
                finish(i)
            back[half].start()

    def attend(keys, values, shut, going):
        score = lax.dot_general(keys, q_all[...], NT, preferred_element_type=f32)
        score = score * DH ** (-0.5) + jnp.concatenate([shut] * (heads // 2), axis=1)
        top = jnp.max(score, axis=0, keepdims=True)
        if going:
            top = jnp.maximum(top, top_v[...])
        weight = jnp.exp(score - top)
        total = jnp.sum(weight, axis=0, keepdims=True)
        out = lax.dot_general(values, weight.astype(bf16), TN, preferred_element_type=f32)
        if going:
            shrink = jnp.exp(top_v[...] - top)
            total += total_v[...] * shrink
            out += out_v[...] * shrink
        top_v[...], total_v[...], out_v[...] = top, total, out

    for load in loads[7:9]:
        load.wait()
    for peer in head_peers:
        for which in range(2):
            there = kv.at[core, which, own_rows(chip * m + peer, rows), :]
            remote(
                there, there, kv1_s.at[which, 0], kv1_r.at[which, peer], {"head": peer}
            ).wait_recv()
    for target in (3, 2, 1):
        pl.when(chip < target)(kv_to(target).start)
    pl.when(core == 0)(kv_own().start)

    @pl.when((chip == 1) & (hd > 0))
    def _():
        linked = jnp.where(doc_last < first_f, 1.0, 0.0)
        for i in range(tree):
            state_from(0, i).wait_recv()
            factor = jnp.exp(sums[i : i + 1, 0:1]) * linked
            state[i] = (state_f[i] + factor * got[0, i].astype(f32)).astype(bf16)
            state_to(i, 3).start()

    @pl.when(chip == 0)
    def _():
        sums_from(1).wait_recv()
        for i in range(tree):
            state_from(1, i).wait_recv()
            factor = sums_got[1, group + i : group + i + 1, 0:1]
            state_x[i] = (got[1, i].astype(f32) + factor * state_f[i]).astype(bf16)
            join_to(i).start()

    loads[9].wait()
    for peer in head_peers:
        there = qs.at[own_rows(peer, rows), :]
        remote(there, there, qs_s.at[0], qs_r.at[peer], {"head": peer}).wait_recv()
    for g in range(heads):
        q_all[g * span : (g + 1) * span, :] = qs[:, g * DH : (g + 1) * DH]
    pl.when(core == 1)(kv_from(0, chip).wait_recv)
    own_keys, own_values = (
        jnp.concatenate([kv[p, which, own_rows(chip, span), :] for p in range(2)], axis=0)
        for which in range(2)
    )
    attend(own_keys, own_values, shut_own[...], False)
    for copy in pair + kv1 + qsc:
        copy.wait_send()
    read_half(1, False)
    read_half(0, True)
    for place in range(chips - 1):

        @pl.when((place < chip) & (core == 1))
        def _():
            kv_from(0, place).wait_recv()
            kv_from(1, place).wait_recv()
            kv_pass(place).start()

    read_half(0, False)
    read_half(1, True)

    @pl.when(chip > 0)
    def _():
        for place in range(chips - 1):
            pl.when((place < chip) & (core == 0))(kv_pass(place).wait_recv)
        for parity in range(2):
            attend(kv[parity, 0, :past, :], kv[parity, 1, :past, :], shut_past[parity], True)

    result = out_v[...] * (1.0 / total_v[...])
    lse = top_v[...] + jnp.log(total_v[...])
    for i in range(heads // 2):
        both_heads = jnp.transpose(result[:, i * DH : (i + 1) * DH].astype(bf16))
        for b in range(2):
            g = 2 * i + b
            soft_out[:, g * DH : (g + 1) * DH] = both_heads[b * span : (b + 1) * span]
            lse_out[g : g + 1, :] = lse[:, g * span : (g + 1) * span]

    for target in (3, 2, 1):
        pl.when(chip < target)(kv_to(target).wait_send)
    pl.when(core == 0)(kv_own().wait_send)
    for place in range(chips - 1):
        pl.when((place < chip) & (core == 1))(kv_pass(place).wait_send)

    @pl.when(chip == 0)
    def _():
        for i in range(group):
            if i < tree:
                join_to(i).wait_send()
            for target in (2, 1) if i >= tree else (1,):
                state_to(i, target).wait_send()

    @pl.when(chip == 1)
    def _():
        for target in (0, 3, 2):
            sums_to(target).wait_send()
        for i in range(group):
            state_to(i, 3).wait_send()
        for i in range(tree):
            alone_to(i).wait_send()

    @pl.when(chip == 3)
    def _():
        for i in range(tree, group):
            state_on(i).wait_send()

    @pl.when(chip == 2)
    def _():
        sums_to(3).wait_send()
        for i in range(group):
            state_to(i, 3).wait_send()

    for half in (1, 0):
        back[half].wait_send()
        there = lin_out.at[:, cols(other * 2 + half, side_heads * DH)]
        remote(there, there, out_s.at[half], out_r.at[half], sibling).wait_recv()


def fused(n, m, query_lin, key_lin, value_lin, log_decay, query_soft, key_soft, value_soft, doc_start):
    span, heads = query_lin.shape[0], log_decay.shape[0]
    rows = query_soft.shape[0]
    chips, chunk, group = n // 2, 2 * span, heads // 2
    bf16, f32 = jnp.bfloat16, jnp.float32
    any_spec = pl.BlockSpec(memory_space=pl.ANY)
    hbm_spec = pl.BlockSpec(memory_space=pltpu.HBM)
    dma = pltpu.SemaphoreType.DMA
    regular = pltpu.SemaphoreType.REGULAR
    results = pl.pallas_call(
        functools.partial(fused_kernel, n, m),
        out_shape=(
            jax.ShapeDtypeStruct((span, heads * DH), bf16),
            jax.ShapeDtypeStruct((span, heads * DH), bf16),
            jax.ShapeDtypeStruct((heads, span), f32),
        ),
        in_specs=[any_spec] * 8,
        out_specs=(pl.BlockSpec(memory_space=pltpu.VMEM),) * 3,
        scratch_shapes=[
            pltpu.VMEM((3, chunk, group * DH), bf16),
            pltpu.VMEM((2, span, group * DH), bf16),
            pltpu.VMEM((2, heads, span), f32),
            pltpu.VMEM((2, 1, span), jnp.int32),
            pltpu.VMEM((2, group, DH, DH), f32),
            pltpu.VMEM((group, DH, DH), f32),
            pltpu.VMEM((group, DH, DH), f32),
            pltpu.VMEM((group, DH, DH), bf16),
            pltpu.VMEM((group // 2, DH, DH), bf16),
            pltpu.VMEM((chips - 1, group, DH, DH), bf16),
            pltpu.VMEM((8, DH), f32),
            pltpu.VMEM((chips - 1, 8, DH), f32),
            pltpu.VMEM((group, chunk, DH), f32),
            pltpu.VMEM((chunk, group * DH), bf16),
            pltpu.VMEM((span, heads * DH), bf16),
            pltpu.VMEM((heads * span, DH), bf16),
            pltpu.VMEM((2, 2, chips * span, DH), bf16),
            pltpu.VMEM((chunk, 2 * span), f32),
            pltpu.VMEM((2, (chips - 1) * span, 2 * span), f32),
            pltpu.VMEM((1, heads * span), f32),
            pltpu.VMEM((1, heads * span), f32),
            pltpu.VMEM((DH, heads * span), f32),
            dma((14,)),
            dma((7,)), dma((7,)),
            dma((2, m - 1)), dma((2, m)), dma((m - 1,)), dma((m,)),
            dma((chips,)), dma((2, chips)), dma((chips,)),
            dma((chips, group)), dma((chips - 1, group)), dma((chips,)), dma((chips - 1,)),
            dma((2,)), dma((2,)), regular, regular, regular,
        ],
        compiler_params=pltpu.CompilerParams(
            collective_id=0, has_side_effects=True, vmem_limit_bytes=32 * 1024 * 1024
        ),
    )(*(pltpu.with_memory_space_constraint(x, pltpu.HBM) for x in (
        query_lin, key_lin, value_lin, log_decay, query_soft, key_soft, value_soft,
        doc_start.reshape(1, span),
    )))
    return pl.pallas_call(
        store_kernel,
        out_shape=tuple(jax.ShapeDtypeStruct(part.shape, part.dtype) for part in results),
        in_specs=[any_spec] * 3,
        out_specs=(hbm_spec,) * 3,
        scratch_shapes=[dma((3,))],
    )(*(pltpu.with_memory_space_constraint(part, pltpu.VMEM) for part in results))


def store_kernel(a, b, c, a_out, b_out, c_out, sem):
    copies = [
        pltpu.make_async_copy(src, dst, sem.at[i])
        for i, (src, dst) in enumerate(((a, a_out), (b, b_out), (c, c_out)))
    ]
    for copy in copies:
        copy.start()
    for copy in copies:
        copy.wait()


def per_device(
    query_lin, key_lin, value_lin, log_decay, query_soft, key_soft, value_soft, doc_start
):
    n, m = lax.axis_size("seq"), lax.axis_size("head")
    span, heads = query_lin.shape[0], log_decay.shape[0]
    if heads == n == 8 and m == 4 and span == DH // 2 and key_soft.shape[1] == m * DH:
        return fused(
            n, m, query_lin, key_lin, value_lin, log_decay,
            query_soft, key_soft, value_soft, doc_start,
        )
    lin_out = lightning_part(query_lin, key_lin, value_lin, log_decay, doc_start)
    soft_out, soft_lse = softmax_part(query_soft, key_soft, value_soft, doc_start)
    return (lin_out, soft_out, soft_lse)


def solution(mesh):
    return jax.shard_map(
        per_device,
        mesh=mesh,
        in_specs=(
            P("seq", "head"),
            P("seq", "head"),
            P("seq", "head"),
            P("head", "seq"),
            P(("seq", "head"), None),
            P(("seq", "head"), None),
            P(("seq", "head"), None),
            P("seq"),
        ),
        out_specs=(P("seq", "head"), P("seq", "head"), P("head", "seq")),
        check_vma=False,
    )
```
